256 devices in a mesh: dir: 4 (over x_lo, core), tb: 64 (over z, y, x_hi).
Axes of the slice: x: 4 (x_hi: 2, x_lo: 2; x = x_hi * 2 + x_lo), y: 4, z: 8, core: 2. Of those that a mesh axis runs over, the one named last changes fastest.
Arguments:
- visibilities: bfloat16 [65536, 128], P('tb'), may hold values from -6 to 6
- uv_coords: bfloat16 [2, 65536], P(None, 'tb'), may hold values from -32 to 32
- comp_lm: float32 [2, 12288], P(None, 'dir'), may hold values from -0.25 to 0.25
- spectra: bfloat16 [2, 12288, 128], P(None, 'dir'), may hold values from -0.1875 to 0.1875
- ridge_weight: float32 [128], replicated, may hold values from 32 to 512
- assignment: int32 [12288], P('dir'), may hold values from 0 to 3071, as said below
- peel_order: int32 [12], P('dir'), may hold values from 0 to 2, as said below
- block_tile: int32 [2048, 1], P('tb'), may hold values from 0 to 63; in each aligned block of 32 rows (0 to 31, 32 to 63, ...) at most 2 rows name the same one
Outputs:
- residual: bfloat16 [65536, 128], P('tb')
- subgrids: float32 [64, 2, 1024, 128], P('tb', None, 'dir')
The draws below stay inside these ranges and needn't reach their ends.
Inputs may be any that keep to these rules, and one draw needn't show every extreme that they name: `assignment`: each owner's 3 * 1024 entries are a permutation of its local component numbers. `peel_order`: each owner's 3 entries are a permutation of its directions. `block_tile`: among the 32 blocks of one index of tb no tile is named more than 2 times; every tile is named by some block of the whole array.
All inputs are finite; a program needn't handle non-finite values.
Results may differ from the reference program's by a relative error of at most 0.0064.
Values may be sent and summed in bfloat16 or wider, within the bound.
No kernel may reach another device: no remote copies, remote signals or barrier semaphores. Data moves between devices by JAX's collectives and lax.ppermute only.
A program may use at most 64 MiB of HBM per device.

```python
import math
import jax
import jax.numpy as jnp
import numpy as np
from jax import lax

COLS = 128
NCOMP = 1024
GRID = 32
DIR_DEV = 3
ITERS = 4
BB = 32
GB = 128
ROWS_DEV = 1024
NB = 32
MOST = 2
SAMPLES = 65536
BLOCKS = 2048
TILES = 64
NPOOL = 12288
PIX = 1024
N_DIR = 4


def shuffle_pool(subkey):
    return jax.random.permutation(subkey, DIR_DEV * NCOMP)


def shuffle_order(subkey):
    return jax.random.permutation(subkey, DIR_DEV)


def draw_assignment(key, part):
    subkeys = jax.random.split(jax.random.fold_in(key, 11), N_DIR)
    permuted = jax.vmap(shuffle_pool)(subkeys)
    return permuted.reshape(-1).astype(jnp.int32)


def draw_peel_order(key, part):
    subkeys = jax.random.split(jax.random.fold_in(key, 23), N_DIR)
    permuted = jax.vmap(shuffle_order)(subkeys)
    return permuted.reshape(-1).astype(jnp.int32)


def shard_levels(own_key, dims, cuts, low, largest):
    loudness = 1.0
    for dim, blocks in cuts:
        steps = jax.random.uniform(jax.random.fold_in(jax.random.fold_in(own_key, 6), dim), (blocks,), jnp.float32, low / len(cuts), largest / len(cuts))
        loudness = loudness * jnp.repeat(jnp.exp(steps), dims[dim] // blocks).reshape((-1,) + (1,) * (len(dims) - 1 - dim))
    return loudness


def deal_out(rng, own, number, rows, amount, top, reach, lean):
    ranking = jax.random.permutation(rng, amount)
    crowded, common = portions_of(amount, rows * top, reach, lean, True), portions_of(amount, rows * top, reach, lean, False)
    places = jnp.arange(amount)

    def named(tallies, offset_by):
        used = int((tallies > 0).sum())
        fixed = max(1, used // 4)
        shifted = fixed + (places - fixed + offset_by * (used - fixed)) % max(1, amount - fixed)
        return jnp.zeros((amount,), jnp.int32).at[ranking[jnp.where(places < fixed, places, shifted)]].set(jnp.asarray(tallies, jnp.int32))

    tallies = jnp.where(number % 4 == 0, named(crowded, number // 4), named(common, number - number // 4 - 1))
    mixed = jax.random.permutation(jax.random.fold_in(own, 3), amount)
    donor, receiver = mixed[0:amount // 2 * 2:2], mixed[1:amount // 2 * 2:2]
    room = jnp.minimum(tallies[donor] - 1, reach - tallies[receiver]) // 2
    room = jnp.where((donor == ranking[0]) | (receiver == ranking[0]) | (tallies[receiver] == 0), 0, jnp.maximum(room, 0))
    shifted = jax.random.randint(jax.random.fold_in(own, 4), (amount // 2,), 0, 1 << 20) % (room + 1)
    tallies = tallies.at[donor].add(-shifted).at[receiver].add(shifted)
    labels = jnp.searchsorted(jnp.cumsum(tallies), jnp.arange(rows * top), side="right").astype(jnp.int32)
    listing = labels.reshape(top, rows).T
    listing = listing[jax.random.permutation(jax.random.fold_in(own, 1), rows)]
    offset_by = jax.random.randint(jax.random.fold_in(own, 2), (rows, 1), 0, top)
    return jnp.take_along_axis(listing, (jnp.arange(top)[None, :] + offset_by) % top, axis=1)


def portions_of(number_of, total, bound, lean, full):
    loads = [(1 << 20) // math.isqrt(grade ** lean) + 1 for grade in range(1, number_of + 1)]
    largest = bound if full else min(bound, max(-(-total // number_of), total * loads[0] // sum(loads)))
    least = 1 if total - largest >= number_of - 1 else 0
    given, surplus = [largest] + [least] * (number_of - 1), total - largest - least * (number_of - 1)
    while surplus > 0:
        candidates = [i for i in range(1, number_of) if given[i] < largest] or [i for i in range(1, number_of) if given[i] < bound]
        pool, remaining = sum([loads[i] for i in candidates]), surplus
        for i in candidates:
            more = min(bound - given[i], max(1, remaining * loads[i] // pool), surplus)
            given[i] = given[i] + more
            surplus = surplus - more
    return np.array(given)


def bell_draw(key, dims, scale, most, cuts=(), held_as=jnp.bfloat16):
    loudness = shard_levels(key, dims, cuts, -0.22, 0.18) if cuts else 1.0
    result = jax.random.normal(key, dims, jnp.float32) * scale * loudness
    return jnp.minimum(jnp.maximum(result, -most), most).astype(held_as)


def setup_inputs(seed: int = 0) -> dict:
    arg_keys = jax.random.split(jax.random.key(seed), 9)
    visibilities = bell_draw(arg_keys[0], (SAMPLES, COLS), 1.0, 6.0, ((0, 64),))
    uv_coords = jnp.clip(jax.random.uniform(arg_keys[1], (2, SAMPLES), jnp.float32, -32.0, 32.0) * shard_levels(arg_keys[1], (2, SAMPLES), ((1, 64),), -0.4, 0.0), -32.0, 32.0).astype(jnp.bfloat16)
    comp_lm = jnp.clip(jax.random.uniform(arg_keys[2], (2, NPOOL), jnp.float32, -0.25, 0.25) * shard_levels(arg_keys[2], (2, NPOOL), ((1, 4),), -0.4, 0.0), -0.25, 0.25)
    spectra = bell_draw(arg_keys[3], (2, NPOOL, COLS), NCOMP ** -0.5, 0.1875, ((1, 4),))
    ridge_weight = jnp.clip(jnp.exp(jax.random.uniform(arg_keys[4], (COLS,), jnp.float32, math.log(32.0), math.log(512.0))), 32.0, 512.0)
    assignment = draw_assignment(jax.random.fold_in(arg_keys[8], 71), 0)
    peel_order = draw_peel_order(jax.random.fold_in(arg_keys[8], 71), 0)
    block_tile_keys = jax.random.split(jax.random.fold_in(arg_keys[7], 1), BLOCKS // NB)
    block_tile_turns = jax.random.permutation(jax.random.fold_in(arg_keys[7], 3), BLOCKS // NB)
    block_tile = jax.vmap(lambda own, number: deal_out(jax.random.fold_in(arg_keys[7], 2), own, number, NB, TILES, 1, MOST, 2))(block_tile_keys, block_tile_turns).reshape((BLOCKS, 1))
    return {"visibilities": visibilities, "uv_coords": uv_coords, "comp_lm": comp_lm, "spectra": spectra, "ridge_weight": ridge_weight, "assignment": assignment, "peel_order": peel_order, "block_tile": block_tile}


TWO_PI = 2.0 * math.pi


def phase_table(coords, lm_dir):
    phases = TWO_PI * (coords[0][:, None] * lm_dir[0][None, :] + coords[1][:, None] * lm_dir[1][None, :])
    return jnp.concatenate([jnp.cos(phases), jnp.sin(phases)], axis=1).astype(jnp.bfloat16)


def predict(coords, lm_dir, spec_dir):
    phase_rows = phase_table(coords, lm_dir)
    return jnp.dot(phase_rows, spec_dir.reshape(-1, spec_dir.shape[-1]), preferred_element_type=jnp.float32)


def neighbours(gain_values):
    blocks, columns = gain_values.shape
    paired = gain_values.reshape(blocks, columns // 2, 2)
    padded = jnp.pad(paired, ((0, 0), (1, 1), (0, 0)), mode="edge")
    return (0.5 * (padded[:, :-2] + padded[:, 2:])).reshape(blocks, columns)


def fit_subtract(remains, model_rows, ridge_weight):
    blocks = remains.shape[0] // GB
    res_blocks = remains.reshape(blocks, GB, -1)
    mod_blocks = model_rows.reshape(blocks, GB, -1)
    cross_sum = jnp.sum(res_blocks * mod_blocks, axis=1)
    power_sum = jnp.sum(mod_blocks * mod_blocks, axis=1)
    gain_values = jnp.ones_like(cross_sum)
    for sweep_index in range(ITERS):
        gain_values = (cross_sum + ridge_weight * neighbours(gain_values)) / (power_sum + ridge_weight)
    return (res_blocks - gain_values[:, None, :] * mod_blocks).reshape(remains.shape)


def grid_table(coords, x_pixel, y_pixel):
    phases = TWO_PI * (coords[0][:, None] * x_pixel[None, :] + coords[1][:, None] * y_pixel[None, :]) / (2.0 * GRID)
    return jnp.cos(phases).astype(jnp.bfloat16), jnp.sin(phases).astype(jnp.bfloat16)


def reference(visibilities, uv_coords, comp_lm, spectra, ridge_weight, assignment, peel_order, block_tile):
    columns = visibilities.shape[1]
    ndirs = peel_order.shape[0]
    pool_owner = DIR_DEV * NCOMP
    groups = visibilities.shape[0] // ROWS_DEV

    def one_group(group_index):
        first_row = group_index * ROWS_DEV
        remains = lax.dynamic_slice_in_dim(visibilities, first_row, ROWS_DEV, 0).astype(jnp.float32)
        coords = lax.dynamic_slice_in_dim(uv_coords, first_row, ROWS_DEV, 1).astype(jnp.float32)
        rounded = remains.astype(jnp.bfloat16)
        for position in range(ndirs):
            owner_base = (position // DIR_DEV) * pool_owner
            first_entry = owner_base + peel_order[position] * NCOMP
            chosen = owner_base + lax.dynamic_slice_in_dim(assignment, first_entry, NCOMP, 0)
            model_rows = predict(coords, comp_lm[:, chosen], spectra[:, chosen])
            remains = fit_subtract(remains, model_rows, ridge_weight)
            if (position + 1) % DIR_DEV == 0:
                rounded = lax.optimization_barrier(remains.astype(jnp.bfloat16))
                remains = rounded.astype(jnp.float32)
        return rounded

    residual = lax.map(one_group, jnp.arange(groups, dtype=jnp.int32)).reshape(-1, columns)
    pixels = jnp.arange(PIX, dtype=jnp.int32)
    x_pixel = (pixels // GRID - GRID // 2).astype(jnp.float32)
    y_pixel = (pixels % GRID - GRID // 2).astype(jnp.float32)
    blocks = residual.reshape(-1, BB, columns)
    block_coords = uv_coords.astype(jnp.float32).reshape(2, -1, BB).transpose(1, 0, 2)
    contract = (((0,), (0,)), ((), ()))

    def add_block(subgrids, block_items):
        block_rows, coords, tile_index = block_items
        cos_table, sin_table = grid_table(coords, x_pixel, y_pixel)
        real_part = lax.dot_general(cos_table, block_rows, contract, preferred_element_type=jnp.float32)
        imag_part = lax.dot_general(sin_table, block_rows, contract, preferred_element_type=jnp.float32)
        update = jnp.stack([real_part, imag_part])
        return subgrids.at[tile_index].add(update), None

    initial = jnp.zeros((TILES, 2, PIX, columns), jnp.float32)
    subgrids, unused = lax.scan(add_block, initial, (blocks, block_coords, block_tile[:, 0]))
    return residual, subgrids * (float(ROWS_DEV) ** -0.5)
```

```python
import jax
import jax.numpy as jnp
from jax import lax
from jax.experimental import pallas as pl
from jax.experimental.pallas import tpu as pltpu
from jax.sharding import PartitionSpec as P

NCOMP = 1024
GRID = 32
DIR_DEV = 3
ITERS = 4
BB = 32
GB = 128
ROWS_DEV = 1024
PIX = 1024
COLS = 128
N_DIR = 4
N_TB = 64
NB = 32
SLOTS = 2
QROWS = ROWS_DEV // N_DIR
HALF = BB // 2
POOL = DIR_DEV * NCOMP
WIDE = DIR_DEV * COLS
CHUNK = 256
NCHUNK = POOL // CHUNK
SEND_ROWS = SLOTS * HALF + 8

F32 = jnp.float32
BF16 = jnp.bfloat16

SIN_C = (2.6417407853784525, -1.0859537956447276, 0.1306204657138272)
COS_C = (1.681792784129167, -2.074822793580374, 0.42650038149094444, -0.03432262097868313)
ROOT2 = 1.4142135623730951


def vmem():
    return pl.BlockSpec(memory_space=pltpu.VMEM)


def smem():
    return pl.BlockSpec(memory_space=pltpu.SMEM)


def params(mib):
    return pltpu.CompilerParams(vmem_limit_bytes=mib << 20)


def cos_sin_turns(turns):
    r = turns - jnp.round(turns)
    z = r * r
    s = ((SIN_C[2] * z + SIN_C[1]) * z + SIN_C[0]) * r
    c = ((COS_C[3] * z + COS_C[2]) * z + COS_C[1]) * z + COS_C[0]
    s1 = s * c
    c1 = ROOT2 - s * s
    return 1.0 - s1 * s1, s1 * c1


def three_parts(value):
    high = value.astype(BF16)
    left = value - high.astype(F32)
    mid = left.astype(BF16)
    low = (left - mid.astype(F32)).astype(BF16)
    return high, mid, low


def prepare_kernel(order_ref, assign_ref, lm_ref, uv_ref, spec_ref, lm8_ref, uv8_ref, wide_ref, pos_ref):
    lh, lmid, ll = three_parts(lm_ref[...])
    zero = jnp.zeros((2, POOL), BF16)
    lm8_ref[...] = jnp.concatenate(
        [lh[0:1], lmid[0:1], ll[0:1], lh[1:2], lmid[1:2], ll[1:2], zero], axis=0
    )
    for q in range(N_DIR):
        u = uv_ref[0:1, q * QROWS : (q + 1) * QROWS]
        v = uv_ref[1:2, q * QROWS : (q + 1) * QROWS]
        uv8_ref[q] = jnp.concatenate([u, u, u, v, v, v, jnp.zeros((2, QROWS), BF16)], axis=0)
    assign = assign_ref[...]
    low = assign & 127
    high = assign >> 7
    segment = lax.broadcasted_iota(jnp.int32, (1, POOL), 1) // NCOMP
    place = jnp.zeros((1, POOL), F32)
    for p in range(DIR_DEV):
        place = jnp.where(segment == order_ref[p], float(p), place)
    low_hot = (lax.broadcasted_iota(jnp.int32, (128, POOL), 0) == low).astype(F32).astype(BF16)
    high_hot = jnp.where(lax.broadcasted_iota(jnp.int32, (32, POOL), 0) == high, place, 0.0).astype(BF16)
    pos_ref[...] = lax.dot_general(
        low_hot, high_hot, (((1,), (1,)), ((), ())), preferred_element_type=F32
    )

    def mask_chunk(j, carry):
        for h in range(CHUNK // 128):
            column = 2 * j + h
            pick = (lax.broadcasted_iota(jnp.int32, (32, 128), 0) == column).astype(F32).astype(BF16)
            place_here = jnp.dot(pos_ref[...].astype(BF16), pick, preferred_element_type=F32)
            for part in range(2):
                rows = spec_ref[part, pl.ds(pl.multiple_of(column * 128, 128), 128), :].astype(F32)
                for p in range(DIR_DEV):
                    kept = jnp.where(place_here == float(p), rows, 0.0).astype(BF16)
                    first = part * CHUNK + h * 128
                    wide_ref[j, first : first + 128, p * COLS : (p + 1) * COLS] = kept
        return carry

    lax.fori_loop(0, NCHUNK, mask_chunk, 0)


def prepare(peel_order, assignment, comp_lm, uv_coords, spectra):
    return pl.pallas_call(
        prepare_kernel,
        out_shape=(
            jax.ShapeDtypeStruct((8, POOL), BF16),
            jax.ShapeDtypeStruct((N_DIR, 8, QROWS), BF16),
            jax.ShapeDtypeStruct((NCHUNK, 2 * CHUNK, WIDE), BF16),
        ),
        in_specs=[smem(), vmem(), vmem(), vmem(), vmem()],
        out_specs=(vmem(), vmem(), vmem()),
        scratch_shapes=[pltpu.VMEM((128, 32), F32)],
        compiler_params=params(16),
        name="prepare",
    )(peel_order, assignment.reshape(1, POOL), comp_lm, uv_coords, spectra)


def predict_kernel(flips, ids_ref, uv8_ref, lm8_ref, wide_ref, *rest):
    out_refs = rest[: len(flips)]
    tab_a, tab_b, acc_ref = rest[len(flips) :]
    me = ids_ref[0]
    uv_rows = jnp.concatenate([uv8_ref[me ^ x].astype(F32).T for x in flips], axis=0).astype(BF16)

    def table(j, tab_ref):
        lm = lm8_ref[:, pl.ds(pl.multiple_of(j * CHUNK, CHUNK), CHUNK)]
        turns = jnp.dot(uv_rows, lm, preferred_element_type=F32)
        cos, sin = cos_sin_turns(turns)
        tab_ref[:, :CHUNK] = cos.astype(BF16)
        tab_ref[:, CHUNK:] = sin.astype(BF16)

    def gather(j, tab_ref):
        acc_ref[...] += jnp.dot(tab_ref[...], wide_ref[j], preferred_element_type=F32)

    acc_ref[...] = jnp.zeros(acc_ref.shape, F32)
    table(0, tab_a)

    def step(i, carry):
        gather(2 * i, tab_a)
        table(2 * i + 1, tab_b)
        gather(2 * i + 1, tab_b)
        table(jnp.minimum(2 * i + 2, NCHUNK - 1), tab_a)
        return carry

    lax.fori_loop(0, NCHUNK // 2 - 1, step, 0)
    table(NCHUNK - 1, tab_b)
    gather(NCHUNK - 2, tab_a)
    gather(NCHUNK - 1, tab_b)
    for n in range(len(flips)):
        for p in range(DIR_DEV):
            out_refs[n][p] = acc_ref[n * QROWS : (n + 1) * QROWS, p * COLS : (p + 1) * COLS].astype(BF16)


def predict(flips, ids, uv8, lm8, wide):
    rows = QROWS * len(flips)

    def kernel(*refs):
        predict_kernel(flips, *refs)

    return pl.pallas_call(
        kernel,
        out_shape=tuple(jax.ShapeDtypeStruct((DIR_DEV, QROWS, COLS), BF16) for _ in flips),
        in_specs=[smem(), vmem(), vmem(), vmem()],
        out_specs=tuple(vmem() for _ in flips),
        scratch_shapes=[
            pltpu.VMEM((rows, 2 * CHUNK), BF16),
            pltpu.VMEM((rows, 2 * CHUNK), BF16),
            pltpu.VMEM((rows, WIDE), F32),
        ],
        compiler_params=params(16),
        name="predict",
    )(ids, uv8, lm8, wide)


def per_block_sum(value):
    return jnp.sum(value.reshape(QROWS // GB, GB, COLS), axis=1)


def peel_kernel(ids_ref, vis_ref, ridge_ref, m0_ref, m1_ref, m2_ref, m3_ref, out_ref, model_ref, inv_ref):
    me = ids_ref[0]
    ridge = ridge_ref[...]
    for x, ref in enumerate((m0_ref, m1_ref, m2_ref, m3_ref)):
        owner = me ^ x
        for p in range(DIR_DEV):
            model = ref[p].astype(F32)
            model_ref[owner * DIR_DEV + p] = model
            inv_ref[owner * DIR_DEV + p] = 1.0 / (per_block_sum(model * model) + ridge)
    lane = lax.broadcasted_iota(jnp.int32, (QROWS // GB, COLS), 1)

    def neighbours(gain):
        lower = jnp.where(lane < 2, gain, pltpu.roll(gain, 2, 1))
        upper = jnp.where(lane >= COLS - 2, gain, pltpu.roll(gain, COLS - 2, 1))
        return 0.5 * (lower + upper)

    remains = vis_ref[pl.ds(pl.multiple_of(me * QROWS, QROWS), QROWS), :].astype(F32)
    for j in range(N_DIR * DIR_DEV):
        model = model_ref[j]
        inv = inv_ref[j]
        cross = per_block_sum(remains * model) * inv
        pull = ridge * inv
        gain = cross + pull
        for _ in range(ITERS - 1):
            gain = cross + pull * neighbours(gain)
        spread = jnp.concatenate(
            [jnp.broadcast_to(gain[b : b + 1], (GB, COLS)) for b in range(QROWS // GB)], axis=0
        )
        remains = remains - spread * model
        if (j + 1) % DIR_DEV == 0:
            remains = remains.astype(BF16).astype(F32)
    out_ref[...] = remains.astype(BF16)


def peel(ids, visibilities, ridge_weight, models):
    return pl.pallas_call(
        peel_kernel,
        out_shape=jax.ShapeDtypeStruct((QROWS, COLS), BF16),
        in_specs=[smem()] + [vmem()] * 6,
        out_specs=vmem(),
        scratch_shapes=[
            pltpu.VMEM((N_DIR * DIR_DEV, QROWS, COLS), F32),
            pltpu.VMEM((N_DIR * DIR_DEV, QROWS // GB, COLS), F32),
        ],
        compiler_params=params(16),
        name="peel",
    )(ids, visibilities, ridge_weight.reshape(1, COLS), *models)


def label_kernel(ids_ref, tile_ref, uv_ref, out_ref):
    half = ids_ref[1]
    offset = ids_ref[2]
    tiles = tile_ref[...].astype(F32)
    block_of_lane = lax.broadcasted_iota(jnp.int32, (NB, ROWS_DEV), 1) // BB
    expand = (block_of_lane == lax.broadcasted_iota(jnp.int32, (NB, ROWS_DEV), 0)).astype(F32)
    tile_of_lane = jnp.sum(expand * tiles, axis=0, keepdims=True)
    sub = lax.broadcasted_iota(jnp.int32, (NB, NB), 0)
    col = lax.broadcasted_iota(jnp.int32, (NB, NB), 1)
    tile_row = jnp.sum(jnp.where(sub == col, tiles, 0.0), axis=0, keepdims=True)
    slot = jnp.sum(jnp.where((tiles == tile_row) & (col < sub), 1.0, 0.0), axis=1, keepdims=True)
    slot_of_row = lax.dot_general(
        expand.astype(BF16),
        jnp.broadcast_to(slot, (NB, COLS)).astype(BF16),
        (((0,), (0,)), ((), ())),
        preferred_element_type=F32,
    )
    within = lax.broadcasted_iota(jnp.int32, (ROWS_DEV, COLS), 0) % BB - half * HALF
    lane = lax.broadcasted_iota(jnp.int32, (ROWS_DEV, COLS), 1)
    goal = slot_of_row.astype(jnp.int32) * HALF + within + offset
    spot = jnp.where((goal == lane) & (within >= 0) & (within < HALF), 1.0, 0.0).astype(BF16)
    row = lax.broadcasted_iota(jnp.int32, (N_TB * 8, ROWS_DEV), 0)
    u = uv_ref[0:1, :].astype(F32)
    v = uv_ref[1:2, :].astype(F32)
    value = jnp.where(row % 8 == 0, u, jnp.where(row % 8 == 1, v, 0.0))
    value = jnp.where((row // 8).astype(F32) == tile_of_lane, value, 0.0).astype(BF16)
    out = jnp.dot(value, spot, preferred_element_type=F32)
    out_ref[...] = out.reshape(N_TB, 8, COLS).astype(BF16)


def label(ids, block_tile, uv_coords):
    return pl.pallas_call(
        label_kernel,
        out_shape=jax.ShapeDtypeStruct((N_TB, 8, COLS), BF16),
        in_specs=[smem(), vmem(), vmem()],
        out_specs=vmem(),
        compiler_params=params(16),
        name="label",
    )(ids, block_tile, uv_coords)


def pack_kernel(ids_ref, tile_ref, r0_ref, r1_ref, r2_ref, r3_ref, coords_ref, out_ref, all_ref, stage_ref, seen_ref):
    me = ids_ref[0]
    half = ids_ref[1]
    for x, ref in enumerate((r0_ref, r1_ref, r2_ref, r3_ref)):
        rows = ref[...]
        all_ref[pl.ds(pl.multiple_of((me ^ x) * QROWS, QROWS), QROWS), :] = rows
        stage_ref[pl.ds((me ^ x) * (2 * QROWS // BB), 2 * QROWS // BB)] = rows.reshape(
            2 * QROWS // BB, HALF, COLS
        )
    out_ref[:, : SLOTS * HALF, :] = jnp.zeros((N_TB, SLOTS * HALF, COLS), BF16)
    out_ref[:, SLOTS * HALF :, :] = coords_ref[...]

    def clear(t, carry):
        seen_ref[t] = 0
        return carry

    lax.fori_loop(0, N_TB, clear, 0)

    def place(b, carry):
        tile = tile_ref[b]
        slot = seen_ref[tile]
        seen_ref[tile] = slot + 1
        out_ref[tile, pl.ds(pl.multiple_of(slot * HALF, HALF), HALF), :] = stage_ref[2 * b + half]
        return carry

    lax.fori_loop(0, NB, place, 0)


def pack(ids, tile_ids, rows, coords):
    return pl.pallas_call(
        pack_kernel,
        out_shape=(
            jax.ShapeDtypeStruct((N_TB, SEND_ROWS, COLS), BF16),
            jax.ShapeDtypeStruct((ROWS_DEV, COLS), BF16),
        ),
        in_specs=[smem(), smem()] + [vmem()] * 5,
        out_specs=(vmem(), vmem()),
        scratch_shapes=[
            pltpu.VMEM((2 * NB, HALF, COLS), BF16),
            pltpu.SMEM((N_TB,), jnp.int32),
        ],
        compiler_params=params(16),
        name="pack",
    )(ids, tile_ids, *rows, coords)


def grid_kernel(ids_ref, got_ref, keep_ref, give_ref, tab_ref):
    chip = ids_ref[0] // 2
    half = ids_ref[1]
    tiles = N_TB * SLOTS * HALF // 128
    groups = N_TB // tiles
    coords = got_ref[:, SLOTS * HALF :, :].astype(F32).reshape(tiles, groups, 8, COLS)
    coords = jnp.sum(coords, axis=1)
    y_pixel = (lax.broadcasted_iota(jnp.int32, (GRID, 1), 0) - GRID // 2).astype(F32)
    order = lax.broadcasted_iota(jnp.int32, (16, 1), 0)
    x_pixel = (16 * chip + 8 * ((order // 8) ^ half) + order % 8 - GRID // 2).astype(F32)
    scale = 1.0 / (2.0 * GRID)
    for tile in range(tiles):
        u = coords[tile, 0:1, :] * scale
        v = coords[tile, 1:2, :] * scale
        cx, sx = cos_sin_turns(x_pixel * u)
        cy, sy = cos_sin_turns(y_pixel * v)
        lanes = slice(tile * 128, (tile + 1) * 128)
        for x in range(16):
            a, b = cx[x : x + 1], sx[x : x + 1]
            tab_ref[x * GRID : (x + 1) * GRID, lanes] = (a * cy - b * sy).astype(BF16)
            tab_ref[512 + x * GRID : 512 + (x + 1) * GRID, lanes] = (b * cy + a * sy).astype(BF16)
    rows = got_ref[:, : SLOTS * HALF, :].reshape(N_TB * SLOTS * HALF, COLS)
    total = jnp.dot(tab_ref[...], rows, preferred_element_type=F32) * float(ROWS_DEV) ** (-0.5)
    for part in range(2):
        keep_ref[part] = total[part * 512 : part * 512 + 256]
        give_ref[part] = total[part * 512 + 256 : part * 512 + 512]


def grid_rows(ids, got):
    return pl.pallas_call(
        grid_kernel,
        out_shape=(
            jax.ShapeDtypeStruct((2, PIX // N_DIR, COLS), F32),
            jax.ShapeDtypeStruct((2, PIX // N_DIR, COLS), F32),
        ),
        in_specs=[smem(), vmem()],
        out_specs=(vmem(), vmem()),
        scratch_shapes=[pltpu.VMEM((1024, N_TB * SLOTS * HALF), BF16)],
        compiler_params=params(24),
        name="grid",
    )(ids, got)


def swap(value, flip):
    return lax.ppermute(value, "dir", [(i, i ^ flip) for i in range(N_DIR)])


def local(
    visibilities, uv_coords, comp_lm, spectra, ridge_weight, assignment, peel_order, block_tile
):
    me = lax.axis_index("dir")
    station = lax.axis_index("tb")
    ids = jnp.stack([me, me % 2, (station % 4) * BB]).astype(jnp.int32)
    lm8, uv8, wide = prepare(peel_order, assignment, comp_lm, uv_coords, spectra)
    (far_a,) = predict((2,), ids, uv8, lm8, wide)
    got_a = swap(far_a, 2)
    (far_b,) = predict((3,), ids, uv8, lm8, wide)
    got_b = swap(far_b, 3)
    near, own = predict((1, 0), ids, uv8, lm8, wide)
    got_near = swap(near, 1)
    rows = peel(ids, visibilities, ridge_weight, (own, got_near, got_a, got_b))
    coords = label(ids, block_tile, uv_coords)
    gathered = (rows, swap(rows, 1), swap(rows, 2), swap(rows, 3))
    send, residual = pack(ids, block_tile[:, 0], gathered, coords)
    got = lax.all_to_all(send, "tb", split_axis=0, concat_axis=0, tiled=True)
    keep, give = grid_rows(ids, got)
    subgrids = (keep + swap(give, 1))[None]
    return residual, subgrids


def solution(mesh):
    return jax.shard_map(
        local,
        mesh=mesh,
        in_specs=(
            P("tb", None),
            P(None, "tb"),
            P(None, "dir"),
            P(None, "dir", None),
            P(),
            P("dir"),
            P("dir"),
            P("tb", None),
        ),
        out_specs=(P("tb", None), P("tb", None, "dir", None)),
        check_vma=False,
    )
```

```python
import jax
import jax.numpy as jnp
from jax import lax
from jax.experimental import pallas as pl
from jax.experimental.pallas import tpu as pltpu
from jax.sharding import PartitionSpec as P

NCOMP = 1024
GRID = 32
DIR_DEV = 3
ITERS = 4
BB = 32
GB = 128
ROWS_DEV = 1024
PIX = 1024
COLS = 128
N_DIR = 4
N_TB = 64
NB = 32
QROWS = ROWS_DEV // N_DIR
HALF = BB // 2
POOL = DIR_DEV * NCOMP
WIDE = DIR_DEV * COLS
CHUNK = 256
NCHUNK = POOL // CHUNK
MESSAGE = 8 * HALF + 8

F32 = jnp.float32
BF16 = jnp.bfloat16

SIN_C = (2.6417407853784525, -1.0859537956447276, 0.1306204657138272)
COS_C = (1.681792784129167, -2.074822793580374, 0.42650038149094444, -0.03432262097868313)
ROOT2 = 1.4142135623730951


def vmem():
    return pl.BlockSpec(memory_space=pltpu.VMEM)


def smem():
    return pl.BlockSpec(memory_space=pltpu.SMEM)


def params(mib):
    return pltpu.CompilerParams(vmem_limit_bytes=mib << 20)


def cos_sin_turns(turns):
    r = turns - jnp.round(turns)
    z = r * r
    s = ((SIN_C[2] * z + SIN_C[1]) * z + SIN_C[0]) * r
    c = ((COS_C[3] * z + COS_C[2]) * z + COS_C[1]) * z + COS_C[0]
    s1 = s * c
    c1 = ROOT2 - s * s
    return 1.0 - s1 * s1, s1 * c1


def three_parts(value):
    high = value.astype(BF16)
    left = value - high.astype(F32)
    mid = left.astype(BF16)
    low = (left - mid.astype(F32)).astype(BF16)
    return high, mid, low


def prepare_kernel(
    order_hbm, assign_hbm, lm_hbm, uv_hbm, spec_hbm, lm8_ref, uv8_ref, wide_ref,
    order_ref, assign_ref, lm_ref, uv_ref, spec_ref, pos_ref, sems
):
    pairs = (
        (assign_hbm, assign_ref), (order_hbm, order_ref), (lm_hbm, lm_ref), (uv_hbm, uv_ref), (spec_hbm, spec_ref)
    )
    copies = [pltpu.make_async_copy(src, dst, sems.at[n]) for n, (src, dst) in enumerate(pairs)]
    for copy in copies:
        copy.start()
    for copy in copies[:4]:
        copy.wait()
    lh, lmid, ll = three_parts(lm_ref[...])
    zero = jnp.zeros((2, POOL), BF16)
    lm8_ref[...] = jnp.concatenate(
        [lh[0:1], lmid[0:1], ll[0:1], lh[1:2], lmid[1:2], ll[1:2], zero], axis=0
    )
    for q in range(N_DIR):
        u = uv_ref[0:1, q * QROWS : (q + 1) * QROWS]
        v = uv_ref[1:2, q * QROWS : (q + 1) * QROWS]
        uv8_ref[q] = jnp.concatenate([u, u, u, v, v, v, jnp.zeros((2, QROWS), BF16)], axis=0)
    assign = assign_ref[...]
    low = assign & 127
    high = assign >> 7
    segment = lax.broadcasted_iota(jnp.int32, (1, POOL), 1) // NCOMP
    place = jnp.zeros((1, POOL), F32)
    for p in range(DIR_DEV):
        place = jnp.where(segment == order_ref[p], float(p), place)
    low_hot = (lax.broadcasted_iota(jnp.int32, (128, POOL), 0) == low).astype(F32).astype(BF16)
    high_hot = jnp.where(lax.broadcasted_iota(jnp.int32, (32, POOL), 0) == high, place, 0.0).astype(BF16)
    pos_ref[...] = lax.dot_general(
        low_hot, high_hot, (((1,), (1,)), ((), ())), preferred_element_type=F32
    )
    copies[4].wait()

    def mask_chunk(j, carry):
        for h in range(CHUNK // 128):
            column = 2 * j + h
            pick = (lax.broadcasted_iota(jnp.int32, (32, 128), 0) == column).astype(F32).astype(BF16)
            place_here = jnp.dot(pos_ref[...].astype(BF16), pick, preferred_element_type=F32)
            for part in range(2):
                rows = spec_ref[part, pl.ds(pl.multiple_of(column * 128, 128), 128), :].astype(F32)
                for p in range(DIR_DEV):
                    kept = jnp.where(place_here == float(p), rows, 0.0).astype(BF16)
                    first = part * CHUNK + h * 128
                    wide_ref[j, first : first + 128, p * COLS : (p + 1) * COLS] = kept
        return carry

    lax.fori_loop(0, NCHUNK, mask_chunk, 0)


def prepare(peel_order, assignment, comp_lm, uv_coords, spectra):
    return pl.pallas_call(
        prepare_kernel,
        out_shape=(
            jax.ShapeDtypeStruct((8, POOL), BF16),
            jax.ShapeDtypeStruct((N_DIR, 8, QROWS), BF16),
            jax.ShapeDtypeStruct((NCHUNK, 2 * CHUNK, WIDE), BF16),
        ),
        in_specs=[pl.BlockSpec(memory_space=pl.ANY)] * 5,
        out_specs=(vmem(), vmem(), vmem()),
        scratch_shapes=[
            pltpu.SMEM((DIR_DEV,), jnp.int32),
            pltpu.VMEM((1, POOL), jnp.int32),
            pltpu.VMEM((2, POOL), F32),
            pltpu.VMEM((2, ROWS_DEV), BF16),
            pltpu.VMEM((2, POOL, COLS), BF16),
            pltpu.VMEM((128, 32), F32),
            pltpu.SemaphoreType.DMA((5,)),
        ],
        compiler_params=params(16),
        name="prepare",
    )(peel_order, assignment.reshape(1, POOL), comp_lm, uv_coords, spectra)


def predict_kernel(flips, ids_ref, uv8_ref, lm8_ref, wide_ref, *rest):
    out_refs = rest[: len(flips)]
    tab_a, tab_b, acc_ref = rest[len(flips) :]
    me = ids_ref[0]
    uv_rows = jnp.concatenate([uv8_ref[me ^ x].astype(F32).T for x in flips], axis=0).astype(BF16)

    def table(j, tab_ref):
        lm = lm8_ref[:, pl.ds(pl.multiple_of(j * CHUNK, CHUNK), CHUNK)]
        turns = jnp.dot(uv_rows, lm, preferred_element_type=F32)
        cos, sin = cos_sin_turns(turns)
        tab_ref[:, :CHUNK] = cos.astype(BF16)
        tab_ref[:, CHUNK:] = sin.astype(BF16)

    def gather(j, tab_ref):
        acc_ref[...] += jnp.dot(tab_ref[...], wide_ref[j], preferred_element_type=F32)

    acc_ref[...] = jnp.zeros(acc_ref.shape, F32)
    table(0, tab_a)

    def step(i, carry):
        gather(2 * i, tab_a)
        table(2 * i + 1, tab_b)
        gather(2 * i + 1, tab_b)
        table(jnp.minimum(2 * i + 2, NCHUNK - 1), tab_a)
        return carry

    lax.fori_loop(0, NCHUNK // 2 - 1, step, 0)
    table(NCHUNK - 1, tab_b)
    gather(NCHUNK - 2, tab_a)
    gather(NCHUNK - 1, tab_b)
    for n in range(len(flips)):
        for p in range(DIR_DEV):
            out_refs[n][p] = acc_ref[n * QROWS : (n + 1) * QROWS, p * COLS : (p + 1) * COLS].astype(BF16)


def predict(flips, ids, uv8, lm8, wide):
    rows = QROWS * len(flips)

    def kernel(*refs):
        predict_kernel(flips, *refs)

    return pl.pallas_call(
        kernel,
        out_shape=tuple(jax.ShapeDtypeStruct((DIR_DEV, QROWS, COLS), BF16) for _ in flips),
        in_specs=[smem(), vmem(), vmem(), vmem()],
        out_specs=tuple(vmem() for _ in flips),
        scratch_shapes=[
            pltpu.VMEM((rows, 2 * CHUNK), BF16),
            pltpu.VMEM((rows, 2 * CHUNK), BF16),
            pltpu.VMEM((rows, WIDE), F32),
        ],
        compiler_params=params(16),
        name="predict",
    )(ids, uv8, lm8, wide)


def per_block_sum(value):
    return jnp.sum(value.reshape(QROWS // GB, GB, COLS), axis=1)


def peel_kernel(ids_ref, vis_ref, ridge_ref, m0_ref, m1_ref, m2_ref, m3_ref, out_ref, model_ref, inv_ref):
    me = ids_ref[0]
    ridge = ridge_ref[...]
    for x, ref in enumerate((m0_ref, m1_ref, m2_ref, m3_ref)):
        owner = me ^ x
        for p in range(DIR_DEV):
            model = ref[p].astype(F32)
            model_ref[owner * DIR_DEV + p] = model
            inv_ref[owner * DIR_DEV + p] = 1.0 / (per_block_sum(model * model) + ridge)
    lane = lax.broadcasted_iota(jnp.int32, (QROWS // GB, COLS), 1)

    def neighbours(gain):
        lower = jnp.where(lane < 2, gain, pltpu.roll(gain, 2, 1))
        upper = jnp.where(lane >= COLS - 2, gain, pltpu.roll(gain, COLS - 2, 1))
        return 0.5 * (lower + upper)

    remains = vis_ref[pl.ds(pl.multiple_of(me * QROWS, QROWS), QROWS), :].astype(F32)
    for j in range(N_DIR * DIR_DEV):
        model = model_ref[j]
        inv = inv_ref[j]
        cross = per_block_sum(remains * model) * inv
        pull = ridge * inv
        gain = cross + pull
        for _ in range(ITERS - 1):
            gain = cross + pull * neighbours(gain)
        spread = jnp.concatenate(
            [jnp.broadcast_to(gain[b : b + 1], (GB, COLS)) for b in range(QROWS // GB)], axis=0
        )
        remains = remains - spread * model
        if (j + 1) % DIR_DEV == 0:
            remains = remains.astype(BF16).astype(F32)
    out_ref[...] = remains.astype(BF16)


def peel(ids, visibilities, ridge_weight, models):
    return pl.pallas_call(
        peel_kernel,
        out_shape=jax.ShapeDtypeStruct((QROWS, COLS), BF16),
        in_specs=[smem()] + [vmem()] * 6,
        out_specs=vmem(),
        scratch_shapes=[
            pltpu.VMEM((N_DIR * DIR_DEV, QROWS, COLS), F32),
            pltpu.VMEM((N_DIR * DIR_DEV, QROWS // GB, COLS), F32),
        ],
        compiler_params=params(16),
        name="peel",
    )(ids, visibilities, ridge_weight.reshape(1, COLS), *models)


def plane_offset(target, station):
    return (((target >> 1) - (station >> 1)) & 3) * 2 + ((target ^ station) & 1)


def plane_target(station, step):
    return ((((station >> 1) + (step >> 1)) & 3) << 1) | ((station ^ step) & 1)


def label_kernel(ids_ref, tile_ref, uv_ref, out_ref):
    half, z, xy = ids_ref[1], ids_ref[2], ids_ref[3]
    tiles = tile_ref[...]
    block_of_lane = lax.broadcasted_iota(jnp.int32, (NB, ROWS_DEV), 1) // BB
    expand = block_of_lane == lax.broadcasted_iota(jnp.int32, (NB, ROWS_DEV), 0)
    sub = lax.broadcasted_iota(jnp.int32, (NB, NB), 0)
    col = lax.broadcasted_iota(jnp.int32, (NB, NB), 1)
    tile_row = jnp.sum(jnp.where(sub == col, tiles.astype(F32), 0.0), axis=0, keepdims=True)
    slot = jnp.sum(jnp.where((tiles.astype(F32) == tile_row) & (col < sub), 1.0, 0.0), axis=1, keepdims=True)
    up = ((tiles >> 3) - z) & 7
    across = plane_offset(tiles & 7, xy)
    code = jnp.where(slot < 0.5, up * 8 + (tiles & 7), 64 + across * 8 + (tiles >> 3)).astype(F32)
    code_of_lane = jnp.sum(jnp.where(expand, code, 0.0), axis=0, keepdims=True)
    within = lax.broadcasted_iota(jnp.int32, (ROWS_DEV, COLS), 0) % BB - half * HALF
    lane = lax.broadcasted_iota(jnp.int32, (ROWS_DEV, COLS), 1)
    spot = jnp.where(lane % HALF == within, 1.0, 0.0).astype(BF16)
    row = lax.broadcasted_iota(jnp.int32, (128, ROWS_DEV), 0).astype(F32)
    mine = row == code_of_lane
    u = jnp.where(mine, uv_ref[0:1, :].astype(F32), 0.0).astype(BF16)
    v = jnp.where(mine, uv_ref[1:2, :].astype(F32), 0.0).astype(BF16)
    u = jnp.dot(u, spot, preferred_element_type=F32)
    v = jnp.dot(v, spot, preferred_element_type=F32)
    step = (lax.broadcasted_iota(jnp.int32, (128, COLS), 0) // 8) % 8
    group = lax.broadcasted_iota(jnp.int32, (128, COLS), 1) // HALF
    out = jnp.where(group == step, u, jnp.where(group == (step + 4) % 8, v, 0.0))
    out_ref[...] = out.reshape(16, 8, COLS).astype(BF16)


def label(ids, block_tile, uv_coords):
    return pl.pallas_call(
        label_kernel,
        out_shape=jax.ShapeDtypeStruct((16, 8, COLS), BF16),
        in_specs=[smem(), vmem(), vmem()],
        out_specs=vmem(),
        compiler_params=params(16),
        name="label",
    )(ids, block_tile, uv_coords)


def pack_kernel(ids_ref, tile_ref, r0_ref, r1_ref, r2_ref, r3_ref, coords_ref, *rest):
    out_refs = rest[:16]
    all_ref, stage_ref, work_ref, seen_ref = rest[16:]
    me, half, z, xy = ids_ref[0], ids_ref[1], ids_ref[2], ids_ref[3]
    for x, ref in enumerate((r0_ref, r1_ref, r2_ref, r3_ref)):
        rows = ref[...]
        all_ref[pl.ds(pl.multiple_of((me ^ x) * QROWS, QROWS), QROWS), :] = rows
        stage_ref[pl.ds((me ^ x) * (2 * QROWS // BB), 2 * QROWS // BB)] = rows.reshape(
            2 * QROWS // BB, HALF, COLS
        )
    work_ref[...] = jnp.zeros((16, 128, COLS), BF16)

    def clear(t, carry):
        seen_ref[t] = 0
        return carry

    lax.fori_loop(0, N_TB, clear, 0)

    def place(b, carry):
        tile = tile_ref[b]
        second = seen_ref[tile]
        seen_ref[tile] = 1
        up = ((tile >> 3) - z) & 7
        across = 8 + plane_offset(tile & 7, xy)
        message = jnp.where(second == 0, up, across)
        piece = jnp.where(second == 0, tile & 7, tile >> 3)
        work_ref[message, pl.ds(pl.multiple_of(piece * HALF, HALF), HALF), :] = stage_ref[2 * b + half]
        return carry

    lax.fori_loop(0, NB, place, 0)
    for n in range(16):
        out_refs[n][:128, :] = work_ref[n]
        out_refs[n][128:, :] = coords_ref[n]


def pack(ids, tile_ids, rows, coords):
    message = jax.ShapeDtypeStruct((MESSAGE, COLS), BF16)
    out = pl.pallas_call(
        pack_kernel,
        out_shape=(message,) * 16 + (jax.ShapeDtypeStruct((ROWS_DEV, COLS), BF16),),
        in_specs=[smem(), smem()] + [vmem()] * 5,
        out_specs=(vmem(),) * 17,
        scratch_shapes=[
            pltpu.VMEM((2 * NB, HALF, COLS), BF16),
            pltpu.VMEM((16, 128, COLS), BF16),
            pltpu.SMEM((N_TB,), jnp.int32),
        ],
        compiler_params=params(16),
        name="pack",
    )(ids, tile_ids, *rows, coords)
    return out[:8], out[8:16], out[16]


def regroup_kernel(second_is_plane, ids_ref, *refs):
    in_refs, out_refs, (coords_ref,) = refs[:8], refs[8:16], refs[16:]
    z, xy = ids_ref[2], ids_ref[3]
    for d in range(8):
        coords_ref[d * 8 : d * 8 + 8, :] = in_refs[d][128:, :].astype(F32)
    for e in range(8):
        piece = plane_target(xy, e) if second_is_plane else (z + e) & 7
        for d in range(8):
            out_refs[e][d * HALF : (d + 1) * HALF, :] = in_refs[d][
                pl.ds(pl.multiple_of(piece * HALF, HALF), HALF), :
            ]
        out_refs[e][128:, :] = coords_ref[pl.ds(piece, 8, stride=8), :].astype(BF16)


def regroup(ids, messages, second_is_plane):
    message = jax.ShapeDtypeStruct((MESSAGE, COLS), BF16)

    def kernel(*refs):
        regroup_kernel(second_is_plane, *refs)

    return pl.pallas_call(
        kernel,
        out_shape=(message,) * 8,
        in_specs=[smem()] + [vmem()] * 8,
        out_specs=(vmem(),) * 8,
        scratch_shapes=[pltpu.VMEM((64, COLS), F32)],
        compiler_params=params(16),
        name="regroup",
    )(ids, *messages)


def grid_kernel(ids_ref, *refs):
    in_refs, (keep_ref, give_ref, tab_ref, row_ref) = refs[:16], refs[16:]
    chip = ids_ref[0] // 2
    half = ids_ref[1]
    y_pixel = (lax.broadcasted_iota(jnp.int32, (GRID, 1), 0) - GRID // 2).astype(F32)
    order = lax.broadcasted_iota(jnp.int32, (16, 1), 0)
    x_pixel = (16 * chip + 8 * ((order // 8) ^ half) + order % 8 - GRID // 2).astype(F32)
    scale = 1.0 / (2.0 * GRID)
    sub = lax.broadcasted_iota(jnp.int32, (8, COLS), 0)
    group = lax.broadcasted_iota(jnp.int32, (8, COLS), 1) // HALF
    for tile in range(16):
        coords = in_refs[tile][128:, :].astype(F32)
        u = jnp.sum(jnp.where(group == sub, coords, 0.0), axis=0, keepdims=True) * scale
        v = jnp.sum(jnp.where(group == (sub + 4) % 8, coords, 0.0), axis=0, keepdims=True) * scale
        v = pltpu.roll(v, 64, 1)
        cx, sx = cos_sin_turns(x_pixel * u)
        cy, sy = cos_sin_turns(y_pixel * v)
        lanes = slice(tile * 128, (tile + 1) * 128)
        for x in range(16):
            a, b = cx[x : x + 1], sx[x : x + 1]
            tab_ref[x * GRID : (x + 1) * GRID, lanes] = (a * cy - b * sy).astype(BF16)
            tab_ref[512 + x * GRID : 512 + (x + 1) * GRID, lanes] = (b * cy + a * sy).astype(BF16)
        row_ref[lanes, :] = in_refs[tile][:128, :]
    total = jnp.dot(tab_ref[...], row_ref[...], preferred_element_type=F32) * float(ROWS_DEV) ** (-0.5)
    for part in range(2):
        keep_ref[part] = total[part * 512 : part * 512 + 256]
        give_ref[part] = total[part * 512 + 256 : part * 512 + 512]


def grid_rows(ids, messages):
    return pl.pallas_call(
        grid_kernel,
        out_shape=(
            jax.ShapeDtypeStruct((2, PIX // N_DIR, COLS), F32),
            jax.ShapeDtypeStruct((2, PIX // N_DIR, COLS), F32),
        ),
        in_specs=[smem()] + [vmem()] * 16,
        out_specs=(vmem(), vmem()),
        scratch_shapes=[pltpu.VMEM((1024, 2048), BF16), pltpu.VMEM((2048, COLS), BF16)],
        compiler_params=params(24),
        name="grid",
    )(ids, *messages)


def up_z(messages):
    pairs = [[(i, (i + 8 * d) % N_TB) for i in range(N_TB)] for d in range(8)]
    return [messages[0]] + [lax.ppermute(messages[d], "tb", pairs[d]) for d in range(1, 8)]


def over_plane(messages):
    pairs = [[(i, (i & ~7) + plane_target(i & 7, d)) for i in range(N_TB)] for d in range(8)]
    return [messages[0]] + [lax.ppermute(messages[d], "tb", pairs[d]) for d in range(1, 8)]


def swap(value, flip):
    return lax.ppermute(value, "dir", [(i, i ^ flip) for i in range(N_DIR)])


def local(
    visibilities, uv_coords, comp_lm, spectra, ridge_weight, assignment, peel_order, block_tile
):
    me = lax.axis_index("dir")
    station = lax.axis_index("tb")
    ids = jnp.stack([me, me & 1, station >> 3, station & 7]).astype(jnp.int32)
    lm8, uv8, wide = prepare(peel_order, assignment, comp_lm, uv_coords, spectra)
    (far_a,) = predict((2,), ids, uv8, lm8, wide)
    got_a = swap(far_a, 2)
    (far_b,) = predict((3,), ids, uv8, lm8, wide)
    got_b = swap(far_b, 3)
    near, own = predict((1, 0), ids, uv8, lm8, wide)
    got_near = swap(near, 1)
    rows = peel(ids, visibilities, ridge_weight, (own, got_near, got_a, got_b))
    coords = label(ids, block_tile, uv_coords)
    gathered = (rows, swap(rows, 1), swap(rows, 2), swap(rows, 3))
    first_up, first_over, residual = pack(ids, block_tile[:, 0], gathered, coords)
    second_over = regroup(ids, up_z(first_up), True)
    second_up = regroup(ids, over_plane(first_over), False)
    keep, give = grid_rows(ids, over_plane(second_over) + up_z(second_up))
    subgrids = (keep + swap(give, 1))[None]
    return residual, subgrids


def solution(mesh):
    return jax.shard_map(
        local,
        mesh=mesh,
        in_specs=(
            P("tb", None),
            P(None, "tb"),
            P(None, "dir"),
            P(None, "dir", None),
            P(),
            P("dir"),
            P("dir"),
            P("tb", None),
        ),
        out_specs=(P("tb", None), P("tb", None, "dir", None)),
        check_vma=False,
    )
```

```python
import jax
import jax.numpy as jnp
from jax import lax
from jax.experimental import pallas as pl
from jax.experimental.pallas import tpu as pltpu
from jax.sharding import PartitionSpec as P

NCOMP = 1024
GRID = 32
DIR_DEV = 3
ITERS = 4
BB = 32
GB = 128
ROWS_DEV = 1024
PIX = 1024
COLS = 128
N_DIR = 4
N_TB = 64
NB = 32
SLOTS = 2
QROWS = ROWS_DEV // N_DIR
HALF = BB // 2
POOL = DIR_DEV * NCOMP
WIDE = DIR_DEV * COLS
CHUNK = 256
NCHUNK = POOL // CHUNK
SEND_ROWS = SLOTS * HALF + 8

F32 = jnp.float32
BF16 = jnp.bfloat16

SIN_C = (2.6417407853784525, -1.0859537956447276, 0.1306204657138272)
COS_C = (1.681792784129167, -2.074822793580374, 0.42650038149094444, -0.03432262097868313)
ROOT2 = 1.4142135623730951


def vmem():
    return pl.BlockSpec(memory_space=pltpu.VMEM)


def smem():
    return pl.BlockSpec(memory_space=pltpu.SMEM)


def params(mib):
    return pltpu.CompilerParams(vmem_limit_bytes=mib << 20)


def cos_sin_turns(turns):
    r = turns - jnp.round(turns)
    z = r * r
    s = ((SIN_C[2] * z + SIN_C[1]) * z + SIN_C[0]) * r
    c = ((COS_C[3] * z + COS_C[2]) * z + COS_C[1]) * z + COS_C[0]
    s1 = s * c
    c1 = ROOT2 - s * s
    return 1.0 - s1 * s1, s1 * c1


def three_parts(value):
    high = value.astype(BF16)
    left = value - high.astype(F32)
    mid = left.astype(BF16)
    low = (left - mid.astype(F32)).astype(BF16)
    return high, mid, low


def prepare_kernel(
    order_hbm, assign_hbm, lm_hbm, uv_hbm, spec_hbm, lm8_ref, uv8_ref, wide_ref,
    order_ref, assign_ref, lm_ref, uv_ref, spec_ref, pos_ref, sems
):
    pairs = (
        (assign_hbm, assign_ref), (order_hbm, order_ref), (lm_hbm, lm_ref), (uv_hbm, uv_ref), (spec_hbm, spec_ref)
    )
    copies = [pltpu.make_async_copy(src, dst, sems.at[n]) for n, (src, dst) in enumerate(pairs)]
    for copy in copies:
        copy.start()
    for copy in copies[:4]:
        copy.wait()
    lh, lmid, ll = three_parts(lm_ref[...])
    zero = jnp.zeros((2, POOL), BF16)
    lm8_ref[...] = jnp.concatenate(
        [lh[0:1], lmid[0:1], ll[0:1], lh[1:2], lmid[1:2], ll[1:2], zero], axis=0
    )
    for q in range(N_DIR):
        u = uv_ref[0:1, q * QROWS : (q + 1) * QROWS]
        v = uv_ref[1:2, q * QROWS : (q + 1) * QROWS]
        uv8_ref[q] = jnp.concatenate([u, u, u, v, v, v, jnp.zeros((2, QROWS), BF16)], axis=0)
    assign = assign_ref[...]
    low = assign & 127
    high = assign >> 7
    segment = lax.broadcasted_iota(jnp.int32, (1, POOL), 1) // NCOMP
    place = jnp.zeros((1, POOL), F32)
    for p in range(DIR_DEV):
        place = jnp.where(segment == order_ref[p], float(p), place)
    low_hot = (lax.broadcasted_iota(jnp.int32, (128, POOL), 0) == low).astype(F32).astype(BF16)
    high_hot = jnp.where(lax.broadcasted_iota(jnp.int32, (32, POOL), 0) == high, place, 0.0).astype(BF16)
    pos = lax.dot_general(low_hot, high_hot, (((1,), (1,)), ((), ())), preferred_element_type=F32)
    column = lax.broadcasted_iota(jnp.int32, (32, POOL), 1) // 128
    pick = (column == lax.broadcasted_iota(jnp.int32, (32, POOL), 0)).astype(F32).astype(BF16)
    pos_ref[...] = jnp.dot(pos.astype(BF16), pick, preferred_element_type=F32)
    copies[4].wait()
    for column in range(POOL // 128):
        place_here = pos_ref[:, column * 128 : (column + 1) * 128]
        for p in range(DIR_DEV):
            mask = jnp.where(place_here == float(p), 1.0, 0.0).astype(BF16)
            for part in range(2):
                first = part * CHUNK + (column % 2) * 128
                wide_ref[column // 2, first : first + 128, p * COLS : (p + 1) * COLS] = (
                    spec_ref[part, column * 128 : (column + 1) * 128, :] * mask
                )


def prepare(peel_order, assignment, comp_lm, uv_coords, spectra):
    return pl.pallas_call(
        prepare_kernel,
        out_shape=(
            jax.ShapeDtypeStruct((8, POOL), BF16),
            jax.ShapeDtypeStruct((N_DIR, 8, QROWS), BF16),
            jax.ShapeDtypeStruct((NCHUNK, 2 * CHUNK, WIDE), BF16),
        ),
        in_specs=[pl.BlockSpec(memory_space=pltpu.MemorySpace.HBM)] * 5,
        out_specs=(vmem(), vmem(), vmem()),
        scratch_shapes=[
            pltpu.SMEM((DIR_DEV,), jnp.int32),
            pltpu.VMEM((1, POOL), jnp.int32),
            pltpu.VMEM((2, POOL), F32),
            pltpu.VMEM((2, ROWS_DEV), BF16),
            pltpu.VMEM((2, POOL, COLS), BF16),
            pltpu.VMEM((128, POOL), F32),
            pltpu.SemaphoreType.DMA((5,)),
        ],
        compiler_params=params(16),
        name="prepare",
    )(*(
        pltpu.with_memory_space_constraint(value, pltpu.MemorySpace.HBM)
        for value in (peel_order, assignment.reshape(1, POOL), comp_lm, uv_coords, spectra)
    ))


def predict_kernel(flips, ids_ref, uv8_ref, lm8_ref, wide_ref, *rest):
    out_refs = rest[: len(flips)]
    tab_a, tab_b, acc_ref = rest[len(flips) :]
    me = ids_ref[0]
    uv_rows = jnp.concatenate([uv8_ref[me ^ x].astype(F32).T for x in flips], axis=0).astype(BF16)

    def table(j, tab_ref):
        lm = lm8_ref[:, j * CHUNK : (j + 1) * CHUNK]
        turns = jnp.dot(uv_rows, lm, preferred_element_type=F32)
        cos, sin = cos_sin_turns(turns)
        tab_ref[:, :CHUNK] = cos.astype(BF16)
        tab_ref[:, CHUNK:] = sin.astype(BF16)

    tabs = (tab_a, tab_b)
    table(0, tab_a)
    for j in range(NCHUNK):
        if j + 1 < NCHUNK:
            table(j + 1, tabs[(j + 1) % 2])
        part = jnp.dot(tabs[j % 2][...], wide_ref[j], preferred_element_type=F32)
        if j == 0:
            acc_ref[...] = part
        else:
            acc_ref[...] += part
    for n in range(len(flips)):
        for p in range(DIR_DEV):
            out_refs[n][p] = acc_ref[n * QROWS : (n + 1) * QROWS, p * COLS : (p + 1) * COLS].astype(BF16)


def predict(flips, ids, uv8, lm8, wide):
    rows = QROWS * len(flips)

    def kernel(*refs):
        predict_kernel(flips, *refs)

    return pl.pallas_call(
        kernel,
        out_shape=tuple(jax.ShapeDtypeStruct((DIR_DEV, QROWS, COLS), BF16) for _ in flips),
        in_specs=[smem(), vmem(), vmem(), vmem()],
        out_specs=tuple(vmem() for _ in flips),
        scratch_shapes=[
            pltpu.VMEM((rows, 2 * CHUNK), BF16),
            pltpu.VMEM((rows, 2 * CHUNK), BF16),
            pltpu.VMEM((rows, WIDE), F32),
        ],
        cost_estimate=pl.CostEstimate(
            flops=2 * rows * 2 * POOL * 2 * WIDE,
            transcendentals=0,
            bytes_accessed=2 * (2 * POOL * WIDE + rows * WIDE),
        ),
        compiler_params=params(16),
        name="predict",
    )(ids, uv8, lm8, wide)


def per_block_sum(value):
    return jnp.sum(value.reshape(QROWS // GB, GB, COLS), axis=1)


def peel_kernel(ids_ref, vis_ref, ridge_ref, m0_ref, m1_ref, m2_ref, m3_ref, out_ref, model_ref, inv_ref):
    me = ids_ref[0]
    ridge = ridge_ref[...]
    for x, ref in enumerate((m0_ref, m1_ref, m2_ref, m3_ref)):
        owner = me ^ x
        for p in range(DIR_DEV):
            model = ref[p].astype(F32)
            model_ref[owner * DIR_DEV + p] = model
            inv_ref[owner * DIR_DEV + p] = 1.0 / (per_block_sum(model * model) + ridge)
    lane = lax.broadcasted_iota(jnp.int32, (QROWS // GB, COLS), 1)

    def neighbours(gain):
        lower = jnp.where(lane < 2, gain, pltpu.roll(gain, 2, 1))
        upper = jnp.where(lane >= COLS - 2, gain, pltpu.roll(gain, COLS - 2, 1))
        return 0.5 * (lower + upper)

    remains = vis_ref[pl.ds(pl.multiple_of(me * QROWS, QROWS), QROWS), :].astype(F32)
    for j in range(N_DIR * DIR_DEV):
        model = model_ref[j]
        inv = inv_ref[j]
        cross = per_block_sum(remains * model) * inv
        pull = ridge * inv
        gain = cross + pull
        for _ in range(ITERS - 1):
            gain = cross + pull * neighbours(gain)
        spread = jnp.concatenate(
            [jnp.broadcast_to(gain[b : b + 1], (GB, COLS)) for b in range(QROWS // GB)], axis=0
        )
        remains = remains - spread * model
        if (j + 1) % DIR_DEV == 0:
            remains = remains.astype(BF16).astype(F32)
    out_ref[...] = remains.astype(BF16)


def peel(ids, visibilities, ridge_weight, models):
    return pl.pallas_call(
        peel_kernel,
        out_shape=jax.ShapeDtypeStruct((QROWS, COLS), BF16),
        in_specs=[smem()] + [vmem()] * 6,
        out_specs=vmem(),
        scratch_shapes=[
            pltpu.VMEM((N_DIR * DIR_DEV, QROWS, COLS), F32),
            pltpu.VMEM((N_DIR * DIR_DEV, QROWS // GB, COLS), F32),
        ],
        compiler_params=params(16),
        name="peel",
    )(ids, visibilities, ridge_weight.reshape(1, COLS), *models)


def label_kernel(ids_ref, tile_id_ref, tile_ref, uv_ref, out_ref, slot_ref, seen_ref):
    half = ids_ref[1]
    offset = ids_ref[2]
    tiles = tile_ref[...].astype(F32)
    block_of_lane = lax.broadcasted_iota(jnp.int32, (NB, ROWS_DEV), 1) // BB
    expand = (block_of_lane == lax.broadcasted_iota(jnp.int32, (NB, ROWS_DEV), 0)).astype(F32)
    tile_of_lane = jnp.sum(expand * tiles, axis=0, keepdims=True)
    sub = lax.broadcasted_iota(jnp.int32, (NB, NB), 0)
    col = lax.broadcasted_iota(jnp.int32, (NB, NB), 1)
    tile_row = jnp.sum(jnp.where(sub == col, tiles, 0.0), axis=0, keepdims=True)
    slot = jnp.sum(jnp.where((tiles == tile_row) & (col < sub), 1.0, 0.0), axis=1, keepdims=True)
    slot_of_row = lax.dot_general(
        expand.astype(BF16),
        jnp.broadcast_to(slot, (NB, COLS)).astype(BF16),
        (((0,), (0,)), ((), ())),
        preferred_element_type=F32,
    )
    within = lax.broadcasted_iota(jnp.int32, (ROWS_DEV, COLS), 0) % BB - half * HALF
    lane = lax.broadcasted_iota(jnp.int32, (ROWS_DEV, COLS), 1)
    goal = slot_of_row.astype(jnp.int32) * HALF + within + offset
    spot = jnp.where((goal == lane) & (within >= 0) & (within < HALF), 1.0, 0.0).astype(BF16)
    row = lax.broadcasted_iota(jnp.int32, (N_TB * 8, ROWS_DEV), 0)
    u = uv_ref[0:1, :].astype(F32)
    v = uv_ref[1:2, :].astype(F32)
    value = jnp.where(row % 8 == 0, u, jnp.where(row % 8 == 1, v, 0.0))
    value = jnp.where((row // 8).astype(F32) == tile_of_lane, value, 0.0).astype(BF16)
    out = jnp.dot(value, spot, preferred_element_type=F32)
    out_ref[:, : SLOTS * HALF, :] = jnp.zeros((N_TB, SLOTS * HALF, COLS), BF16)
    out_ref[:, SLOTS * HALF :, :] = out.reshape(N_TB, 8, COLS).astype(BF16)
    for t in range(N_TB):
        seen_ref[t] = 0
    for b in range(NB):
        tile = tile_id_ref[b]
        slot_ref[b] = seen_ref[tile]
        seen_ref[tile] = 1


def label(ids, tile_ids, block_tile, uv_coords):
    return pl.pallas_call(
        label_kernel,
        out_shape=(
            jax.ShapeDtypeStruct((N_TB, SEND_ROWS, COLS), BF16),
            jax.ShapeDtypeStruct((NB,), jnp.int32),
        ),
        in_specs=[smem(), smem(), vmem(), vmem()],
        out_specs=(vmem(), smem()),
        scratch_shapes=[pltpu.SMEM((N_TB,), jnp.int32)],
        compiler_params=params(16),
        name="label",
    )(ids, tile_ids, block_tile, uv_coords)


def pack_kernel(ids_ref, tile_ref, slot_ref, r0_ref, r1_ref, r2_ref, r3_ref, base_ref, out_ref, stage_ref):
    me = ids_ref[0]
    half = ids_ref[1]
    out_ref[...] = base_ref[...]
    for x, ref in enumerate((r0_ref, r1_ref, r2_ref, r3_ref)):
        stage_ref[pl.ds((me ^ x) * (2 * QROWS // BB), 2 * QROWS // BB)] = ref[...].reshape(
            2 * QROWS // BB, HALF, COLS
        )
    for b in range(NB):
        first = pl.multiple_of(slot_ref[b] * HALF, HALF)
        out_ref[tile_ref[b], pl.ds(first, HALF), :] = stage_ref[2 * b + half]


def pack(ids, tile_ids, slots, rows, base):
    return pl.pallas_call(
        pack_kernel,
        out_shape=jax.ShapeDtypeStruct((N_TB, SEND_ROWS, COLS), BF16),
        in_specs=[smem(), smem(), smem()] + [vmem()] * 5,
        out_specs=vmem(),
        scratch_shapes=[pltpu.VMEM((2 * NB, HALF, COLS), BF16)],
        compiler_params=params(16),
        name="pack",
    )(ids, tile_ids, slots, *rows, base)


def join_kernel(ids_ref, r0_ref, r1_ref, r2_ref, r3_ref, out_ref):
    me = ids_ref[0]
    for x, ref in enumerate((r0_ref, r1_ref, r2_ref, r3_ref)):
        out_ref[pl.ds(pl.multiple_of((me ^ x) * QROWS, QROWS), QROWS), :] = ref[...]


def join(ids, rows):
    return pl.pallas_call(
        join_kernel,
        out_shape=jax.ShapeDtypeStruct((ROWS_DEV, COLS), BF16),
        in_specs=[smem()] + [vmem()] * 4,
        out_specs=vmem(),
        compiler_params=params(16),
        name="join",
    )(ids, *rows)


def grid_kernel(ids_ref, got_ref, keep_ref, give_ref, tab_ref):
    chip = ids_ref[0] // 2
    half = ids_ref[1]
    tiles = N_TB * SLOTS * HALF // 128
    groups = N_TB // tiles
    coords = got_ref[:, SLOTS * HALF :, :].astype(F32).reshape(tiles, groups, 8, COLS)
    coords = jnp.sum(coords, axis=1)
    y_pixel = (lax.broadcasted_iota(jnp.int32, (GRID, 1), 0) - GRID // 2).astype(F32)
    order = lax.broadcasted_iota(jnp.int32, (16, 1), 0)
    x_pixel = (16 * chip + 8 * ((order // 8) ^ half) + order % 8 - GRID // 2).astype(F32)
    scale = 1.0 / (2.0 * GRID)
    for tile in range(tiles):
        u = coords[tile, 0:1, :] * scale
        v = coords[tile, 1:2, :] * scale
        cx, sx = cos_sin_turns(x_pixel * u)
        cy, sy = cos_sin_turns(y_pixel * v)
        lanes = slice(tile * 128, (tile + 1) * 128)
        for x in range(16):
            a, b = cx[x : x + 1], sx[x : x + 1]
            tab_ref[x * GRID : (x + 1) * GRID, lanes] = (a * cy - b * sy).astype(BF16)
            tab_ref[512 + x * GRID : 512 + (x + 1) * GRID, lanes] = (b * cy + a * sy).astype(BF16)
    rows = got_ref[:, : SLOTS * HALF, :].reshape(N_TB * SLOTS * HALF, COLS)
    total = jnp.dot(tab_ref[...], rows, preferred_element_type=F32) * float(ROWS_DEV) ** (-0.5)
    for part in range(2):
        keep_ref[part] = total[part * 512 : part * 512 + 256]
        give_ref[part] = total[part * 512 + 256 : part * 512 + 512]


def grid_rows(ids, got):
    return pl.pallas_call(
        grid_kernel,
        out_shape=(
            jax.ShapeDtypeStruct((2, PIX // N_DIR, COLS), F32),
            jax.ShapeDtypeStruct((2, PIX // N_DIR, COLS), F32),
        ),
        in_specs=[smem(), vmem()],
        out_specs=(vmem(), vmem()),
        scratch_shapes=[pltpu.VMEM((1024, N_TB * SLOTS * HALF), BF16)],
        compiler_params=params(24),
        name="grid",
    )(ids, got)


def after(value, done):
    return lax.optimization_barrier((value, done))[0]


def swap(value, flip):
    return lax.ppermute(value, "dir", [(i, i ^ flip) for i in range(N_DIR)])


def local(
    visibilities, uv_coords, comp_lm, spectra, ridge_weight, assignment, peel_order, block_tile
):
    me = lax.axis_index("dir")
    station = lax.axis_index("tb")
    ids = jnp.stack([me, me % 2, (station % 4) * BB]).astype(jnp.int32)
    lm8, uv8, wide = prepare(peel_order, assignment, comp_lm, uv_coords, spectra)
    (far_a,) = predict((2,), ids, uv8, lm8, wide)
    got_a = swap(far_a, 2)
    (far_b,) = predict((3,), ids, uv8, lm8, wide)
    got_b = swap(far_b, 3)
    near, own = predict((1, 0), ids, uv8, lm8, wide)
    got_near = swap(near, 1)
    rows = peel(ids, visibilities, ridge_weight, (own, got_near, got_a, got_b))
    gathered = (rows, swap(rows, 1), swap(rows, 2), swap(rows, 3))
    tile_ids = block_tile[:, 0]
    base, slots = label(after(ids, rows), tile_ids, block_tile, uv_coords)
    send = pack(ids, tile_ids, slots, gathered, base)
    got = lax.all_to_all(send, "tb", split_axis=0, concat_axis=0, tiled=True)
    residual = join(after(ids, send), gathered)
    keep, give = grid_rows(after(ids, residual), got)
    subgrids = (keep + swap(give, 1))[None]
    return residual, subgrids


def solution(mesh):
    return jax.shard_map(
        local,
        mesh=mesh,
        in_specs=(
            P("tb", None),
            P(None, "tb"),
            P(None, "dir"),
            P(None, "dir", None),
            P(),
            P("dir"),
            P("dir"),
            P("tb", None),
        ),
        out_specs=(P("tb", None), P("tb", None, "dir", None)),
        check_vma=False,
    )
```

```python
import jax
import jax.numpy as jnp
from jax import lax
from jax.experimental import pallas as pl
from jax.experimental.pallas import tpu as pltpu
from jax.sharding import PartitionSpec as P

NCOMP = 1024
GRID = 32
DIR_DEV = 3
ITERS = 4
BB = 32
GB = 128
ROWS_DEV = 1024
PIX = 1024
COLS = 128
N_DIR = 4
N_TB = 64
NB = 32
SLOTS = 2
QROWS = ROWS_DEV // N_DIR
PART = BB // N_DIR
POOL = DIR_DEV * NCOMP
WIDE = DIR_DEV * COLS
CHUNK = 256
NCHUNK = POOL // CHUNK
SEND_ROWS = SLOTS * PART + 8
QBLOCKS = QROWS // BB

F32 = jnp.float32
BF16 = jnp.bfloat16

SIN_C = (2.6417407853784525, -1.0859537956447276, 0.1306204657138272)
COS_C = (1.681792784129167, -2.074822793580374, 0.42650038149094444, -0.03432262097868313)
ROOT2 = 1.4142135623730951


def vmem():
    return pl.BlockSpec(memory_space=pltpu.VMEM)


def smem():
    return pl.BlockSpec(memory_space=pltpu.SMEM)


def params(mib):
    return pltpu.CompilerParams(vmem_limit_bytes=mib << 20)


def cos_sin_turns(turns):
    r = turns - jnp.round(turns)
    z = r * r
    s = ((SIN_C[2] * z + SIN_C[1]) * z + SIN_C[0]) * r
    c = ((COS_C[3] * z + COS_C[2]) * z + COS_C[1]) * z + COS_C[0]
    s1 = s * c
    c1 = ROOT2 - s * s
    return 1.0 - s1 * s1, s1 * c1


def three_parts(value):
    high = value.astype(BF16)
    left = value - high.astype(F32)
    mid = left.astype(BF16)
    low = (left - mid.astype(F32)).astype(BF16)
    return high, mid, low


def prepare_kernel(
    order_hbm, assign_hbm, lm_hbm, uv_hbm, spec_hbm, lm8_ref, uv8_ref, wide_ref,
    order_ref, assign_ref, lm_ref, uv_ref, spec_ref, pos_ref, sems
):
    pairs = (
        (assign_hbm, assign_ref), (order_hbm, order_ref), (lm_hbm, lm_ref), (uv_hbm, uv_ref), (spec_hbm, spec_ref)
    )
    copies = [pltpu.make_async_copy(src, dst, sems.at[n]) for n, (src, dst) in enumerate(pairs)]
    for copy in copies:
        copy.start()
    for copy in copies[:4]:
        copy.wait()
    lh, lmid, ll = three_parts(lm_ref[...])
    zero = jnp.zeros((2, POOL), BF16)
    lm8_ref[...] = jnp.concatenate(
        [lh[0:1], lmid[0:1], ll[0:1], lh[1:2], lmid[1:2], ll[1:2], zero], axis=0
    )
    for q in range(N_DIR):
        u = uv_ref[0:1, q * QROWS : (q + 1) * QROWS]
        v = uv_ref[1:2, q * QROWS : (q + 1) * QROWS]
        uv8_ref[q] = jnp.concatenate([u, u, u, v, v, v, jnp.zeros((2, QROWS), BF16)], axis=0)
    assign = assign_ref[...]
    low = assign & 127
    high = assign >> 7
    segment = lax.broadcasted_iota(jnp.int32, (1, POOL), 1) // NCOMP
    place = jnp.zeros((1, POOL), F32)
    for p in range(DIR_DEV):
        place = jnp.where(segment == order_ref[p], float(p), place)
    low_hot = (lax.broadcasted_iota(jnp.int32, (128, POOL), 0) == low).astype(F32).astype(BF16)
    high_hot = jnp.where(lax.broadcasted_iota(jnp.int32, (32, POOL), 0) == high, place, 0.0).astype(BF16)
    pos = lax.dot_general(low_hot, high_hot, (((1,), (1,)), ((), ())), preferred_element_type=F32)
    column = lax.broadcasted_iota(jnp.int32, (32, POOL), 1) // 128
    pick = (column == lax.broadcasted_iota(jnp.int32, (32, POOL), 0)).astype(F32).astype(BF16)
    pos_ref[...] = jnp.dot(pos.astype(BF16), pick, preferred_element_type=F32)
    copies[4].wait()
    for column in range(POOL // 128):
        place_here = pos_ref[:, column * 128 : (column + 1) * 128]
        for p in range(DIR_DEV):
            mask = jnp.where(place_here == float(p), 1.0, 0.0).astype(BF16)
            for part in range(2):
                first = part * CHUNK + (column % 2) * 128
                wide_ref[column // 2, first : first + 128, p * COLS : (p + 1) * COLS] = (
                    spec_ref[part, column * 128 : (column + 1) * 128, :] * mask
                )


def prepare(peel_order, assignment, comp_lm, uv_coords, spectra):
    return pl.pallas_call(
        prepare_kernel,
        out_shape=(
            jax.ShapeDtypeStruct((8, POOL), BF16),
            jax.ShapeDtypeStruct((N_DIR, 8, QROWS), BF16),
            jax.ShapeDtypeStruct((NCHUNK, 2 * CHUNK, WIDE), BF16),
        ),
        in_specs=[pl.BlockSpec(memory_space=pltpu.MemorySpace.HBM)] * 5,
        out_specs=(vmem(), vmem(), vmem()),
        scratch_shapes=[
            pltpu.SMEM((DIR_DEV,), jnp.int32),
            pltpu.VMEM((1, POOL), jnp.int32),
            pltpu.VMEM((2, POOL), F32),
            pltpu.VMEM((2, ROWS_DEV), BF16),
            pltpu.VMEM((2, POOL, COLS), BF16),
            pltpu.VMEM((128, POOL), F32),
            pltpu.SemaphoreType.DMA((5,)),
        ],
        compiler_params=params(16),
        name="prepare",
    )(*(
        pltpu.with_memory_space_constraint(value, pltpu.MemorySpace.HBM)
        for value in (peel_order, assignment.reshape(1, POOL), comp_lm, uv_coords, spectra)
    ))


def predict_kernel(flips, ids_ref, uv8_ref, lm8_ref, wide_ref, *rest):
    out_refs = rest[: len(flips)]
    tab_a, tab_b, acc_ref = rest[len(flips) :]
    me = ids_ref[0]
    uv_rows = jnp.concatenate([uv8_ref[me ^ x].astype(F32).T for x in flips], axis=0).astype(BF16)

    def table(j, tab_ref):
        lm = lm8_ref[:, j * CHUNK : (j + 1) * CHUNK]
        turns = jnp.dot(uv_rows, lm, preferred_element_type=F32)
        cos, sin = cos_sin_turns(turns)
        tab_ref[:, :CHUNK] = cos.astype(BF16)
        tab_ref[:, CHUNK:] = sin.astype(BF16)

    tabs = (tab_a, tab_b)
    table(0, tab_a)
    for j in range(NCHUNK):
        if j + 1 < NCHUNK:
            table(j + 1, tabs[(j + 1) % 2])
        part = jnp.dot(tabs[j % 2][...], wide_ref[j], preferred_element_type=F32)
        if j == 0:
            acc_ref[...] = part
        else:
            acc_ref[...] += part
    for n in range(len(flips)):
        for p in range(DIR_DEV):
            out_refs[n][p] = acc_ref[n * QROWS : (n + 1) * QROWS, p * COLS : (p + 1) * COLS].astype(BF16)


def predict(flips, ids, uv8, lm8, wide):
    rows = QROWS * len(flips)

    def kernel(*refs):
        predict_kernel(flips, *refs)

    return pl.pallas_call(
        kernel,
        out_shape=tuple(jax.ShapeDtypeStruct((DIR_DEV, QROWS, COLS), BF16) for _ in flips),
        in_specs=[smem(), vmem(), vmem(), vmem()],
        out_specs=tuple(vmem() for _ in flips),
        scratch_shapes=[
            pltpu.VMEM((rows, 2 * CHUNK), BF16),
            pltpu.VMEM((rows, 2 * CHUNK), BF16),
            pltpu.VMEM((rows, WIDE), F32),
        ],
        cost_estimate=pl.CostEstimate(
            flops=2 * rows * 2 * POOL * 2 * WIDE,
            transcendentals=0,
            bytes_accessed=2 * (2 * POOL * WIDE + rows * WIDE),
        ),
        compiler_params=params(16),
        name="predict",
    )(ids, uv8, lm8, wide)


def per_block_sum(value):
    return jnp.sum(value.reshape(QROWS // GB, GB, COLS), axis=1)


def peel_kernel(ids_ref, vis_ref, ridge_ref, m0_ref, m1_ref, m2_ref, m3_ref, out_ref, *rest):
    part_refs, (model_ref, inv_ref, part_ref) = rest[:N_DIR], rest[N_DIR:]
    me = ids_ref[0]
    ridge = ridge_ref[...]
    for x, ref in enumerate((m0_ref, m1_ref, m2_ref, m3_ref)):
        owner = me ^ x
        for p in range(DIR_DEV):
            model = ref[p].astype(F32)
            model_ref[owner * DIR_DEV + p] = model
            inv_ref[owner * DIR_DEV + p] = 1.0 / (per_block_sum(model * model) + ridge)
    lane = lax.broadcasted_iota(jnp.int32, (QROWS // GB, COLS), 1)

    def neighbours(gain):
        lower = jnp.where(lane < 2, gain, pltpu.roll(gain, 2, 1))
        upper = jnp.where(lane >= COLS - 2, gain, pltpu.roll(gain, COLS - 2, 1))
        return 0.5 * (lower + upper)

    remains = vis_ref[pl.ds(pl.multiple_of(me * QROWS, QROWS), QROWS), :].astype(F32)
    for j in range(N_DIR * DIR_DEV):
        model = model_ref[j]
        inv = inv_ref[j]
        cross = per_block_sum(remains * model) * inv
        pull = ridge * inv
        gain = cross + pull
        for _ in range(ITERS - 1):
            gain = cross + pull * neighbours(gain)
        spread = jnp.concatenate(
            [jnp.broadcast_to(gain[b : b + 1], (GB, COLS)) for b in range(QROWS // GB)], axis=0
        )
        remains = remains - spread * model
        if (j + 1) % DIR_DEV == 0:
            remains = remains.astype(BF16).astype(F32)
    out_ref[...] = remains.astype(BF16)
    part_ref[...] = remains.reshape(QBLOCKS, N_DIR, PART, COLS)
    for x in range(N_DIR):
        part_refs[x][...] = part_ref[:, me ^ x].astype(BF16)


def peel(ids, visibilities, ridge_weight, models):
    out = pl.pallas_call(
        peel_kernel,
        out_shape=(jax.ShapeDtypeStruct((QROWS, COLS), BF16),)
        + (jax.ShapeDtypeStruct((QBLOCKS, PART, COLS), BF16),) * N_DIR,
        in_specs=[smem()] + [vmem()] * 6,
        out_specs=(vmem(),) * (1 + N_DIR),
        scratch_shapes=[
            pltpu.VMEM((N_DIR * DIR_DEV, QROWS, COLS), F32),
            pltpu.VMEM((N_DIR * DIR_DEV, QROWS // GB, COLS), F32),
            pltpu.VMEM((QBLOCKS, N_DIR, PART, COLS), F32),
        ],
        compiler_params=params(16),
        name="peel",
    )(ids, visibilities, ridge_weight.reshape(1, COLS), *models)
    return out[0], out[1:]


def label_kernel(ids_ref, tile_id_ref, tile_ref, uv_ref, out_ref, slot_ref, seen_ref):
    me = ids_ref[0]
    offset = ids_ref[2]
    tiles = tile_ref[...].astype(F32)
    block_of_lane = lax.broadcasted_iota(jnp.int32, (NB, ROWS_DEV), 1) // BB
    expand = (block_of_lane == lax.broadcasted_iota(jnp.int32, (NB, ROWS_DEV), 0)).astype(F32)
    tile_of_lane = jnp.sum(expand * tiles, axis=0, keepdims=True)
    sub = lax.broadcasted_iota(jnp.int32, (NB, NB), 0)
    col = lax.broadcasted_iota(jnp.int32, (NB, NB), 1)
    tile_row = jnp.sum(jnp.where(sub == col, tiles, 0.0), axis=0, keepdims=True)
    slot = jnp.sum(jnp.where((tiles == tile_row) & (col < sub), 1.0, 0.0), axis=1, keepdims=True)
    slot_of_row = lax.dot_general(
        expand.astype(BF16),
        jnp.broadcast_to(slot, (NB, COLS)).astype(BF16),
        (((0,), (0,)), ((), ())),
        preferred_element_type=F32,
    )
    within = lax.broadcasted_iota(jnp.int32, (ROWS_DEV, COLS), 0) % BB - me * PART
    lane = lax.broadcasted_iota(jnp.int32, (ROWS_DEV, COLS), 1)
    goal = slot_of_row.astype(jnp.int32) * PART + within + offset
    spot = jnp.where((goal == lane) & (within >= 0) & (within < PART), 1.0, 0.0).astype(BF16)
    row = lax.broadcasted_iota(jnp.int32, (N_TB * 8, ROWS_DEV), 0)
    u = uv_ref[0:1, :].astype(F32)
    v = uv_ref[1:2, :].astype(F32)
    value = jnp.where(row % 8 == 0, u, jnp.where(row % 8 == 1, v, 0.0))
    value = jnp.where((row // 8).astype(F32) == tile_of_lane, value, 0.0).astype(BF16)
    out = jnp.dot(value, spot, preferred_element_type=F32)
    out_ref[:, : SLOTS * PART, :] = jnp.zeros((N_TB, SLOTS * PART, COLS), BF16)
    out_ref[:, SLOTS * PART :, :] = out.reshape(N_TB, 8, COLS).astype(BF16)
    for t in range(N_TB):
        seen_ref[t] = 0
    for b in range(NB):
        tile = tile_id_ref[b]
        slot_ref[b] = seen_ref[tile]
        seen_ref[tile] = 1


def label(ids, tile_ids, block_tile, uv_coords):
    return pl.pallas_call(
        label_kernel,
        out_shape=(
            jax.ShapeDtypeStruct((N_TB, SEND_ROWS, COLS), BF16),
            jax.ShapeDtypeStruct((NB,), jnp.int32),
        ),
        in_specs=[smem(), smem(), vmem(), vmem()],
        out_specs=(vmem(), smem()),
        scratch_shapes=[pltpu.SMEM((N_TB,), jnp.int32)],
        compiler_params=params(16),
        name="label",
    )(ids, tile_ids, block_tile, uv_coords)


def pack_kernel(ids_ref, tile_ref, slot_ref, r0_ref, r1_ref, r2_ref, r3_ref, base_ref, out_ref, stage_ref):
    me = ids_ref[0]
    out_ref[...] = base_ref[...]
    for x, ref in enumerate((r0_ref, r1_ref, r2_ref, r3_ref)):
        stage_ref[pl.ds((me ^ x) * QBLOCKS, QBLOCKS)] = ref[...]
    for b in range(NB):
        first = pl.multiple_of(slot_ref[b] * PART, PART)
        out_ref[tile_ref[b], pl.ds(first, PART), :] = stage_ref[b]


def pack(ids, tile_ids, slots, rows, base):
    return pl.pallas_call(
        pack_kernel,
        out_shape=jax.ShapeDtypeStruct((N_TB, SEND_ROWS, COLS), BF16),
        in_specs=[smem(), smem(), smem()] + [vmem()] * 5,
        out_specs=vmem(),
        scratch_shapes=[pltpu.VMEM((NB, PART, COLS), BF16)],
        compiler_params=params(16),
        name="pack",
    )(ids, tile_ids, slots, *rows, base)


def join_kernel(ids_ref, r0_ref, r1_ref, r2_ref, r3_ref, out_ref):
    me = ids_ref[0]
    for x, ref in enumerate((r0_ref, r1_ref, r2_ref, r3_ref)):
        out_ref[pl.ds(pl.multiple_of((me ^ x) * QROWS, QROWS), QROWS), :] = ref[...]


def join(ids, rows):
    return pl.pallas_call(
        join_kernel,
        out_shape=jax.ShapeDtypeStruct((ROWS_DEV, COLS), BF16),
        in_specs=[smem()] + [vmem()] * 4,
        out_specs=vmem(),
        compiler_params=params(16),
        name="join",
    )(ids, *rows)


def grid_kernel(other, ids_ref, mine_ref, partner_ref, out_ref, tab_ref, row_ref):
    chip = (ids_ref[0] // 2) ^ other
    core = ids_ref[1]
    tiles = N_TB * SLOTS * PART // 128
    groups = N_TB // tiles
    y_pixel = (lax.broadcasted_iota(jnp.int32, (GRID, 1), 0) - GRID // 2).astype(F32)
    order = lax.broadcasted_iota(jnp.int32, (8, 1), 0)
    x_pixel = (16 * chip + 8 * core + order - GRID // 2).astype(F32)
    scale = 1.0 / (2.0 * GRID)
    for n, ref in enumerate((mine_ref, partner_ref)):
        coords = ref[:, SLOTS * PART :, :].astype(F32).reshape(tiles, groups, 8, COLS)
        coords = jnp.sum(coords, axis=1)
        for tile in range(tiles):
            u = coords[tile, 0:1, :] * scale
            v = coords[tile, 1:2, :] * scale
            cx, sx = cos_sin_turns(x_pixel * u)
            cy, sy = cos_sin_turns(y_pixel * v)
            first = (n * tiles + tile) * 128
            lanes = slice(first, first + 128)
            for x in range(8):
                a, b = cx[x : x + 1], sx[x : x + 1]
                tab_ref[x * GRID : (x + 1) * GRID, lanes] = (a * cy - b * sy).astype(BF16)
                tab_ref[256 + x * GRID : 256 + (x + 1) * GRID, lanes] = (b * cy + a * sy).astype(BF16)
        row_ref[n * tiles * 128 : (n + 1) * tiles * 128, :] = ref[:, : SLOTS * PART, :].reshape(
            tiles * 128, COLS
        )
    total = jnp.dot(tab_ref[...], row_ref[...], preferred_element_type=F32) * float(ROWS_DEV) ** (-0.5)
    out_ref[...] = total.reshape(2, PIX // N_DIR, COLS)


def grid_rows(other, ids, mine, partner):
    def kernel(*refs):
        grid_kernel(other, *refs)

    return pl.pallas_call(
        kernel,
        out_shape=jax.ShapeDtypeStruct((2, PIX // N_DIR, COLS), F32),
        in_specs=[smem(), vmem(), vmem()],
        out_specs=vmem(),
        scratch_shapes=[pltpu.VMEM((512, 2048), BF16), pltpu.VMEM((2048, COLS), BF16)],
        cost_estimate=pl.CostEstimate(flops=2 * 10**9, transcendentals=0, bytes_accessed=10**6),
        compiler_params=params(24),
        name="grid",
    )(ids, mine, partner)


def after(value, done):
    return lax.optimization_barrier((value, done))[0]


def swap(value, flip):
    return lax.ppermute(value, "dir", [(i, i ^ flip) for i in range(N_DIR)])


def local(
    visibilities, uv_coords, comp_lm, spectra, ridge_weight, assignment, peel_order, block_tile
):
    me = lax.axis_index("dir")
    station = lax.axis_index("tb")
    ids = jnp.stack([me, me % 2, (station % 8) * (SLOTS * PART)]).astype(jnp.int32)
    lm8, uv8, wide = prepare(peel_order, assignment, comp_lm, uv_coords, spectra)
    (far_a,) = predict((2,), ids, uv8, lm8, wide)
    got_a = swap(far_a, 2)
    (far_b,) = predict((3,), ids, uv8, lm8, wide)
    got_b = swap(far_b, 3)
    near, own = predict((1, 0), ids, uv8, lm8, wide)
    got_near = swap(near, 1)
    rows, parts = peel(ids, visibilities, ridge_weight, (own, got_near, got_a, got_b))
    tile_ids = block_tile[:, 0]
    base, slots = label(after(ids, rows), tile_ids, block_tile, uv_coords)
    shared = [parts[0]] + [swap(parts[x], x) for x in range(1, N_DIR)]
    send = pack(ids, tile_ids, slots, shared, base)
    got = lax.all_to_all(send, "tb", split_axis=0, concat_axis=0, tiled=True)
    late = after(rows, send)
    residual = join(ids, [late] + [swap(late, x) for x in range(1, N_DIR)])
    got = after(got, residual)
    partner = swap(got, 1)
    give = grid_rows(1, ids, got, partner)
    moved = swap(give, 2)
    keep = grid_rows(0, ids, got, partner)
    return residual, (keep + moved)[None]


def solution(mesh):
    return jax.shard_map(
        local,
        mesh=mesh,
        in_specs=(
            P("tb", None),
            P(None, "tb"),
            P(None, "dir"),
            P(None, "dir", None),
            P(),
            P("dir"),
            P("dir"),
            P("tb", None),
        ),
        out_specs=(P("tb", None), P("tb", None, "dir", None)),
        check_vma=False,
    )
```

```python
import jax
import jax.numpy as jnp
from jax import lax
from jax.experimental import pallas as pl
from jax.experimental.pallas import tpu as pltpu
from jax.sharding import PartitionSpec as P

NCOMP = 1024
GRID = 32
DIR_DEV = 3
ITERS = 4
BB = 32
GB = 128
ROWS_DEV = 1024
PIX = 1024
COLS = 128
N_DIR = 4
N_TB = 64
NB = 32
SLOTS = 2
QROWS = ROWS_DEV // N_DIR
PART = BB // 2
POOL = DIR_DEV * NCOMP
WIDE = DIR_DEV * COLS
CHUNK = 256
NCHUNK = POOL // CHUNK
SEND_ROWS = SLOTS * PART + 8
QBLOCKS = QROWS // BB

F32 = jnp.float32
BF16 = jnp.bfloat16

SIN_C = (2.6417407853784525, -1.0859537956447276, 0.1306204657138272)
COS_C = (1.681792784129167, -2.074822793580374, 0.42650038149094444, -0.03432262097868313)
ROOT2 = 1.4142135623730951


def vmem():
    return pl.BlockSpec(memory_space=pltpu.VMEM)


def smem():
    return pl.BlockSpec(memory_space=pltpu.SMEM)


def params(mib):
    return pltpu.CompilerParams(vmem_limit_bytes=mib << 20)


def cos_sin_turns(turns):
    r = turns - jnp.round(turns)
    z = r * r
    s = ((SIN_C[2] * z + SIN_C[1]) * z + SIN_C[0]) * r
    c = ((COS_C[3] * z + COS_C[2]) * z + COS_C[1]) * z + COS_C[0]
    s1 = s * c
    c1 = ROOT2 - s * s
    return 1.0 - s1 * s1, s1 * c1


def three_parts(value):
    high = value.astype(BF16)
    left = value - high.astype(F32)
    mid = left.astype(BF16)
    low = (left - mid.astype(F32)).astype(BF16)
    return high, mid, low


def prepare_kernel(
    order_hbm, assign_hbm, lm_hbm, uv_hbm, spec_hbm, lm8_ref, uv8_ref, wide_ref,
    order_ref, assign_ref, lm_ref, uv_ref, spec_ref, pos_ref, sems
):
    pairs = (
        (assign_hbm, assign_ref), (order_hbm, order_ref), (lm_hbm, lm_ref), (uv_hbm, uv_ref), (spec_hbm, spec_ref)
    )
    copies = [pltpu.make_async_copy(src, dst, sems.at[n]) for n, (src, dst) in enumerate(pairs)]
    for copy in copies:
        copy.start()
    for copy in copies[:4]:
        copy.wait()
    lh, lmid, ll = three_parts(lm_ref[...])
    zero = jnp.zeros((2, POOL), BF16)
    lm8_ref[...] = jnp.concatenate(
        [lh[0:1], lmid[0:1], ll[0:1], lh[1:2], lmid[1:2], ll[1:2], zero], axis=0
    )
    for q in range(N_DIR):
        u = uv_ref[0:1, q * QROWS : (q + 1) * QROWS]
        v = uv_ref[1:2, q * QROWS : (q + 1) * QROWS]
        uv8_ref[q] = jnp.concatenate([u, u, u, v, v, v, jnp.zeros((2, QROWS), BF16)], axis=0)
    assign = assign_ref[...]
    low = assign & 127
    high = assign >> 7
    segment = lax.broadcasted_iota(jnp.int32, (1, POOL), 1) // NCOMP
    place = jnp.zeros((1, POOL), F32)
    for p in range(DIR_DEV):
        place = jnp.where(segment == order_ref[p], float(p), place)
    low_hot = (lax.broadcasted_iota(jnp.int32, (128, POOL), 0) == low).astype(F32).astype(BF16)
    high_hot = jnp.where(lax.broadcasted_iota(jnp.int32, (32, POOL), 0) == high, place, 0.0).astype(BF16)
    pos = lax.dot_general(low_hot, high_hot, (((1,), (1,)), ((), ())), preferred_element_type=F32)
    column = lax.broadcasted_iota(jnp.int32, (32, POOL), 1) // 128
    pick = (column == lax.broadcasted_iota(jnp.int32, (32, POOL), 0)).astype(F32).astype(BF16)
    pos_ref[...] = jnp.dot(pos.astype(BF16), pick, preferred_element_type=F32)
    copies[4].wait()
    for column in range(POOL // 128):
        place_here = pos_ref[:, column * 128 : (column + 1) * 128]
        for p in range(DIR_DEV):
            mask = jnp.where(place_here == float(p), 1.0, 0.0).astype(BF16)
            for part in range(2):
                first = part * CHUNK + (column % 2) * 128
                wide_ref[column // 2, first : first + 128, p * COLS : (p + 1) * COLS] = (
                    spec_ref[part, column * 128 : (column + 1) * 128, :] * mask
                )


def prepare(peel_order, assignment, comp_lm, uv_coords, spectra):
    return pl.pallas_call(
        prepare_kernel,
        out_shape=(
            jax.ShapeDtypeStruct((8, POOL), BF16),
            jax.ShapeDtypeStruct((N_DIR, 8, QROWS), BF16),
            jax.ShapeDtypeStruct((NCHUNK, 2 * CHUNK, WIDE), BF16),
        ),
        in_specs=[pl.BlockSpec(memory_space=pltpu.MemorySpace.HBM)] * 5,
        out_specs=(vmem(), vmem(), vmem()),
        scratch_shapes=[
            pltpu.SMEM((DIR_DEV,), jnp.int32),
            pltpu.VMEM((1, POOL), jnp.int32),
            pltpu.VMEM((2, POOL), F32),
            pltpu.VMEM((2, ROWS_DEV), BF16),
            pltpu.VMEM((2, POOL, COLS), BF16),
            pltpu.VMEM((128, POOL), F32),
            pltpu.SemaphoreType.DMA((5,)),
        ],
        compiler_params=params(16),
        name="prepare",
    )(*(
        pltpu.with_memory_space_constraint(value, pltpu.MemorySpace.HBM)
        for value in (peel_order, assignment.reshape(1, POOL), comp_lm, uv_coords, spectra)
    ))


def predict_kernel(flips, ids_ref, uv8_ref, lm8_ref, wide_ref, *rest):
    out_refs = rest[: len(flips)]
    tab_a, tab_b, acc_ref = rest[len(flips) :]
    me = ids_ref[0]
    uv_rows = jnp.concatenate([uv8_ref[me ^ x].astype(F32).T for x in flips], axis=0).astype(BF16)

    def table(j, tab_ref):
        lm = lm8_ref[:, j * CHUNK : (j + 1) * CHUNK]
        turns = jnp.dot(uv_rows, lm, preferred_element_type=F32)
        cos, sin = cos_sin_turns(turns)
        tab_ref[:, :CHUNK] = cos.astype(BF16)
        tab_ref[:, CHUNK:] = sin.astype(BF16)

    tabs = (tab_a, tab_b)
    table(0, tab_a)
    for j in range(NCHUNK):
        if j + 1 < NCHUNK:
            table(j + 1, tabs[(j + 1) % 2])
        part = jnp.dot(tabs[j % 2][...], wide_ref[j], preferred_element_type=F32)
        if j == 0:
            acc_ref[...] = part
        else:
            acc_ref[...] += part
    for n in range(len(flips)):
        for p in range(DIR_DEV):
            out_refs[n][p] = acc_ref[n * QROWS : (n + 1) * QROWS, p * COLS : (p + 1) * COLS].astype(BF16)


def predict(flips, ids, uv8, lm8, wide):
    rows = QROWS * len(flips)

    def kernel(*refs):
        predict_kernel(flips, *refs)

    return pl.pallas_call(
        kernel,
        out_shape=tuple(jax.ShapeDtypeStruct((DIR_DEV, QROWS, COLS), BF16) for _ in flips),
        in_specs=[smem(), vmem(), vmem(), vmem()],
        out_specs=tuple(vmem() for _ in flips),
        scratch_shapes=[
            pltpu.VMEM((rows, 2 * CHUNK), BF16),
            pltpu.VMEM((rows, 2 * CHUNK), BF16),
            pltpu.VMEM((rows, WIDE), F32),
        ],
        cost_estimate=pl.CostEstimate(
            flops=2 * rows * 2 * POOL * 2 * WIDE,
            transcendentals=0,
            bytes_accessed=2 * (2 * POOL * WIDE + rows * WIDE),
        ),
        compiler_params=params(16),
        name="predict",
    )(ids, uv8, lm8, wide)


def per_block_sum(value):
    return jnp.sum(value.reshape(QROWS // GB, GB, COLS), axis=1)


def peel_kernel(ids_ref, vis_ref, ridge_ref, m0_ref, m1_ref, m2_ref, m3_ref, out_ref, *rest):
    part_refs, (model_ref, inv_ref, part_ref) = rest[:N_DIR], rest[N_DIR:]
    me = ids_ref[0]
    ridge = ridge_ref[...]
    for x, ref in enumerate((m0_ref, m1_ref, m2_ref, m3_ref)):
        owner = me ^ x
        for p in range(DIR_DEV):
            model = ref[p].astype(F32)
            model_ref[owner * DIR_DEV + p] = model
            inv_ref[owner * DIR_DEV + p] = 1.0 / (per_block_sum(model * model) + ridge)
    lane = lax.broadcasted_iota(jnp.int32, (QROWS // GB, COLS), 1)

    def neighbours(gain):
        lower = jnp.where(lane < 2, gain, pltpu.roll(gain, 2, 1))
        upper = jnp.where(lane >= COLS - 2, gain, pltpu.roll(gain, COLS - 2, 1))
        return 0.5 * (lower + upper)

    remains = vis_ref[pl.ds(pl.multiple_of(me * QROWS, QROWS), QROWS), :].astype(F32)
    for j in range(N_DIR * DIR_DEV):
        model = model_ref[j]
        inv = inv_ref[j]
        cross = per_block_sum(remains * model) * inv
        pull = ridge * inv
        gain = cross + pull
        for _ in range(ITERS - 1):
            gain = cross + pull * neighbours(gain)
        spread = jnp.concatenate(
            [jnp.broadcast_to(gain[b : b + 1], (GB, COLS)) for b in range(QROWS // GB)], axis=0
        )
        remains = remains - spread * model
        if (j + 1) % DIR_DEV == 0:
            remains = remains.astype(BF16).astype(F32)
    out_ref[...] = remains.astype(BF16)
    part_ref[...] = remains.reshape(QBLOCKS, 2, PART, COLS)
    for x in range(N_DIR):
        part_refs[x][...] = part_ref[:, (me ^ x) & 1].astype(BF16)


def peel(ids, visibilities, ridge_weight, models):
    out = pl.pallas_call(
        peel_kernel,
        out_shape=(jax.ShapeDtypeStruct((QROWS, COLS), BF16),)
        + (jax.ShapeDtypeStruct((QBLOCKS, PART, COLS), BF16),) * N_DIR,
        in_specs=[smem()] + [vmem()] * 6,
        out_specs=(vmem(),) * (1 + N_DIR),
        scratch_shapes=[
            pltpu.VMEM((N_DIR * DIR_DEV, QROWS, COLS), F32),
            pltpu.VMEM((N_DIR * DIR_DEV, QROWS // GB, COLS), F32),
            pltpu.VMEM((QBLOCKS, 2, PART, COLS), F32),
        ],
        compiler_params=params(16),
        name="peel",
    )(ids, visibilities, ridge_weight.reshape(1, COLS), *models)
    return out[0], out[1:]


def label_kernel(ids_ref, tile_id_ref, tile_ref, uv_ref, out_ref, slot_ref, seen_ref):
    half = ids_ref[1]
    offset = ids_ref[2]
    tiles = tile_ref[...].astype(F32)
    block_of_lane = lax.broadcasted_iota(jnp.int32, (NB, ROWS_DEV), 1) // BB
    expand = (block_of_lane == lax.broadcasted_iota(jnp.int32, (NB, ROWS_DEV), 0)).astype(F32)
    tile_of_lane = jnp.sum(expand * tiles, axis=0, keepdims=True)
    sub = lax.broadcasted_iota(jnp.int32, (NB, NB), 0)
    col = lax.broadcasted_iota(jnp.int32, (NB, NB), 1)
    tile_row = jnp.sum(jnp.where(sub == col, tiles, 0.0), axis=0, keepdims=True)
    slot = jnp.sum(jnp.where((tiles == tile_row) & (col < sub), 1.0, 0.0), axis=1, keepdims=True)
    slot_of_row = lax.dot_general(
        expand.astype(BF16),
        jnp.broadcast_to(slot, (NB, COLS)).astype(BF16),
        (((0,), (0,)), ((), ())),
        preferred_element_type=F32,
    )
    within = lax.broadcasted_iota(jnp.int32, (ROWS_DEV, COLS), 0) % BB - half * PART
    lane = lax.broadcasted_iota(jnp.int32, (ROWS_DEV, COLS), 1)
    goal = slot_of_row.astype(jnp.int32) * PART + within + offset
    spot = jnp.where((goal == lane) & (within >= 0) & (within < PART), 1.0, 0.0).astype(BF16)
    row = lax.broadcasted_iota(jnp.int32, (N_TB * 8, ROWS_DEV), 0)
    u = uv_ref[0:1, :].astype(F32)
    v = uv_ref[1:2, :].astype(F32)
    value = jnp.where(row % 8 == 0, u, jnp.where(row % 8 == 1, v, 0.0))
    value = jnp.where((row // 8).astype(F32) == tile_of_lane, value, 0.0).astype(BF16)
    out = jnp.dot(value, spot, preferred_element_type=F32)
    out_ref[:, : SLOTS * PART, :] = jnp.zeros((N_TB, SLOTS * PART, COLS), BF16)
    out_ref[:, SLOTS * PART :, :] = out.reshape(N_TB, 8, COLS).astype(BF16)
    for t in range(N_TB):
        seen_ref[t] = 0
    for b in range(NB):
        tile = tile_id_ref[b]
        slot_ref[b] = seen_ref[tile]
        seen_ref[tile] = 1


def label(ids, tile_ids, block_tile, uv_coords):
    return pl.pallas_call(
        label_kernel,
        out_shape=(
            jax.ShapeDtypeStruct((N_TB, SEND_ROWS, COLS), BF16),
            jax.ShapeDtypeStruct((NB,), jnp.int32),
        ),
        in_specs=[smem(), smem(), vmem(), vmem()],
        out_specs=(vmem(), smem()),
        scratch_shapes=[pltpu.SMEM((N_TB,), jnp.int32)],
        compiler_params=params(16),
        name="label",
    )(ids, tile_ids, block_tile, uv_coords)


def pack_kernel(ids_ref, tile_ref, slot_ref, r0_ref, r1_ref, r2_ref, r3_ref, base_ref, out_ref, stage_ref):
    me = ids_ref[0]
    out_ref[...] = base_ref[...]
    for x, ref in enumerate((r0_ref, r1_ref, r2_ref, r3_ref)):
        stage_ref[pl.ds((me ^ x) * QBLOCKS, QBLOCKS)] = ref[...]
    for b in range(NB):
        first = pl.multiple_of(slot_ref[b] * PART, PART)
        out_ref[tile_ref[b], pl.ds(first, PART), :] = stage_ref[b]


def pack(ids, tile_ids, slots, rows, base):
    return pl.pallas_call(
        pack_kernel,
        out_shape=jax.ShapeDtypeStruct((N_TB, SEND_ROWS, COLS), BF16),
        in_specs=[smem(), smem(), smem()] + [vmem()] * 5,
        out_specs=vmem(),
        scratch_shapes=[pltpu.VMEM((NB, PART, COLS), BF16)],
        compiler_params=params(16),
        name="pack",
    )(ids, tile_ids, slots, *rows, base)


def join_kernel(ids_ref, r0_ref, r1_ref, r2_ref, r3_ref, out_ref):
    me = ids_ref[0]
    for x, ref in enumerate((r0_ref, r1_ref, r2_ref, r3_ref)):
        out_ref[pl.ds(pl.multiple_of((me ^ x) * QROWS, QROWS), QROWS), :] = ref[...]


def join(ids, rows):
    return pl.pallas_call(
        join_kernel,
        out_shape=jax.ShapeDtypeStruct((ROWS_DEV, COLS), BF16),
        in_specs=[smem()] + [vmem()] * 4,
        out_specs=vmem(),
        compiler_params=params(16),
        name="join",
    )(ids, *rows)


def grid_kernel(ids_ref, got_ref, keep_ref, give_ref, tab_ref):
    chip = ids_ref[0] // 2
    half = ids_ref[1]
    tiles = N_TB * SLOTS * PART // 128
    groups = N_TB // tiles
    coords = got_ref[:, SLOTS * PART :, :].astype(F32).reshape(tiles, groups, 8, COLS)
    coords = jnp.sum(coords, axis=1)
    y_pixel = (lax.broadcasted_iota(jnp.int32, (GRID, 1), 0) - GRID // 2).astype(F32)
    order = lax.broadcasted_iota(jnp.int32, (16, 1), 0)
    x_pixel = (16 * chip + 8 * ((order // 8) ^ half) + order % 8 - GRID // 2).astype(F32)
    scale = 1.0 / (2.0 * GRID)
    for tile in range(tiles):
        u = coords[tile, 0:1, :] * scale
        v = coords[tile, 1:2, :] * scale
        cx, sx = cos_sin_turns(x_pixel * u)
        cy, sy = cos_sin_turns(y_pixel * v)
        lanes = slice(tile * 128, (tile + 1) * 128)
        for x in range(16):
            a, b = cx[x : x + 1], sx[x : x + 1]
            tab_ref[x * GRID : (x + 1) * GRID, lanes] = (a * cy - b * sy).astype(BF16)
            tab_ref[512 + x * GRID : 512 + (x + 1) * GRID, lanes] = (b * cy + a * sy).astype(BF16)
    rows = got_ref[:, : SLOTS * PART, :].reshape(N_TB * SLOTS * PART, COLS)
    total = jnp.dot(tab_ref[...], rows, preferred_element_type=F32) * float(ROWS_DEV) ** (-0.5)
    for part in range(2):
        keep_ref[part] = total[part * 512 : part * 512 + 256]
        give_ref[part] = total[part * 512 + 256 : part * 512 + 512]


def grid_rows(ids, got):
    return pl.pallas_call(
        grid_kernel,
        out_shape=(
            jax.ShapeDtypeStruct((2, PIX // N_DIR, COLS), F32),
            jax.ShapeDtypeStruct((2, PIX // N_DIR, COLS), F32),
        ),
        in_specs=[smem(), vmem()],
        out_specs=(vmem(), vmem()),
        scratch_shapes=[pltpu.VMEM((1024, N_TB * SLOTS * PART), BF16)],
        compiler_params=params(24),
        name="grid",
    )(ids, got)


def after(value, done):
    return lax.optimization_barrier((value, done))[0]


def swap(value, flip):
    return lax.ppermute(value, "dir", [(i, i ^ flip) for i in range(N_DIR)])


def local(
    visibilities, uv_coords, comp_lm, spectra, ridge_weight, assignment, peel_order, block_tile
):
    me = lax.axis_index("dir")
    station = lax.axis_index("tb")
    ids = jnp.stack([me, me % 2, (station % 4) * (SLOTS * PART)]).astype(jnp.int32)
    lm8, uv8, wide = prepare(peel_order, assignment, comp_lm, uv_coords, spectra)
    far_a, far_b = predict((2, 3), ids, uv8, lm8, wide)
    got_a, got_b = swap(far_a, 2), swap(far_b, 3)
    near, own = predict((1, 0), ids, uv8, lm8, wide)
    got_near = swap(near, 1)
    tile_ids = block_tile[:, 0]
    base, slots = label(after(ids, own), tile_ids, block_tile, uv_coords)
    rows, parts = peel(after(ids, slots), visibilities, ridge_weight, (own, got_near, got_a, got_b))
    shared = [parts[0]] + [swap(parts[x], x) for x in range(1, N_DIR)]
    send = pack(ids, tile_ids, slots, shared, base)
    got = lax.all_to_all(send, "tb", split_axis=0, concat_axis=0, tiled=True)
    late = after(rows, send)
    residual = join(ids, [late] + [swap(late, x) for x in range(1, N_DIR)])
    keep, give = grid_rows(after(ids, residual), got)
    return residual, (keep + swap(give, 1))[None]


def solution(mesh):
    return jax.shard_map(
        local,
        mesh=mesh,
        in_specs=(
            P("tb", None),
            P(None, "tb"),
            P(None, "dir"),
            P(None, "dir", None),
            P(),
            P("dir"),
            P("dir"),
            P("tb", None),
        ),
        out_specs=(P("tb", None), P("tb", None, "dir", None)),
        check_vma=False,
    )
```

```python
import jax
import jax.numpy as jnp
from jax import lax
from jax.experimental import pallas as pl
from jax.experimental.pallas import tpu as pltpu
from jax.sharding import PartitionSpec as P

NCOMP = 1024
GRID = 32
DIR_DEV = 3
ITERS = 4
BB = 32
GB = 128
ROWS_DEV = 1024
PIX = 1024
COLS = 128
N_DIR = 4
N_TB = 64
NB = 32
SLOTS = 2
QROWS = ROWS_DEV // N_DIR
PART = BB // 2
POOL = DIR_DEV * NCOMP
WIDE = DIR_DEV * COLS
CHUNK = 256
NCHUNK = POOL // CHUNK
SEND_ROWS = SLOTS * PART + 8
QBLOCKS = QROWS // BB

F32 = jnp.float32
BF16 = jnp.bfloat16

SIN_C = (2.6417407853784525, -1.0859537956447276, 0.1306204657138272)
COS_C = (1.681792784129167, -2.074822793580374, 0.42650038149094444, -0.03432262097868313)
ROOT2 = 1.4142135623730951


def vmem():
    return pl.BlockSpec(memory_space=pltpu.VMEM)


def smem():
    return pl.BlockSpec(memory_space=pltpu.SMEM)


def params(mib):
    return pltpu.CompilerParams(vmem_limit_bytes=mib << 20)


def cos_sin_turns(turns):
    r = turns - jnp.round(turns)
    z = r * r
    s = ((SIN_C[2] * z + SIN_C[1]) * z + SIN_C[0]) * r
    c = ((COS_C[3] * z + COS_C[2]) * z + COS_C[1]) * z + COS_C[0]
    s1 = s * c
    c1 = ROOT2 - s * s
    return 1.0 - s1 * s1, s1 * c1


def three_parts(value):
    high = value.astype(BF16)
    left = value - high.astype(F32)
    mid = left.astype(BF16)
    low = (left - mid.astype(F32)).astype(BF16)
    return high, mid, low


def prepare_kernel(
    order_hbm, assign_hbm, lm_hbm, uv_hbm, spec_hbm, lm8_ref, uv8_ref, wide_ref,
    order_ref, assign_ref, lm_ref, uv_ref, spec_ref, pos_ref, sems
):
    pairs = (
        (assign_hbm, assign_ref), (order_hbm, order_ref), (lm_hbm, lm_ref), (uv_hbm, uv_ref), (spec_hbm, spec_ref)
    )
    copies = [pltpu.make_async_copy(src, dst, sems.at[n]) for n, (src, dst) in enumerate(pairs)]
    for copy in copies:
        copy.start()
    for copy in copies[:4]:
        copy.wait()
    lh, lmid, ll = three_parts(lm_ref[...])
    zero = jnp.zeros((2, POOL), BF16)
    lm8_ref[...] = jnp.concatenate(
        [lh[0:1], lmid[0:1], ll[0:1], lh[1:2], lmid[1:2], ll[1:2], zero], axis=0
    )
    for q in range(N_DIR):
        u = uv_ref[0:1, q * QROWS : (q + 1) * QROWS]
        v = uv_ref[1:2, q * QROWS : (q + 1) * QROWS]
        uv8_ref[q] = jnp.concatenate([u, u, u, v, v, v, jnp.zeros((2, QROWS), BF16)], axis=0)
    assign = assign_ref[...]
    low = assign & 127
    high = assign >> 7
    segment = lax.broadcasted_iota(jnp.int32, (1, POOL), 1) // NCOMP
    place = jnp.zeros((1, POOL), F32)
    for p in range(DIR_DEV):
        place = jnp.where(segment == order_ref[p], float(p), place)
    low_hot = (lax.broadcasted_iota(jnp.int32, (128, POOL), 0) == low).astype(F32).astype(BF16)
    high_hot = jnp.where(lax.broadcasted_iota(jnp.int32, (32, POOL), 0) == high, place, 0.0).astype(BF16)
    pos = lax.dot_general(low_hot, high_hot, (((1,), (1,)), ((), ())), preferred_element_type=F32)
    column = lax.broadcasted_iota(jnp.int32, (32, POOL), 1) // 128
    pick = (column == lax.broadcasted_iota(jnp.int32, (32, POOL), 0)).astype(F32).astype(BF16)
    pos_ref[...] = jnp.dot(pos.astype(BF16), pick, preferred_element_type=F32)
    copies[4].wait()
    for column in range(POOL // 128):
        place_here = pos_ref[:, column * 128 : (column + 1) * 128]
        for p in range(DIR_DEV):
            mask = jnp.where(place_here == float(p), 1.0, 0.0).astype(BF16)
            for part in range(2):
                first = part * CHUNK + (column % 2) * 128
                wide_ref[column // 2, first : first + 128, p * COLS : (p + 1) * COLS] = (
                    spec_ref[part, column * 128 : (column + 1) * 128, :] * mask
                )


def prepare(peel_order, assignment, comp_lm, uv_coords, spectra):
    return pl.pallas_call(
        prepare_kernel,
        out_shape=(
            jax.ShapeDtypeStruct((8, POOL), BF16),
            jax.ShapeDtypeStruct((N_DIR, 8, QROWS), BF16),
            jax.ShapeDtypeStruct((NCHUNK, 2 * CHUNK, WIDE), BF16),
        ),
        in_specs=[pl.BlockSpec(memory_space=pltpu.MemorySpace.HBM)] * 5,
        out_specs=(vmem(), vmem(), vmem()),
        scratch_shapes=[
            pltpu.SMEM((DIR_DEV,), jnp.int32),
            pltpu.VMEM((1, POOL), jnp.int32),
            pltpu.VMEM((2, POOL), F32),
            pltpu.VMEM((2, ROWS_DEV), BF16),
            pltpu.VMEM((2, POOL, COLS), BF16),
            pltpu.VMEM((128, POOL), F32),
            pltpu.SemaphoreType.DMA((5,)),
        ],
        compiler_params=params(16),
        name="prepare",
    )(*(
        pltpu.with_memory_space_constraint(value, pltpu.MemorySpace.HBM)
        for value in (peel_order, assignment.reshape(1, POOL), comp_lm, uv_coords, spectra)
    ))


def predict_kernel(flips, ids_ref, uv8_ref, lm8_ref, wide_ref, *rest):
    out_refs = rest[: len(flips)]
    tab_a, tab_b, acc_ref = rest[len(flips) :]
    me = ids_ref[0]
    uv_rows = jnp.concatenate([uv8_ref[me ^ x].astype(F32).T for x in flips], axis=0).astype(BF16)

    def table(j, tab_ref):
        lm = lm8_ref[:, j * CHUNK : (j + 1) * CHUNK]
        turns = jnp.dot(uv_rows, lm, preferred_element_type=F32)
        cos, sin = cos_sin_turns(turns)
        tab_ref[:, :CHUNK] = cos.astype(BF16)
        tab_ref[:, CHUNK:] = sin.astype(BF16)

    tabs = (tab_a, tab_b)
    table(0, tab_a)
    for j in range(NCHUNK):
        if j + 1 < NCHUNK:
            table(j + 1, tabs[(j + 1) % 2])
        part = jnp.dot(tabs[j % 2][...], wide_ref[j], preferred_element_type=F32)
        if j == 0:
            acc_ref[...] = part
        else:
            acc_ref[...] += part
    for n in range(len(flips)):
        for p in range(DIR_DEV):
            out_refs[n][p] = acc_ref[n * QROWS : (n + 1) * QROWS, p * COLS : (p + 1) * COLS].astype(BF16)


def predict(flips, ids, uv8, lm8, wide):
    rows = QROWS * len(flips)

    def kernel(*refs):
        predict_kernel(flips, *refs)

    return pl.pallas_call(
        kernel,
        out_shape=tuple(jax.ShapeDtypeStruct((DIR_DEV, QROWS, COLS), BF16) for _ in flips),
        in_specs=[smem(), vmem(), vmem(), vmem()],
        out_specs=tuple(vmem() for _ in flips),
        scratch_shapes=[
            pltpu.VMEM((rows, 2 * CHUNK), BF16),
            pltpu.VMEM((rows, 2 * CHUNK), BF16),
            pltpu.VMEM((rows, WIDE), F32),
        ],
        cost_estimate=pl.CostEstimate(
            flops=2 * rows * 2 * POOL * 2 * WIDE,
            transcendentals=0,
            bytes_accessed=2 * (2 * POOL * WIDE + rows * WIDE),
        ),
        compiler_params=params(16),
        name="predict",
    )(ids, uv8, lm8, wide)


def per_block_sum(value):
    return jnp.sum(value.reshape(QROWS // GB, GB, COLS), axis=1)


def lane_shift(value, by):
    return pltpu.roll(value, (-by) % COLS, 1)


def sweeps(pull):
    lane = lax.broadcasted_iota(jnp.int32, pull.shape, 1)
    first, last = lane < 2, lane >= COLS - 2
    band = {0: jnp.ones_like(pull)}
    free = pull
    for _ in range(ITERS - 1):
        lower = {d: lane_shift(value, -2) for d, value in band.items()}
        upper = {d: lane_shift(value, 2) for d, value in band.items()}
        new = {}
        for d, value in band.items():
            for at, inside, kept in ((d - 2, lower[d], first), (d + 2, upper[d], last)):
                moved = jnp.where(kept, 0.0, inside)
                new[at] = new[at] + moved if at in new else moved
                stays = jnp.where(kept, value, 0.0)
                new[d] = new[d] + stays if d in new else stays
        band = {d: (0.5 * pull) * value for d, value in new.items()}
        band[0] = band[0] + 1.0
        around = jnp.where(first, free, lane_shift(free, -2)) + jnp.where(last, free, lane_shift(free, 2))
        free = pull * (0.5 * around)
    return band, free


SHIFTS = tuple(range(-2 * (ITERS - 1), 2 * ITERS, 2))


def peel_kernel(ids_ref, vis_ref, ridge_ref, m0_ref, m1_ref, m2_ref, m3_ref, out_ref, *rest):
    part_refs, (model_ref, inv_ref, band_ref, part_ref) = rest[:N_DIR], rest[N_DIR:]
    me = ids_ref[0]
    ridge = ridge_ref[...]
    blocks = QROWS // GB
    for x, ref in enumerate((m0_ref, m1_ref, m2_ref, m3_ref)):
        owner = me ^ x
        for p in range(DIR_DEV):
            model = ref[p].astype(F32)
            model_ref[owner * DIR_DEV + p] = model
            inv_ref[pl.ds((owner * DIR_DEV + p) * 8, blocks), :] = per_block_sum(model * model)
    inv = 1.0 / (inv_ref[...] + ridge)
    band, free = sweeps(ridge * inv)
    for n, d in enumerate(SHIFTS):
        band_ref[n] = band[d] * lane_shift(inv, d)
    band_ref[len(SHIFTS)] = free
    remains = vis_ref[pl.ds(pl.multiple_of(me * QROWS, QROWS), QROWS), :].astype(F32)
    for j in range(N_DIR * DIR_DEV):
        model = model_ref[j]
        cross = per_block_sum(remains * model)
        gain = band_ref[len(SHIFTS), j * 8 : j * 8 + blocks, :]
        for n, d in enumerate(SHIFTS):
            gain = gain + band_ref[n, j * 8 : j * 8 + blocks, :] * (lane_shift(cross, d) if d else cross)
        spread = jnp.concatenate(
            [jnp.broadcast_to(gain[b : b + 1], (GB, COLS)) for b in range(blocks)], axis=0
        )
        remains = remains - spread * model
        if (j + 1) % DIR_DEV == 0:
            remains = remains.astype(BF16).astype(F32)
    out_ref[...] = remains.astype(BF16)
    part_ref[...] = remains.reshape(QBLOCKS, 2, PART, COLS)
    for x in range(N_DIR):
        part_refs[x][...] = part_ref[:, (me ^ x) & 1].astype(BF16)


def peel(ids, visibilities, ridge_weight, models):
    out = pl.pallas_call(
        peel_kernel,
        out_shape=(jax.ShapeDtypeStruct((QROWS, COLS), BF16),)
        + (jax.ShapeDtypeStruct((QBLOCKS, PART, COLS), BF16),) * N_DIR,
        in_specs=[smem()] + [vmem()] * 6,
        out_specs=(vmem(),) * (1 + N_DIR),
        scratch_shapes=[
            pltpu.VMEM((N_DIR * DIR_DEV, QROWS, COLS), F32),
            pltpu.VMEM((N_DIR * DIR_DEV * 8, COLS), F32),
            pltpu.VMEM((len(SHIFTS) + 1, N_DIR * DIR_DEV * 8, COLS), F32),
            pltpu.VMEM((QBLOCKS, 2, PART, COLS), F32),
        ],
        compiler_params=params(16),
        name="peel",
    )(ids, visibilities, ridge_weight.reshape(1, COLS), *models)
    return out[0], out[1:]


def label_kernel(ids_ref, tile_id_ref, tile_ref, uv_ref, out_ref, slot_ref, seen_ref):
    half = ids_ref[1]
    offset = ids_ref[2]
    tiles = tile_ref[...].astype(F32)
    block_of_lane = lax.broadcasted_iota(jnp.int32, (NB, ROWS_DEV), 1) // BB
    expand = (block_of_lane == lax.broadcasted_iota(jnp.int32, (NB, ROWS_DEV), 0)).astype(F32)
    tile_of_lane = jnp.sum(expand * tiles, axis=0, keepdims=True)
    sub = lax.broadcasted_iota(jnp.int32, (NB, NB), 0)
    col = lax.broadcasted_iota(jnp.int32, (NB, NB), 1)
    tile_row = jnp.sum(jnp.where(sub == col, tiles, 0.0), axis=0, keepdims=True)
    slot = jnp.sum(jnp.where((tiles == tile_row) & (col < sub), 1.0, 0.0), axis=1, keepdims=True)
    slot_of_row = lax.dot_general(
        expand.astype(BF16),
        jnp.broadcast_to(slot, (NB, COLS)).astype(BF16),
        (((0,), (0,)), ((), ())),
        preferred_element_type=F32,
    )
    within = lax.broadcasted_iota(jnp.int32, (ROWS_DEV, COLS), 0) % BB - half * PART
    lane = lax.broadcasted_iota(jnp.int32, (ROWS_DEV, COLS), 1)
    goal = slot_of_row.astype(jnp.int32) * PART + within + offset
    spot = jnp.where((goal == lane) & (within >= 0) & (within < PART), 1.0, 0.0).astype(BF16)
    row = lax.broadcasted_iota(jnp.int32, (N_TB * 8, ROWS_DEV), 0)
    u = uv_ref[0:1, :].astype(F32)
    v = uv_ref[1:2, :].astype(F32)
    value = jnp.where(row % 8 == 0, u, jnp.where(row % 8 == 1, v, 0.0))
    value = jnp.where((row // 8).astype(F32) == tile_of_lane, value, 0.0).astype(BF16)
    out = jnp.dot(value, spot, preferred_element_type=F32)
    out_ref[:, : SLOTS * PART, :] = jnp.zeros((N_TB, SLOTS * PART, COLS), BF16)
    out_ref[:, SLOTS * PART :, :] = out.reshape(N_TB, 8, COLS).astype(BF16)
    for t in range(N_TB):
        seen_ref[t] = 0
    for b in range(NB):
        tile = tile_id_ref[b]
        slot_ref[b] = seen_ref[tile]
        seen_ref[tile] = 1


def label(ids, tile_ids, block_tile, uv_coords):
    return pl.pallas_call(
        label_kernel,
        out_shape=(
            jax.ShapeDtypeStruct((N_TB, SEND_ROWS, COLS), BF16),
            jax.ShapeDtypeStruct((NB,), jnp.int32),
        ),
        in_specs=[smem(), smem(), vmem(), vmem()],
        out_specs=(vmem(), smem()),
        scratch_shapes=[pltpu.SMEM((N_TB,), jnp.int32)],
        compiler_params=params(16),
        name="label",
    )(ids, tile_ids, block_tile, uv_coords)


def pack_kernel(ids_ref, tile_ref, slot_ref, r0_ref, r1_ref, r2_ref, r3_ref, base_ref, out_ref, stage_ref):
    me = ids_ref[0]
    out_ref[...] = base_ref[...]
    for x, ref in enumerate((r0_ref, r1_ref, r2_ref, r3_ref)):
        stage_ref[pl.ds((me ^ x) * QBLOCKS, QBLOCKS)] = ref[...]
    for b in range(NB):
        first = pl.multiple_of(slot_ref[b] * PART, PART)
        out_ref[tile_ref[b], pl.ds(first, PART), :] = stage_ref[b]


def pack(ids, tile_ids, slots, rows, base):
    return pl.pallas_call(
        pack_kernel,
        out_shape=jax.ShapeDtypeStruct((N_TB, SEND_ROWS, COLS), BF16),
        in_specs=[smem(), smem(), smem()] + [vmem()] * 5,
        out_specs=vmem(),
        scratch_shapes=[pltpu.VMEM((NB, PART, COLS), BF16)],
        compiler_params=params(16),
        name="pack",
    )(ids, tile_ids, slots, *rows, base)


def join_kernel(ids_ref, r0_ref, r1_ref, r2_ref, r3_ref, out_ref):
    me = ids_ref[0]
    for x, ref in enumerate((r0_ref, r1_ref, r2_ref, r3_ref)):
        out_ref[pl.ds(pl.multiple_of((me ^ x) * QROWS, QROWS), QROWS), :] = ref[...]


def join(ids, rows):
    return pl.pallas_call(
        join_kernel,
        out_shape=jax.ShapeDtypeStruct((ROWS_DEV, COLS), BF16),
        in_specs=[smem()] + [vmem()] * 4,
        out_specs=vmem(),
        compiler_params=params(16),
        name="join",
    )(ids, *rows)


def grid_kernel(ids_ref, got_ref, keep_ref, give_ref, tab_ref, acc_ref):
    chip = ids_ref[0] // 2
    half = ids_ref[1]
    tiles = N_TB * SLOTS * PART // 128
    groups = N_TB // tiles
    coords = got_ref[:, SLOTS * PART :, :].astype(F32).reshape(tiles, groups, 8, COLS)
    coords = jnp.sum(coords, axis=1)
    y_pixel = (lax.broadcasted_iota(jnp.int32, (GRID, 1), 0) - GRID // 2).astype(F32)
    order = lax.broadcasted_iota(jnp.int32, (16, 1), 0)
    x_pixel = (16 * chip + 8 * ((order // 8) ^ half) + order % 8 - GRID // 2).astype(F32)
    scale = 1.0 / (2.0 * GRID)
    step = 256
    per_step = step // 128

    def product(n):
        sources = step // (SLOTS * PART)
        rows = got_ref[n * sources : (n + 1) * sources, : SLOTS * PART, :].reshape(step, COLS)
        return jnp.dot(tab_ref[n], rows, preferred_element_type=F32)

    for tile in range(tiles):
        u = coords[tile, 0:1, :] * scale
        v = coords[tile, 1:2, :] * scale
        cx, sx = cos_sin_turns(x_pixel * u)
        cy, sy = cos_sin_turns(y_pixel * v)
        n, lanes = tile // per_step, slice(tile % per_step * 128, (tile % per_step + 1) * 128)
        for x in range(16):
            a, b = cx[x : x + 1], sx[x : x + 1]
            tab_ref[n, x * GRID : (x + 1) * GRID, lanes] = (a * cy - b * sy).astype(BF16)
            tab_ref[n, 512 + x * GRID : 512 + (x + 1) * GRID, lanes] = (b * cy + a * sy).astype(BF16)
        if tile % per_step == per_step - 1:
            if n == 0:
                acc_ref[...] = product(n)
            else:
                acc_ref[...] += product(n)
    total = acc_ref[...] * float(ROWS_DEV) ** (-0.5)
    for part in range(2):
        keep_ref[part] = total[part * 512 : part * 512 + 256]
        give_ref[part] = total[part * 512 + 256 : part * 512 + 512]


def grid_rows(ids, got):
    return pl.pallas_call(
        grid_kernel,
        out_shape=(
            jax.ShapeDtypeStruct((2, PIX // N_DIR, COLS), F32),
            jax.ShapeDtypeStruct((2, PIX // N_DIR, COLS), F32),
        ),
        in_specs=[smem(), vmem()],
        out_specs=(vmem(), vmem()),
        scratch_shapes=[
            pltpu.VMEM((N_TB * SLOTS * PART // 256, 1024, 256), BF16),
            pltpu.VMEM((1024, COLS), F32),
        ],
        compiler_params=params(24),
        name="grid",
    )(ids, got)


def after(value, done):
    return lax.optimization_barrier((value, done))[0]


def swap(value, flip):
    return lax.ppermute(value, "dir", [(i, i ^ flip) for i in range(N_DIR)])


def local(
    visibilities, uv_coords, comp_lm, spectra, ridge_weight, assignment, peel_order, block_tile
):
    me = lax.axis_index("dir")
    station = lax.axis_index("tb")
    ids = jnp.stack([me, me % 2, (station % 4) * (SLOTS * PART)]).astype(jnp.int32)
    lm8, uv8, wide = prepare(peel_order, assignment, comp_lm, uv_coords, spectra)
    far_a, far_b = predict((2, 3), ids, uv8, lm8, wide)
    got_a, got_b = swap(far_a, 2), swap(far_b, 3)
    near, own = predict((1, 0), ids, uv8, lm8, wide)
    got_near = swap(near, 1)
    tile_ids = block_tile[:, 0]
    base, slots = label(after(ids, own), tile_ids, block_tile, uv_coords)
    rows, parts = peel(after(ids, slots), visibilities, ridge_weight, (own, got_near, got_a, got_b))
    shared = [parts[0]] + [swap(parts[x], x) for x in range(1, N_DIR)]
    send = pack(ids, tile_ids, slots, shared, base)
    got = lax.all_to_all(send, "tb", split_axis=0, concat_axis=0, tiled=True)
    late = after(rows, send)
    residual = join(ids, [late] + [swap(late, x) for x in range(1, N_DIR)])
    keep, give = grid_rows(after(ids, residual), got)
    return residual, (keep + swap(give, 1))[None]


def solution(mesh):
    return jax.shard_map(
        local,
        mesh=mesh,
        in_specs=(
            P("tb", None),
            P(None, "tb"),
            P(None, "dir"),
            P(None, "dir", None),
            P(),
            P("dir"),
            P("dir"),
            P("tb", None),
        ),
        out_specs=(P("tb", None), P("tb", None, "dir", None)),
        check_vma=False,
    )
```

```python
import jax
import jax.numpy as jnp
from jax import lax
from jax.experimental import pallas as pl
from jax.experimental.pallas import tpu as pltpu
from jax.sharding import PartitionSpec as P

NCOMP = 1024
GRID = 32
DIR_DEV = 3
ITERS = 4
BB = 32
GB = 128
ROWS_DEV = 1024
PIX = 1024
COLS = 128
N_DIR = 4
N_TB = 64
NB = 32
SLOTS = 2
QROWS = ROWS_DEV // N_DIR
PART = BB // 2
POOL = DIR_DEV * NCOMP
WIDE = DIR_DEV * COLS
CHUNK = 256
NCHUNK = POOL // CHUNK
PIECES = 4
SEND_ROWS = SLOTS * PART + 8
QBLOCKS = QROWS // BB

F32 = jnp.float32
BF16 = jnp.bfloat16

SIN_C = (2.6417407853784525, -1.0859537956447276, 0.1306204657138272)
COS_C = (1.681792784129167, -2.074822793580374, 0.42650038149094444, -0.03432262097868313)
ROOT2 = 1.4142135623730951


def own_place():
    me = lax.axis_index("dir")
    return me, me & 1, (lax.axis_index("tb") & 3) * (SLOTS * PART)


def vmem():
    return pl.BlockSpec(memory_space=pltpu.VMEM)


def smem():
    return pl.BlockSpec(memory_space=pltpu.SMEM)


def params(mib):
    return pltpu.CompilerParams(vmem_limit_bytes=mib << 20)


def cos_sin_turns(turns):
    r = turns - jnp.round(turns)
    z = r * r
    s = ((SIN_C[2] * z + SIN_C[1]) * z + SIN_C[0]) * r
    c = ((COS_C[3] * z + COS_C[2]) * z + COS_C[1]) * z + COS_C[0]
    s1 = s * c
    c1 = ROOT2 - s * s
    return 1.0 - s1 * s1, s1 * c1


def three_parts(value):
    high = value.astype(BF16)
    left = value - high.astype(F32)
    mid = left.astype(BF16)
    low = (left - mid.astype(F32)).astype(BF16)
    return high, mid, low


def prepare_kernel(
    order_hbm, assign_hbm, lm_hbm, uv_hbm, spec_hbm, lm8_ref, uv8_ref, wide_ref,
    order_ref, assign_ref, lm_ref, uv_ref, spec_ref, pos_ref, sems
):
    pairs = [(assign_hbm, assign_ref), (order_hbm, order_ref), (lm_hbm, lm_ref), (uv_hbm, uv_ref)]
    for n in range(PIECES):
        piece = slice(n * (POOL // PIECES), (n + 1) * (POOL // PIECES))
        pairs.append((spec_hbm.at[:, piece, :], spec_ref.at[:, piece, :]))
    copies = [pltpu.make_async_copy(src, dst, sems.at[n]) for n, (src, dst) in enumerate(pairs)]
    for copy in copies:
        copy.start()
    for copy in copies[:4]:
        copy.wait()
    lh, lmid, ll = three_parts(lm_ref[...])
    zero = jnp.zeros((2, POOL), BF16)
    lm8_ref[...] = jnp.concatenate(
        [lh[0:1], lmid[0:1], ll[0:1], lh[1:2], lmid[1:2], ll[1:2], zero], axis=0
    )
    for q in range(N_DIR):
        u = uv_ref[0:1, q * QROWS : (q + 1) * QROWS]
        v = uv_ref[1:2, q * QROWS : (q + 1) * QROWS]
        uv8_ref[q] = jnp.concatenate([u, u, u, v, v, v, jnp.zeros((2, QROWS), BF16)], axis=0)
    assign = assign_ref[...]
    low = assign & 127
    high = assign >> 7
    segment = lax.broadcasted_iota(jnp.int32, (1, POOL), 1) // NCOMP
    place = jnp.zeros((1, POOL), F32)
    for p in range(DIR_DEV):
        place = jnp.where(segment == order_ref[p], float(p), place)
    low_hot = (lax.broadcasted_iota(jnp.int32, (128, POOL), 0) == low).astype(F32).astype(BF16)
    high_hot = jnp.where(lax.broadcasted_iota(jnp.int32, (32, POOL), 0) == high, place, 0.0).astype(BF16)
    pos = lax.dot_general(low_hot, high_hot, (((1,), (1,)), ((), ())), preferred_element_type=F32)
    column = lax.broadcasted_iota(jnp.int32, (32, POOL), 1) // 128
    pick = (column == lax.broadcasted_iota(jnp.int32, (32, POOL), 0)).astype(F32).astype(BF16)
    pos_ref[...] = jnp.dot(pos.astype(BF16), pick, preferred_element_type=F32)
    for column in range(POOL // 128):
        if column % (POOL // 128 // PIECES) == 0:
            copies[4 + column // (POOL // 128 // PIECES)].wait()
        place_here = pos_ref[:, column * 128 : (column + 1) * 128]
        for p in range(DIR_DEV):
            mask = jnp.where(place_here == float(p), 1.0, 0.0).astype(BF16)
            for part in range(2):
                first = part * CHUNK + (column % 2) * 128
                wide_ref[column // 2, first : first + 128, p * COLS : (p + 1) * COLS] = (
                    spec_ref[part, column * 128 : (column + 1) * 128, :] * mask
                )


def prepare(peel_order, assignment, comp_lm, uv_coords, spectra):
    return pl.pallas_call(
        prepare_kernel,
        out_shape=(
            jax.ShapeDtypeStruct((8, POOL), BF16),
            jax.ShapeDtypeStruct((N_DIR, 8, QROWS), BF16),
            jax.ShapeDtypeStruct((NCHUNK, 2 * CHUNK, WIDE), BF16),
        ),
        in_specs=[pl.BlockSpec(memory_space=pltpu.MemorySpace.HBM)] * 5,
        out_specs=(vmem(), vmem(), vmem()),
        scratch_shapes=[
            pltpu.SMEM((DIR_DEV,), jnp.int32),
            pltpu.VMEM((1, POOL), jnp.int32),
            pltpu.VMEM((2, POOL), F32),
            pltpu.VMEM((2, ROWS_DEV), BF16),
            pltpu.VMEM((2, POOL, COLS), BF16),
            pltpu.VMEM((128, POOL), F32),
            pltpu.SemaphoreType.DMA((4 + PIECES,)),
        ],
        compiler_params=params(16),
        name="prepare",
    )(*(
        pltpu.with_memory_space_constraint(value, pltpu.MemorySpace.HBM)
        for value in (peel_order, assignment.reshape(1, POOL), comp_lm, uv_coords, spectra)
    ))


def predict_kernel(flips, uv8_ref, lm8_ref, wide_ref, *rest):
    out_refs = rest[: len(flips)]
    tab_a, tab_b, acc_ref = rest[len(flips) :]
    me = own_place()[0]
    uv_rows = jnp.concatenate([uv8_ref[me ^ x].astype(F32).T for x in flips], axis=0).astype(BF16)

    def table(j, tab_ref):
        lm = lm8_ref[:, j * CHUNK : (j + 1) * CHUNK]
        turns = jnp.dot(uv_rows, lm, preferred_element_type=F32)
        cos, sin = cos_sin_turns(turns)
        tab_ref[:, :CHUNK] = cos.astype(BF16)
        tab_ref[:, CHUNK:] = sin.astype(BF16)

    tabs = (tab_a, tab_b)
    table(0, tab_a)
    for j in range(NCHUNK):
        if j + 1 < NCHUNK:
            table(j + 1, tabs[(j + 1) % 2])
        part = jnp.dot(tabs[j % 2][...], wide_ref[j], preferred_element_type=F32)
        if j == 0:
            acc_ref[...] = part
        else:
            acc_ref[...] += part
    for n in range(len(flips)):
        for p in range(DIR_DEV):
            out_refs[n][p] = acc_ref[n * QROWS : (n + 1) * QROWS, p * COLS : (p + 1) * COLS].astype(BF16)


def predict(flips, uv8, lm8, wide):
    rows = QROWS * len(flips)

    def kernel(*refs):
        predict_kernel(flips, *refs)

    return pl.pallas_call(
        kernel,
        out_shape=tuple(jax.ShapeDtypeStruct((DIR_DEV, QROWS, COLS), BF16) for _ in flips),
        in_specs=[vmem(), vmem(), vmem()],
        out_specs=tuple(vmem() for _ in flips),
        scratch_shapes=[
            pltpu.VMEM((rows, 2 * CHUNK), BF16),
            pltpu.VMEM((rows, 2 * CHUNK), BF16),
            pltpu.VMEM((rows, WIDE), F32),
        ],
        cost_estimate=pl.CostEstimate(
            flops=2 * rows * 2 * POOL * 2 * WIDE,
            transcendentals=0,
            bytes_accessed=2 * (2 * POOL * WIDE + rows * WIDE),
        ),
        compiler_params=params(16),
        name="predict",
    )(uv8, lm8, wide)


def per_block_sum(value):
    return jnp.sum(value.reshape(QROWS // GB, GB, COLS), axis=1)


def lane_shift(value, by):
    return pltpu.roll(value, (-by) % COLS, 1)


def sweeps(pull):
    lane = lax.broadcasted_iota(jnp.int32, pull.shape, 1)
    first, last = lane < 2, lane >= COLS - 2
    band = {0: jnp.ones_like(pull)}
    free = pull
    for _ in range(ITERS - 1):
        lower = {d: lane_shift(value, -2) for d, value in band.items()}
        upper = {d: lane_shift(value, 2) for d, value in band.items()}
        new = {}
        for d, value in band.items():
            for at, inside, kept in ((d - 2, lower[d], first), (d + 2, upper[d], last)):
                moved = jnp.where(kept, 0.0, inside)
                new[at] = new[at] + moved if at in new else moved
                stays = jnp.where(kept, value, 0.0)
                new[d] = new[d] + stays if d in new else stays
        band = {d: (0.5 * pull) * value for d, value in new.items()}
        band[0] = band[0] + 1.0
        around = jnp.where(first, free, lane_shift(free, -2)) + jnp.where(last, free, lane_shift(free, 2))
        free = pull * (0.5 * around)
    return band, free


SHIFTS = tuple(range(-2 * (ITERS - 1), 2 * ITERS, 2))


def peel_kernel(vis_ref, ridge_ref, m0_ref, m1_ref, m2_ref, m3_ref, out_ref, *rest):
    part_refs, (model_ref, inv_ref, band_ref, part_ref) = rest[:N_DIR], rest[N_DIR:]
    me = own_place()[0]
    ridge = ridge_ref[...]
    blocks = QROWS // GB
    for x, ref in enumerate((m0_ref, m1_ref, m2_ref, m3_ref)):
        owner = me ^ x
        for p in range(DIR_DEV):
            model = ref[p].astype(F32)
            model_ref[owner * DIR_DEV + p] = model
            inv_ref[pl.ds((owner * DIR_DEV + p) * 8, blocks), :] = per_block_sum(model * model)
    inv = 1.0 / (inv_ref[...] + ridge)
    band, free = sweeps(ridge * inv)
    for n, d in enumerate(SHIFTS):
        band_ref[n] = band[d] * lane_shift(inv, d)
    band_ref[len(SHIFTS)] = free
    remains = vis_ref[pl.ds(pl.multiple_of(me * QROWS, QROWS), QROWS), :].astype(F32)
    for j in range(N_DIR * DIR_DEV):
        model = model_ref[j]
        cross = per_block_sum(remains * model)
        gain = band_ref[len(SHIFTS), j * 8 : j * 8 + blocks, :]
        for n, d in enumerate(SHIFTS):
            gain = gain + band_ref[n, j * 8 : j * 8 + blocks, :] * (lane_shift(cross, d) if d else cross)
        spread = jnp.concatenate(
            [jnp.broadcast_to(gain[b : b + 1], (GB, COLS)) for b in range(blocks)], axis=0
        )
        remains = remains - spread * model
        if (j + 1) % DIR_DEV == 0:
            remains = remains.astype(BF16).astype(F32)
    out_ref[...] = remains.astype(BF16)
    part_ref[...] = remains.reshape(QBLOCKS, 2, PART, COLS)
    for x in range(N_DIR):
        part_refs[x][...] = part_ref[:, (me ^ x) & 1].astype(BF16)


def peel(visibilities, ridge_weight, models):
    out = pl.pallas_call(
        peel_kernel,
        out_shape=(jax.ShapeDtypeStruct((QROWS, COLS), BF16),)
        + (jax.ShapeDtypeStruct((QBLOCKS, PART, COLS), BF16),) * N_DIR,
        in_specs=[vmem()] * 6,
        out_specs=(vmem(),) * (1 + N_DIR),
        scratch_shapes=[
            pltpu.VMEM((N_DIR * DIR_DEV, QROWS, COLS), F32),
            pltpu.VMEM((N_DIR * DIR_DEV * 8, COLS), F32),
            pltpu.VMEM((len(SHIFTS) + 1, N_DIR * DIR_DEV * 8, COLS), F32),
            pltpu.VMEM((QBLOCKS, 2, PART, COLS), F32),
        ],
        compiler_params=params(16),
        name="peel",
    )(visibilities, ridge_weight.reshape(1, COLS), *models)
    return out[0], out[1:]


def label_kernel(tile_id_ref, tile_ref, uv_ref, out_ref, slot_ref, seen_ref):
    half = own_place()[1]
    offset = own_place()[2]
    tiles = tile_ref[...].astype(F32)
    block_of_lane = lax.broadcasted_iota(jnp.int32, (NB, ROWS_DEV), 1) // BB
    expand = (block_of_lane == lax.broadcasted_iota(jnp.int32, (NB, ROWS_DEV), 0)).astype(F32)
    tile_of_lane = jnp.sum(expand * tiles, axis=0, keepdims=True)
    sub = lax.broadcasted_iota(jnp.int32, (NB, NB), 0)
    col = lax.broadcasted_iota(jnp.int32, (NB, NB), 1)
    tile_row = jnp.sum(jnp.where(sub == col, tiles, 0.0), axis=0, keepdims=True)
    slot = jnp.sum(jnp.where((tiles == tile_row) & (col < sub), 1.0, 0.0), axis=1, keepdims=True)
    slot_of_row = lax.dot_general(
        expand.astype(BF16),
        jnp.broadcast_to(slot, (NB, COLS)).astype(BF16),
        (((0,), (0,)), ((), ())),
        preferred_element_type=F32,
    )
    within = lax.broadcasted_iota(jnp.int32, (ROWS_DEV, COLS), 0) % BB - half * PART
    lane = lax.broadcasted_iota(jnp.int32, (ROWS_DEV, COLS), 1)
    goal = slot_of_row.astype(jnp.int32) * PART + within + offset
    spot = jnp.where((goal == lane) & (within >= 0) & (within < PART), 1.0, 0.0).astype(BF16)
    row = lax.broadcasted_iota(jnp.int32, (N_TB * 8, ROWS_DEV), 0)
    u = uv_ref[0:1, :].astype(F32)
    v = uv_ref[1:2, :].astype(F32)
    value = jnp.where(row % 8 == 0, u, jnp.where(row % 8 == 1, v, 0.0))
    value = jnp.where((row // 8).astype(F32) == tile_of_lane, value, 0.0).astype(BF16)
    out = jnp.dot(value, spot, preferred_element_type=F32)
    out_ref[:, : SLOTS * PART, :] = jnp.zeros((N_TB, SLOTS * PART, COLS), BF16)
    out_ref[:, SLOTS * PART :, :] = out.reshape(N_TB, 8, COLS).astype(BF16)
    for t in range(N_TB):
        seen_ref[t] = 0
    for b in range(NB):
        tile = tile_id_ref[b]
        slot_ref[b] = seen_ref[tile]
        seen_ref[tile] = 1


def label(tile_ids, block_tile, uv_coords):
    return pl.pallas_call(
        label_kernel,
        out_shape=(
            jax.ShapeDtypeStruct((N_TB, SEND_ROWS, COLS), BF16),
            jax.ShapeDtypeStruct((NB,), jnp.int32),
        ),
        in_specs=[smem(), vmem(), vmem()],
        out_specs=(vmem(), smem()),
        scratch_shapes=[pltpu.SMEM((N_TB,), jnp.int32)],
        compiler_params=params(16),
        name="label",
    )(tile_ids, block_tile, uv_coords)


def pack_kernel(tile_ref, slot_ref, r0_ref, r1_ref, r2_ref, r3_ref, base_ref, out_ref, stage_ref):
    me = own_place()[0]
    out_ref[...] = base_ref[...]
    for x, ref in enumerate((r0_ref, r1_ref, r2_ref, r3_ref)):
        stage_ref[pl.ds((me ^ x) * QBLOCKS, QBLOCKS)] = ref[...]
    for b in range(NB):
        first = pl.multiple_of(slot_ref[b] * PART, PART)
        out_ref[tile_ref[b], pl.ds(first, PART), :] = stage_ref[b]


def pack(tile_ids, slots, rows, base):
    return pl.pallas_call(
        pack_kernel,
        out_shape=jax.ShapeDtypeStruct((N_TB, SEND_ROWS, COLS), BF16),
        in_specs=[smem(), smem()] + [vmem()] * 5,
        out_specs=vmem(),
        scratch_shapes=[pltpu.VMEM((NB, PART, COLS), BF16)],
        compiler_params=params(16),
        name="pack",
    )(tile_ids, slots, *rows, base)


def join_kernel(r0_ref, r1_ref, r2_ref, r3_ref, out_ref):
    me = own_place()[0]
    for x, ref in enumerate((r0_ref, r1_ref, r2_ref, r3_ref)):
        out_ref[pl.ds(pl.multiple_of((me ^ x) * QROWS, QROWS), QROWS), :] = ref[...]


def join(rows):
    return pl.pallas_call(
        join_kernel,
        out_shape=jax.ShapeDtypeStruct((ROWS_DEV, COLS), BF16),
        in_specs=[vmem()] * 4,
        out_specs=vmem(),
        compiler_params=params(16),
        name="join",
    )(*rows)


def grid_kernel(got_ref, keep_ref, give_ref, tab_ref, acc_ref):
    chip = own_place()[0] // 2
    half = own_place()[1]
    tiles = N_TB * SLOTS * PART // 128
    groups = N_TB // tiles
    coords = got_ref[:, SLOTS * PART :, :].astype(F32).reshape(tiles, groups, 8, COLS)
    coords = jnp.sum(coords, axis=1)
    y_pixel = (lax.broadcasted_iota(jnp.int32, (GRID, 1), 0) - GRID // 2).astype(F32)
    order = lax.broadcasted_iota(jnp.int32, (16, 1), 0)
    x_pixel = (16 * chip + 8 * ((order // 8) ^ half) + order % 8 - GRID // 2).astype(F32)
    scale = 1.0 / (2.0 * GRID)
    step = 256
    per_step = step // 128

    def product(n):
        sources = step // (SLOTS * PART)
        rows = got_ref[n * sources : (n + 1) * sources, : SLOTS * PART, :].reshape(step, COLS)
        return jnp.dot(tab_ref[n], rows, preferred_element_type=F32)

    for tile in range(tiles):
        u = coords[tile, 0:1, :] * scale
        v = coords[tile, 1:2, :] * scale
        cx, sx = cos_sin_turns(x_pixel * u)
        cy, sy = cos_sin_turns(y_pixel * v)
        n, lanes = tile // per_step, slice(tile % per_step * 128, (tile % per_step + 1) * 128)
        for x in range(16):
            a, b = cx[x : x + 1], sx[x : x + 1]
            tab_ref[n, x * GRID : (x + 1) * GRID, lanes] = (a * cy - b * sy).astype(BF16)
            tab_ref[n, 512 + x * GRID : 512 + (x + 1) * GRID, lanes] = (b * cy + a * sy).astype(BF16)
        if tile % per_step == per_step - 1:
            if n == 0:
                acc_ref[...] = product(n)
            else:
                acc_ref[...] += product(n)
    total = acc_ref[...] * float(ROWS_DEV) ** (-0.5)
    for part in range(2):
        keep_ref[part] = total[part * 512 : part * 512 + 256]
        give_ref[part] = total[part * 512 + 256 : part * 512 + 512]


def grid_rows(got):
    return pl.pallas_call(
        grid_kernel,
        out_shape=(
            jax.ShapeDtypeStruct((2, PIX // N_DIR, COLS), F32),
            jax.ShapeDtypeStruct((2, PIX // N_DIR, COLS), F32),
        ),
        in_specs=[vmem()],
        out_specs=(vmem(), vmem()),
        scratch_shapes=[
            pltpu.VMEM((N_TB * SLOTS * PART // 256, 1024, 256), BF16),
            pltpu.VMEM((1024, COLS), F32),
        ],
        compiler_params=params(24),
        name="grid",
    )(got)


def after(value, done):
    return lax.optimization_barrier((value, done))[0]


def swap(value, flip):
    return lax.ppermute(value, "dir", [(i, i ^ flip) for i in range(N_DIR)])


def local(
    visibilities, uv_coords, comp_lm, spectra, ridge_weight, assignment, peel_order, block_tile
):
    lm8, uv8, wide = prepare(peel_order, assignment, comp_lm, uv_coords, spectra)
    far_a, far_b = predict((2, 3), uv8, lm8, wide)
    got_a, got_b = swap(far_a, 2), swap(far_b, 3)
    near, own = predict((1, 0), uv8, lm8, wide)
    got_near = swap(near, 1)
    tile_ids = block_tile[:, 0]
    base, slots = label(after(tile_ids, own), block_tile, uv_coords)
    rows, parts = peel(after(visibilities, slots), ridge_weight, (own, got_near, got_a, got_b))
    shared = [parts[0]] + [swap(parts[x], x) for x in range(1, N_DIR)]
    send = pack(tile_ids, slots, shared, base)
    got = lax.all_to_all(send, "tb", split_axis=0, concat_axis=0, tiled=True)
    late = after(rows, send)
    residual = join([late] + [swap(late, x) for x in range(1, N_DIR)])
    keep, give = grid_rows(after(got, residual))
    return residual, (keep + swap(give, 1))[None]


def solution(mesh):
    return jax.shard_map(
        local,
        mesh=mesh,
        in_specs=(
            P("tb", None),
            P(None, "tb"),
            P(None, "dir"),
            P(None, "dir", None),
            P(),
            P("dir"),
            P("dir"),
            P("tb", None),
        ),
        out_specs=(P("tb", None), P("tb", None, "dir", None)),
        check_vma=False,
    )
```

```python
import jax
import jax.numpy as jnp
from jax import lax
from jax.experimental import pallas as pl
from jax.experimental.pallas import tpu as pltpu
from jax.sharding import PartitionSpec as P

NCOMP = 1024
GRID = 32
DIR_DEV = 3
ITERS = 4
BB = 32
GB = 128
ROWS_DEV = 1024
PIX = 1024
COLS = 128
N_DIR = 4
N_TB = 64
NB = 32
SLOTS = 2
QROWS = ROWS_DEV // N_DIR
PART = BB // 2
POOL = DIR_DEV * NCOMP
WIDE = DIR_DEV * COLS
CHUNK = 256
NCHUNK = POOL // CHUNK
PIECES = 4
SEND_ROWS = SLOTS * PART + 8
QBLOCKS = QROWS // BB

F32 = jnp.float32
BF16 = jnp.bfloat16

SIN_C = (2.6417407853784525, -1.0859537956447276, 0.1306204657138272)
COS_C = (1.681792784129167, -2.074822793580374, 0.42650038149094444, -0.03432262097868313)
ROOT2 = 1.4142135623730951


def own_place():
    me = lax.axis_index("dir")
    return me, me & 1, (lax.axis_index("tb") & 3) * (SLOTS * PART)


def vmem():
    return pl.BlockSpec(memory_space=pltpu.VMEM)


def smem():
    return pl.BlockSpec(memory_space=pltpu.SMEM)


def params(mib):
    return pltpu.CompilerParams(vmem_limit_bytes=mib << 20)


def cos_sin_turns(turns):
    r = turns - jnp.round(turns)
    z = r * r
    s = ((SIN_C[2] * z + SIN_C[1]) * z + SIN_C[0]) * r
    c = ((COS_C[3] * z + COS_C[2]) * z + COS_C[1]) * z + COS_C[0]
    s1 = s * c
    c1 = ROOT2 - s * s
    return 1.0 - s1 * s1, s1 * c1


def three_parts(value):
    high = value.astype(BF16)
    left = value - high.astype(F32)
    mid = left.astype(BF16)
    low = (left - mid.astype(F32)).astype(BF16)
    return high, mid, low


def prepare_kernel(
    order_hbm, assign_hbm, lm_hbm, uv_hbm, spec_hbm, lm8_ref, uv8_ref, wide_ref,
    order_ref, assign_ref, lm_ref, uv_ref, spec_ref, pos_ref, sems
):
    pairs = [(assign_hbm, assign_ref), (order_hbm, order_ref), (lm_hbm, lm_ref), (uv_hbm, uv_ref)]
    for n in range(PIECES):
        piece = slice(n * (POOL // PIECES), (n + 1) * (POOL // PIECES))
        pairs.append((spec_hbm.at[:, piece, :], spec_ref.at[:, piece, :]))
    copies = [pltpu.make_async_copy(src, dst, sems.at[n]) for n, (src, dst) in enumerate(pairs)]
    for copy in copies:
        copy.start()
    for copy in copies[:4]:
        copy.wait()
    lh, lmid, ll = three_parts(lm_ref[...])
    zero = jnp.zeros((2, POOL), BF16)
    lm8_ref[...] = jnp.concatenate(
        [lh[0:1], lmid[0:1], ll[0:1], lh[1:2], lmid[1:2], ll[1:2], zero], axis=0
    )
    for q in range(N_DIR):
        u = uv_ref[0:1, q * QROWS : (q + 1) * QROWS]
        v = uv_ref[1:2, q * QROWS : (q + 1) * QROWS]
        uv8_ref[q] = jnp.concatenate([u, u, u, v, v, v, jnp.zeros((2, QROWS), BF16)], axis=0)
    assign = assign_ref[...]
    low = assign & 127
    high = assign >> 7
    segment = lax.broadcasted_iota(jnp.int32, (1, POOL), 1) // NCOMP
    place = jnp.zeros((1, POOL), F32)
    for p in range(DIR_DEV):
        place = jnp.where(segment == order_ref[p], float(p), place)
    low_hot = (lax.broadcasted_iota(jnp.int32, (128, POOL), 0) == low).astype(F32).astype(BF16)
    high_hot = jnp.where(lax.broadcasted_iota(jnp.int32, (32, POOL), 0) == high, place, 0.0).astype(BF16)
    pos = lax.dot_general(low_hot, high_hot, (((1,), (1,)), ((), ())), preferred_element_type=F32)
    column = lax.broadcasted_iota(jnp.int32, (32, POOL), 1) // 128
    pick = (column == lax.broadcasted_iota(jnp.int32, (32, POOL), 0)).astype(F32).astype(BF16)
    pos_ref[...] = jnp.dot(pos.astype(BF16), pick, preferred_element_type=F32)
    for column in range(POOL // 128):
        if column % (POOL // 128 // PIECES) == 0:
            copies[4 + column // (POOL // 128 // PIECES)].wait()
        place_here = pos_ref[:, column * 128 : (column + 1) * 128]
        for p in range(DIR_DEV):
            mask = jnp.where(place_here == float(p), 1.0, 0.0).astype(BF16)
            for part in range(2):
                first = part * CHUNK + (column % 2) * 128
                wide_ref[column // 2, first : first + 128, p * COLS : (p + 1) * COLS] = (
                    spec_ref[part, column * 128 : (column + 1) * 128, :] * mask
                )


def prepare(peel_order, assignment, comp_lm, uv_coords, spectra):
    return pl.pallas_call(
        prepare_kernel,
        out_shape=(
            jax.ShapeDtypeStruct((8, POOL), BF16),
            jax.ShapeDtypeStruct((N_DIR, 8, QROWS), BF16),
            jax.ShapeDtypeStruct((NCHUNK, 2 * CHUNK, WIDE), BF16),
        ),
        in_specs=[pl.BlockSpec(memory_space=pltpu.MemorySpace.HBM)] * 5,
        out_specs=(vmem(), vmem(), vmem()),
        scratch_shapes=[
            pltpu.SMEM((DIR_DEV,), jnp.int32),
            pltpu.VMEM((1, POOL), jnp.int32),
            pltpu.VMEM((2, POOL), F32),
            pltpu.VMEM((2, ROWS_DEV), BF16),
            pltpu.VMEM((2, POOL, COLS), BF16),
            pltpu.VMEM((128, POOL), F32),
            pltpu.SemaphoreType.DMA((4 + PIECES,)),
        ],
        compiler_params=params(16),
        name="prepare",
    )(*(
        pltpu.with_memory_space_constraint(value, pltpu.MemorySpace.HBM)
        for value in (peel_order, assignment.reshape(1, POOL), comp_lm, uv_coords, spectra)
    ))


def predict_kernel(flips, uv8_ref, lm8_ref, wide_ref, *rest):
    out_refs = rest[: len(flips)]
    tab_a, tab_b, acc_ref = rest[len(flips) :]
    me = own_place()[0]
    uv_rows = jnp.concatenate([uv8_ref[me ^ x].astype(F32).T for x in flips], axis=0).astype(BF16)

    def table(j, tab_ref):
        lm = lm8_ref[:, j * CHUNK : (j + 1) * CHUNK]
        turns = jnp.dot(uv_rows, lm, preferred_element_type=F32)
        cos, sin = cos_sin_turns(turns)
        tab_ref[:, :CHUNK] = cos.astype(BF16)
        tab_ref[:, CHUNK:] = sin.astype(BF16)

    tabs = (tab_a, tab_b)
    table(0, tab_a)
    for j in range(NCHUNK):
        if j + 1 < NCHUNK:
            table(j + 1, tabs[(j + 1) % 2])
        part = jnp.dot(tabs[j % 2][...], wide_ref[j], preferred_element_type=F32)
        if j == 0:
            acc_ref[...] = part
        else:
            acc_ref[...] += part
    for n in range(len(flips)):
        for p in range(DIR_DEV):
            out_refs[n][p] = acc_ref[n * QROWS : (n + 1) * QROWS, p * COLS : (p + 1) * COLS].astype(BF16)


def predict(flips, uv8, lm8, wide):
    rows = QROWS * len(flips)

    def kernel(*refs):
        predict_kernel(flips, *refs)

    return pl.pallas_call(
        kernel,
        out_shape=tuple(jax.ShapeDtypeStruct((DIR_DEV, QROWS, COLS), BF16) for _ in flips),
        in_specs=[vmem(), vmem(), vmem()],
        out_specs=tuple(vmem() for _ in flips),
        scratch_shapes=[
            pltpu.VMEM((rows, 2 * CHUNK), BF16),
            pltpu.VMEM((rows, 2 * CHUNK), BF16),
            pltpu.VMEM((rows, WIDE), F32),
        ],
        cost_estimate=pl.CostEstimate(
            flops=2 * rows * 2 * POOL * 2 * WIDE,
            transcendentals=0,
            bytes_accessed=2 * (2 * POOL * WIDE + rows * WIDE),
        ),
        compiler_params=params(16),
        name="predict",
    )(uv8, lm8, wide)


def per_block_sum(value):
    return jnp.sum(value.reshape(QROWS // GB, GB, COLS), axis=1)


def lane_shift(value, by):
    return pltpu.roll(value, (-by) % COLS, 1)


def sweeps(pull):
    lane = lax.broadcasted_iota(jnp.int32, pull.shape, 1)
    first, last = lane < 2, lane >= COLS - 2
    band = {0: jnp.ones_like(pull)}
    free = pull
    for _ in range(ITERS - 1):
        lower = {d: lane_shift(value, -2) for d, value in band.items()}
        upper = {d: lane_shift(value, 2) for d, value in band.items()}
        new = {}
        for d, value in band.items():
            for at, inside, kept in ((d - 2, lower[d], first), (d + 2, upper[d], last)):
                moved = jnp.where(kept, 0.0, inside)
                new[at] = new[at] + moved if at in new else moved
                stays = jnp.where(kept, value, 0.0)
                new[d] = new[d] + stays if d in new else stays
        band = {d: (0.5 * pull) * value for d, value in new.items()}
        band[0] = band[0] + 1.0
        around = jnp.where(first, free, lane_shift(free, -2)) + jnp.where(last, free, lane_shift(free, 2))
        free = pull * (0.5 * around)
    return band, free


SHIFTS = tuple(range(-2 * (ITERS - 1), 2 * ITERS, 2))


def peel_kernel(vis_ref, ridge_ref, m0_ref, m1_ref, m2_ref, m3_ref, out_ref, *rest):
    part_refs, (model_ref, inv_ref, band_ref, part_ref) = rest[:N_DIR], rest[N_DIR:]
    me = own_place()[0]
    ridge = ridge_ref[...]
    blocks = QROWS // GB
    for x, ref in enumerate((m0_ref, m1_ref, m2_ref, m3_ref)):
        owner = me ^ x
        for p in range(DIR_DEV):
            model = ref[p].astype(F32)
            model_ref[owner * DIR_DEV + p] = model
            inv_ref[pl.ds((owner * DIR_DEV + p) * 8, blocks), :] = per_block_sum(model * model)
    inv = 1.0 / (inv_ref[...] + ridge)
    band, free = sweeps(ridge * inv)
    for n, d in enumerate(SHIFTS):
        band_ref[n] = band[d] * lane_shift(inv, d)
    band_ref[len(SHIFTS)] = free
    remains = vis_ref[pl.ds(pl.multiple_of(me * QROWS, QROWS), QROWS), :].astype(F32)
    for j in range(N_DIR * DIR_DEV):
        model = model_ref[j]
        cross = per_block_sum(remains * model)
        gain = band_ref[len(SHIFTS), j * 8 : j * 8 + blocks, :]
        for n, d in enumerate(SHIFTS):
            gain = gain + band_ref[n, j * 8 : j * 8 + blocks, :] * (lane_shift(cross, d) if d else cross)
        spread = jnp.concatenate(
            [jnp.broadcast_to(gain[b : b + 1], (GB, COLS)) for b in range(blocks)], axis=0
        )
        remains = remains - spread * model
        if (j + 1) % DIR_DEV == 0:
            remains = remains.astype(BF16).astype(F32)
    out_ref[...] = remains.astype(BF16)
    part_ref[...] = remains.reshape(QBLOCKS, 2, PART, COLS)
    for x in range(N_DIR):
        part_refs[x][...] = part_ref[:, (me ^ x) & 1].astype(BF16)


def peel(visibilities, ridge_weight, models):
    out = pl.pallas_call(
        peel_kernel,
        out_shape=(jax.ShapeDtypeStruct((QROWS, COLS), BF16),)
        + (jax.ShapeDtypeStruct((QBLOCKS, PART, COLS), BF16),) * N_DIR,
        in_specs=[vmem()] * 6,
        out_specs=(vmem(),) * (1 + N_DIR),
        scratch_shapes=[
            pltpu.VMEM((N_DIR * DIR_DEV, QROWS, COLS), F32),
            pltpu.VMEM((N_DIR * DIR_DEV * 8, COLS), F32),
            pltpu.VMEM((len(SHIFTS) + 1, N_DIR * DIR_DEV * 8, COLS), F32),
            pltpu.VMEM((QBLOCKS, 2, PART, COLS), F32),
        ],
        compiler_params=params(16),
        name="peel",
    )(visibilities, ridge_weight.reshape(1, COLS), *models)
    return out[0], out[1:]


def label_kernel(tile_ref, uv_ref, coords_ref, place_ref):
    me, half, offset = own_place()
    tiles = tile_ref[...].astype(F32)
    block_of_lane = lax.broadcasted_iota(jnp.int32, (NB, ROWS_DEV), 1) // BB
    expand = (block_of_lane == lax.broadcasted_iota(jnp.int32, (NB, ROWS_DEV), 0)).astype(F32)
    tile_of_lane = jnp.sum(expand * tiles, axis=0, keepdims=True)
    sub = lax.broadcasted_iota(jnp.int32, (NB, NB), 0)
    col = lax.broadcasted_iota(jnp.int32, (NB, NB), 1)
    tile_row = jnp.sum(jnp.where(sub == col, tiles, 0.0), axis=0, keepdims=True)
    slot = jnp.sum(jnp.where((tiles == tile_row) & (col < sub), 1.0, 0.0), axis=1, keepdims=True)
    part_lane = lax.broadcasted_iota(jnp.int32, (NB, NB * PART), 1)
    block = ((part_lane // (QBLOCKS * PART)) ^ me) * QBLOCKS + (part_lane // PART) % QBLOCKS
    mine = block == lax.broadcasted_iota(jnp.int32, (NB, NB * PART), 0)
    first = (tiles * SLOTS + slot) * PART
    goal_row = jnp.sum(jnp.where(mine, first, 0.0), axis=0, keepdims=True).astype(jnp.int32)
    goal_row = goal_row + part_lane[0:1] % PART
    for n in range(N_TB * SLOTS * PART // 512):
        row = lax.broadcasted_iota(jnp.int32, (512, NB * PART), 0) + n * 512
        place_ref[n * 512 : (n + 1) * 512, :] = jnp.where(row == goal_row, 1.0, 0.0).astype(BF16)
    slot_of_row = lax.dot_general(
        expand.astype(BF16),
        jnp.broadcast_to(slot, (NB, COLS)).astype(BF16),
        (((0,), (0,)), ((), ())),
        preferred_element_type=F32,
    )
    within = lax.broadcasted_iota(jnp.int32, (ROWS_DEV, COLS), 0) % BB - half * PART
    lane = lax.broadcasted_iota(jnp.int32, (ROWS_DEV, COLS), 1)
    goal = slot_of_row.astype(jnp.int32) * PART + within + offset
    spot = jnp.where((goal == lane) & (within >= 0) & (within < PART), 1.0, 0.0).astype(BF16)
    row = lax.broadcasted_iota(jnp.int32, (N_TB * 8, ROWS_DEV), 0)
    u = uv_ref[0:1, :].astype(F32)
    v = uv_ref[1:2, :].astype(F32)
    value = jnp.where(row % 8 == 0, u, jnp.where(row % 8 == 1, v, 0.0))
    value = jnp.where((row // 8).astype(F32) == tile_of_lane, value, 0.0).astype(BF16)
    out = jnp.dot(value, spot, preferred_element_type=F32)
    coords_ref[...] = out.reshape(N_TB, 8, COLS).astype(BF16)


def label(block_tile, uv_coords):
    return pl.pallas_call(
        label_kernel,
        out_shape=(
            jax.ShapeDtypeStruct((N_TB, 8, COLS), BF16),
            jax.ShapeDtypeStruct((N_TB * SLOTS * PART, NB * PART), BF16),
        ),
        in_specs=[vmem(), vmem()],
        out_specs=(vmem(), vmem()),
        compiler_params=params(24),
        name="label",
    )(block_tile, uv_coords)


def pack_kernel(r0_ref, r1_ref, r2_ref, r3_ref, coords_ref, place_ref, out_ref):
    rows = jnp.concatenate(
        [ref[...].reshape(QBLOCKS * PART, COLS) for ref in (r0_ref, r1_ref, r2_ref, r3_ref)], axis=0
    )
    tiles = 512 // (SLOTS * PART)
    for n in range(N_TB // tiles):
        placed = jnp.dot(place_ref[n * 512 : (n + 1) * 512, :], rows, preferred_element_type=F32)
        out_ref[n * tiles : (n + 1) * tiles, : SLOTS * PART, :] = placed.reshape(
            tiles, SLOTS * PART, COLS
        ).astype(BF16)
    out_ref[:, SLOTS * PART :, :] = coords_ref[...]


def pack(rows, coords, place):
    return pl.pallas_call(
        pack_kernel,
        out_shape=jax.ShapeDtypeStruct((N_TB, SEND_ROWS, COLS), BF16),
        in_specs=[vmem()] * 6,
        out_specs=vmem(),
        compiler_params=params(16),
        name="pack",
    )(*rows, coords, place)


def join_kernel(r0_ref, r1_ref, r2_ref, r3_ref, out_ref):
    me = own_place()[0]
    for x, ref in enumerate((r0_ref, r1_ref, r2_ref, r3_ref)):
        out_ref[pl.ds(pl.multiple_of((me ^ x) * QROWS, QROWS), QROWS), :] = ref[...]


def join(rows):
    return pl.pallas_call(
        join_kernel,
        out_shape=jax.ShapeDtypeStruct((ROWS_DEV, COLS), BF16),
        in_specs=[vmem()] * 4,
        out_specs=vmem(),
        compiler_params=params(16),
        name="join",
    )(*rows)


def grid_kernel(got_ref, keep_ref, give_ref, tab_ref, acc_ref):
    chip = own_place()[0] // 2
    half = own_place()[1]
    tiles = N_TB * SLOTS * PART // 128
    groups = N_TB // tiles
    coords = got_ref[:, SLOTS * PART :, :].astype(F32).reshape(tiles, groups, 8, COLS)
    coords = jnp.sum(coords, axis=1)
    y_pixel = (lax.broadcasted_iota(jnp.int32, (GRID, 1), 0) - GRID // 2).astype(F32)
    order = lax.broadcasted_iota(jnp.int32, (16, 1), 0)
    x_pixel = (16 * chip + 8 * ((order // 8) ^ half) + order % 8 - GRID // 2).astype(F32)
    scale = 1.0 / (2.0 * GRID)
    step = 256
    per_step = step // 128

    def product(n):
        sources = step // (SLOTS * PART)
        rows = got_ref[n * sources : (n + 1) * sources, : SLOTS * PART, :].reshape(step, COLS)
        return jnp.dot(tab_ref[n], rows, preferred_element_type=F32)

    for tile in range(tiles):
        u = coords[tile, 0:1, :] * scale
        v = coords[tile, 1:2, :] * scale
        cx, sx = cos_sin_turns(x_pixel * u)
        cy, sy = cos_sin_turns(y_pixel * v)
        n, lanes = tile // per_step, slice(tile % per_step * 128, (tile % per_step + 1) * 128)
        for x in range(16):
            a, b = cx[x : x + 1], sx[x : x + 1]
            tab_ref[n, x * GRID : (x + 1) * GRID, lanes] = (a * cy - b * sy).astype(BF16)
            tab_ref[n, 512 + x * GRID : 512 + (x + 1) * GRID, lanes] = (b * cy + a * sy).astype(BF16)
        if tile % per_step == per_step - 1:
            if n == 0:
                acc_ref[...] = product(n)
            else:
                acc_ref[...] += product(n)
    total = acc_ref[...] * float(ROWS_DEV) ** (-0.5)
    for part in range(2):
        keep_ref[part] = total[part * 512 : part * 512 + 256]
        give_ref[part] = total[part * 512 + 256 : part * 512 + 512]


def grid_rows(got):
    return pl.pallas_call(
        grid_kernel,
        out_shape=(
            jax.ShapeDtypeStruct((2, PIX // N_DIR, COLS), F32),
            jax.ShapeDtypeStruct((2, PIX // N_DIR, COLS), F32),
        ),
        in_specs=[vmem()],
        out_specs=(vmem(), vmem()),
        scratch_shapes=[
            pltpu.VMEM((N_TB * SLOTS * PART // 256, 1024, 256), BF16),
            pltpu.VMEM((1024, COLS), F32),
        ],
        compiler_params=params(24),
        name="grid",
    )(got)


def after(value, done):
    return lax.optimization_barrier((value, done))[0]


def swap(value, flip):
    return lax.ppermute(value, "dir", [(i, i ^ flip) for i in range(N_DIR)])


def local(
    visibilities, uv_coords, comp_lm, spectra, ridge_weight, assignment, peel_order, block_tile
):
    lm8, uv8, wide = prepare(peel_order, assignment, comp_lm, uv_coords, spectra)
    far_a, far_b = predict((2, 3), uv8, lm8, wide)
    got_a, got_b = swap(far_a, 2), swap(far_b, 3)
    near, own = predict((1, 0), uv8, lm8, wide)
    got_near = swap(near, 1)
    rows, parts = peel(visibilities, ridge_weight, (own, got_near, got_a, got_b))
    coords, place = label(after(block_tile, rows), uv_coords)
    shared = [parts[0]] + [swap(parts[x], x) for x in range(1, N_DIR)]
    send = pack(shared, coords, place)
    got = lax.all_to_all(send, "tb", split_axis=0, concat_axis=0, tiled=True)
    late = after(rows, send)
    residual = join([late] + [swap(late, x) for x in range(1, N_DIR)])
    keep, give = grid_rows(after(got, residual))
    return residual, (keep + swap(give, 1))[None]


def solution(mesh):
    return jax.shard_map(
        local,
        mesh=mesh,
        in_specs=(
            P("tb", None),
            P(None, "tb"),
            P(None, "dir"),
            P(None, "dir", None),
            P(),
            P("dir"),
            P("dir"),
            P("tb", None),
        ),
        out_specs=(P("tb", None), P("tb", None, "dir", None)),
        check_vma=False,
    )
```

```python
import jax
import jax.numpy as jnp
from jax import lax
from jax.experimental import pallas as pl
from jax.experimental.pallas import tpu as pltpu
from jax.sharding import PartitionSpec as P

NCOMP = 1024
GRID = 32
DIR_DEV = 3
ITERS = 4
BB = 32
GB = 128
ROWS_DEV = 1024
PIX = 1024
COLS = 128
N_DIR = 4
N_TB = 64
NB = 32
SLOTS = 2
QROWS = ROWS_DEV // N_DIR
PART = BB // 2
POOL = DIR_DEV * NCOMP
WIDE = DIR_DEV * COLS
CHUNK = 256
NCHUNK = POOL // CHUNK
PIECES = 4
SEND_ROWS = SLOTS * PART + 8
QBLOCKS = QROWS // BB

F32 = jnp.float32
BF16 = jnp.bfloat16

SIN_C = (2.6417407853784525, -1.0859537956447276, 0.1306204657138272)
COS_C = (1.681792784129167, -2.074822793580374, 0.42650038149094444, -0.03432262097868313)
ROOT2 = 1.4142135623730951


def own_place():
    me = lax.axis_index("dir")
    return me, me & 1, (lax.axis_index("tb") & 3) * (SLOTS * PART)


def vmem():
    return pl.BlockSpec(memory_space=pltpu.VMEM)


def smem():
    return pl.BlockSpec(memory_space=pltpu.SMEM)


def params(mib):
    return pltpu.CompilerParams(vmem_limit_bytes=mib << 20)


def cos_sin_turns(turns):
    r = turns - jnp.round(turns)
    z = r * r
    s = ((SIN_C[2] * z + SIN_C[1]) * z + SIN_C[0]) * r
    c = ((COS_C[3] * z + COS_C[2]) * z + COS_C[1]) * z + COS_C[0]
    s1 = s * c
    c1 = ROOT2 - s * s
    return 1.0 - s1 * s1, s1 * c1


def three_parts(value):
    high = value.astype(BF16)
    left = value - high.astype(F32)
    mid = left.astype(BF16)
    low = (left - mid.astype(F32)).astype(BF16)
    return high, mid, low


def prepare_kernel(
    order_hbm, assign_hbm, lm_hbm, uv_hbm, spec_hbm, lm8_ref, uv8_ref, wide_ref,
    order_ref, assign_ref, lm_ref, uv_ref, spec_ref, pos_ref, sems
):
    pairs = [(assign_hbm, assign_ref), (order_hbm, order_ref), (lm_hbm, lm_ref), (uv_hbm, uv_ref)]
    for n in range(PIECES):
        piece = slice(n * (POOL // PIECES), (n + 1) * (POOL // PIECES))
        pairs.append((spec_hbm.at[:, piece, :], spec_ref.at[:, piece, :]))
    copies = [pltpu.make_async_copy(src, dst, sems.at[n]) for n, (src, dst) in enumerate(pairs)]
    for copy in copies:
        copy.start()
    for copy in copies[:4]:
        copy.wait()
    lh, lmid, ll = three_parts(lm_ref[...])
    zero = jnp.zeros((2, POOL), BF16)
    lm8_ref[...] = jnp.concatenate(
        [lh[0:1], lmid[0:1], ll[0:1], lh[1:2], lmid[1:2], ll[1:2], zero], axis=0
    )
    for q in range(N_DIR):
        u = uv_ref[0:1, q * QROWS : (q + 1) * QROWS]
        v = uv_ref[1:2, q * QROWS : (q + 1) * QROWS]
        uv8_ref[q] = jnp.concatenate([u, u, u, v, v, v, jnp.zeros((2, QROWS), BF16)], axis=0)
    assign = assign_ref[...]
    low = assign & 127
    high = assign >> 7
    segment = lax.broadcasted_iota(jnp.int32, (1, POOL), 1) // NCOMP
    place = jnp.zeros((1, POOL), F32)
    for p in range(DIR_DEV):
        place = jnp.where(segment == order_ref[p], float(p), place)
    low_hot = (lax.broadcasted_iota(jnp.int32, (128, POOL), 0) == low).astype(F32).astype(BF16)
    high_hot = jnp.where(lax.broadcasted_iota(jnp.int32, (32, POOL), 0) == high, place, 0.0).astype(BF16)
    pos = lax.dot_general(low_hot, high_hot, (((1,), (1,)), ((), ())), preferred_element_type=F32)
    column = lax.broadcasted_iota(jnp.int32, (32, POOL), 1) // 128
    pick = (column == lax.broadcasted_iota(jnp.int32, (32, POOL), 0)).astype(F32).astype(BF16)
    pos_ref[...] = jnp.dot(pos.astype(BF16), pick, preferred_element_type=F32)
    for column in range(POOL // 128):
        if column % (POOL // 128 // PIECES) == 0:
            copies[4 + column // (POOL // 128 // PIECES)].wait()
        place_here = pos_ref[:, column * 128 : (column + 1) * 128]
        for p in range(DIR_DEV):
            mask = jnp.where(place_here == float(p), 1.0, 0.0).astype(BF16)
            for part in range(2):
                first = part * CHUNK + (column % 2) * 128
                wide_ref[column // 2, first : first + 128, p * COLS : (p + 1) * COLS] = (
                    spec_ref[part, column * 128 : (column + 1) * 128, :] * mask
                )


def prepare(peel_order, assignment, comp_lm, uv_coords, spectra):
    return pl.pallas_call(
        prepare_kernel,
        out_shape=(
            jax.ShapeDtypeStruct((8, POOL), BF16),
            jax.ShapeDtypeStruct((N_DIR, 8, QROWS), BF16),
            jax.ShapeDtypeStruct((NCHUNK, 2 * CHUNK, WIDE), BF16),
        ),
        in_specs=[pl.BlockSpec(memory_space=pltpu.MemorySpace.HBM)] * 5,
        out_specs=(vmem(), vmem(), vmem()),
        scratch_shapes=[
            pltpu.SMEM((DIR_DEV,), jnp.int32),
            pltpu.VMEM((1, POOL), jnp.int32),
            pltpu.VMEM((2, POOL), F32),
            pltpu.VMEM((2, ROWS_DEV), BF16),
            pltpu.VMEM((2, POOL, COLS), BF16),
            pltpu.VMEM((128, POOL), F32),
            pltpu.SemaphoreType.DMA((4 + PIECES,)),
        ],
        compiler_params=params(16),
        name="prepare",
    )(*(
        pltpu.with_memory_space_constraint(value, pltpu.MemorySpace.HBM)
        for value in (peel_order, assignment.reshape(1, POOL), comp_lm, uv_coords, spectra)
    ))


def predict_kernel(flips, uv8_ref, lm8_ref, wide_ref, *rest):
    out_refs = rest[: len(flips)]
    tab_a, tab_b, acc_ref = rest[len(flips) :]
    me = own_place()[0]
    uv_rows = jnp.concatenate([uv8_ref[me ^ x].astype(F32).T for x in flips], axis=0).astype(BF16)

    def table(j, tab_ref):
        lm = lm8_ref[:, j * CHUNK : (j + 1) * CHUNK]
        turns = jnp.dot(uv_rows, lm, preferred_element_type=F32)
        cos, sin = cos_sin_turns(turns)
        tab_ref[:, :CHUNK] = cos.astype(BF16)
        tab_ref[:, CHUNK:] = sin.astype(BF16)

    tabs = (tab_a, tab_b)
    table(0, tab_a)
    for j in range(NCHUNK):
        if j + 1 < NCHUNK:
            table(j + 1, tabs[(j + 1) % 2])
        part = jnp.dot(tabs[j % 2][...], wide_ref[j], preferred_element_type=F32)
        if j == 0:
            acc_ref[...] = part
        else:
            acc_ref[...] += part
    for n in range(len(flips)):
        for p in range(DIR_DEV):
            out_refs[n][p] = acc_ref[n * QROWS : (n + 1) * QROWS, p * COLS : (p + 1) * COLS].astype(BF16)


def predict(flips, uv8, lm8, wide):
    rows = QROWS * len(flips)

    def kernel(*refs):
        predict_kernel(flips, *refs)

    return pl.pallas_call(
        kernel,
        out_shape=tuple(jax.ShapeDtypeStruct((DIR_DEV, QROWS, COLS), BF16) for _ in flips),
        in_specs=[vmem(), vmem(), vmem()],
        out_specs=tuple(vmem() for _ in flips),
        scratch_shapes=[
            pltpu.VMEM((rows, 2 * CHUNK), BF16),
            pltpu.VMEM((rows, 2 * CHUNK), BF16),
            pltpu.VMEM((rows, WIDE), F32),
        ],
        cost_estimate=pl.CostEstimate(
            flops=2 * rows * 2 * POOL * 2 * WIDE,
            transcendentals=0,
            bytes_accessed=2 * (2 * POOL * WIDE + rows * WIDE),
        ),
        compiler_params=params(16),
        name="predict",
    )(uv8, lm8, wide)


def per_block_sum(value):
    return jnp.sum(value.reshape(QROWS // GB, GB, COLS), axis=1)


def lane_shift(value, by):
    return pltpu.roll(value, (-by) % COLS, 1)


def sweeps(pull):
    lane = lax.broadcasted_iota(jnp.int32, pull.shape, 1)
    first, last = lane < 2, lane >= COLS - 2
    band = {0: jnp.ones_like(pull)}
    free = pull
    for _ in range(ITERS - 1):
        lower = {d: lane_shift(value, -2) for d, value in band.items()}
        upper = {d: lane_shift(value, 2) for d, value in band.items()}
        new = {}
        for d, value in band.items():
            for at, inside, kept in ((d - 2, lower[d], first), (d + 2, upper[d], last)):
                moved = jnp.where(kept, 0.0, inside)
                new[at] = new[at] + moved if at in new else moved
                stays = jnp.where(kept, value, 0.0)
                new[d] = new[d] + stays if d in new else stays
        band = {d: (0.5 * pull) * value for d, value in new.items()}
        band[0] = band[0] + 1.0
        around = jnp.where(first, free, lane_shift(free, -2)) + jnp.where(last, free, lane_shift(free, 2))
        free = pull * (0.5 * around)
    return band, free


SHIFTS = tuple(range(-2 * (ITERS - 1), 2 * ITERS, 2))


def peel_kernel(vis_ref, ridge_ref, m0_ref, m1_ref, m2_ref, m3_ref, out_ref, *rest):
    part_refs, (model_ref, inv_ref, band_ref, part_ref) = rest[:N_DIR], rest[N_DIR:]
    me = own_place()[0]
    ridge = ridge_ref[...]
    blocks = QROWS // GB
    for x, ref in enumerate((m0_ref, m1_ref, m2_ref, m3_ref)):
        owner = me ^ x
        for p in range(DIR_DEV):
            model = ref[p].astype(F32)
            model_ref[owner * DIR_DEV + p] = model
            inv_ref[pl.ds((owner * DIR_DEV + p) * 8, blocks), :] = per_block_sum(model * model)
    inv = 1.0 / (inv_ref[...] + ridge)
    band, free = sweeps(ridge * inv)
    for n, d in enumerate(SHIFTS):
        band_ref[n] = band[d] * lane_shift(inv, d)
    band_ref[len(SHIFTS)] = free
    remains = vis_ref[pl.ds(pl.multiple_of(me * QROWS, QROWS), QROWS), :].astype(F32)
    for j in range(N_DIR * DIR_DEV):
        model = model_ref[j]
        cross = per_block_sum(remains * model)
        gain = band_ref[len(SHIFTS), j * 8 : j * 8 + blocks, :]
        for n, d in enumerate(SHIFTS):
            gain = gain + band_ref[n, j * 8 : j * 8 + blocks, :] * (lane_shift(cross, d) if d else cross)
        spread = jnp.concatenate(
            [jnp.broadcast_to(gain[b : b + 1], (GB, COLS)) for b in range(blocks)], axis=0
        )
        remains = remains - spread * model
        if (j + 1) % DIR_DEV == 0:
            remains = remains.astype(BF16).astype(F32)
    out_ref[...] = remains.astype(BF16)
    part_ref[...] = remains.reshape(QBLOCKS, 2, PART, COLS)
    for x in range(N_DIR):
        part_refs[x][...] = part_ref[:, (me ^ x) & 1].astype(BF16)


def peel(visibilities, ridge_weight, models):
    out = pl.pallas_call(
        peel_kernel,
        out_shape=(jax.ShapeDtypeStruct((QROWS, COLS), BF16),)
        + (jax.ShapeDtypeStruct((QBLOCKS, PART, COLS), BF16),) * N_DIR,
        in_specs=[vmem()] * 6,
        out_specs=(vmem(),) * (1 + N_DIR),
        scratch_shapes=[
            pltpu.VMEM((N_DIR * DIR_DEV, QROWS, COLS), F32),
            pltpu.VMEM((N_DIR * DIR_DEV * 8, COLS), F32),
            pltpu.VMEM((len(SHIFTS) + 1, N_DIR * DIR_DEV * 8, COLS), F32),
            pltpu.VMEM((QBLOCKS, 2, PART, COLS), F32),
        ],
        compiler_params=params(16),
        name="peel",
    )(visibilities, ridge_weight.reshape(1, COLS), *models)
    return out[0], out[1:]


def label_kernel(tile_id_ref, tile_ref, uv_ref, out_ref, slot_ref, seen_ref):
    half = own_place()[1]
    offset = own_place()[2]
    tiles = tile_ref[...].astype(F32)
    block_of_lane = lax.broadcasted_iota(jnp.int32, (NB, ROWS_DEV), 1) // BB
    expand = (block_of_lane == lax.broadcasted_iota(jnp.int32, (NB, ROWS_DEV), 0)).astype(F32)
    tile_of_lane = jnp.sum(expand * tiles, axis=0, keepdims=True)
    sub = lax.broadcasted_iota(jnp.int32, (NB, NB), 0)
    col = lax.broadcasted_iota(jnp.int32, (NB, NB), 1)
    tile_row = jnp.sum(jnp.where(sub == col, tiles, 0.0), axis=0, keepdims=True)
    slot = jnp.sum(jnp.where((tiles == tile_row) & (col < sub), 1.0, 0.0), axis=1, keepdims=True)
    slot_of_row = lax.dot_general(
        expand.astype(BF16),
        jnp.broadcast_to(slot, (NB, COLS)).astype(BF16),
        (((0,), (0,)), ((), ())),
        preferred_element_type=F32,
    )
    within = lax.broadcasted_iota(jnp.int32, (ROWS_DEV, COLS), 0) % BB - half * PART
    lane = lax.broadcasted_iota(jnp.int32, (ROWS_DEV, COLS), 1)
    goal = slot_of_row.astype(jnp.int32) * PART + within + offset
    spot = jnp.where((goal == lane) & (within >= 0) & (within < PART), 1.0, 0.0).astype(BF16)
    row = lax.broadcasted_iota(jnp.int32, (N_TB * 8, ROWS_DEV), 0)
    u = uv_ref[0:1, :].astype(F32)
    v = uv_ref[1:2, :].astype(F32)
    value = jnp.where(row % 8 == 0, u, jnp.where(row % 8 == 1, v, 0.0))
    value = jnp.where((row // 8).astype(F32) == tile_of_lane, value, 0.0).astype(BF16)
    out = jnp.dot(value, spot, preferred_element_type=F32)
    out_ref[:, : SLOTS * PART, :] = jnp.zeros((N_TB, SLOTS * PART, COLS), BF16)
    out_ref[:, SLOTS * PART :, :] = out.reshape(N_TB, 8, COLS).astype(BF16)
    for t in range(N_TB):
        seen_ref[t] = 0
    for b in range(NB):
        tile = tile_id_ref[b]
        slot_ref[b] = seen_ref[tile]
        seen_ref[tile] = 1


def label(tile_ids, block_tile, uv_coords):
    return pl.pallas_call(
        label_kernel,
        out_shape=(
            jax.ShapeDtypeStruct((N_TB, SEND_ROWS, COLS), BF16),
            jax.ShapeDtypeStruct((NB,), jnp.int32),
        ),
        in_specs=[smem(), vmem(), vmem()],
        out_specs=(vmem(), smem()),
        scratch_shapes=[pltpu.SMEM((N_TB,), jnp.int32)],
        compiler_params=params(16),
        name="label",
    )(tile_ids, block_tile, uv_coords)


def pack_kernel(tile_ref, slot_ref, r0_ref, r1_ref, r2_ref, r3_ref, base_ref, out_ref, stage_ref):
    me = own_place()[0]
    out_ref[...] = base_ref[...]
    for x, ref in enumerate((r0_ref, r1_ref, r2_ref, r3_ref)):
        stage_ref[pl.ds((me ^ x) * QBLOCKS, QBLOCKS)] = ref[...]
    for b in range(NB):
        first = pl.multiple_of(slot_ref[b] * PART, PART)
        out_ref[tile_ref[b], pl.ds(first, PART), :] = stage_ref[b]


def pack(tile_ids, slots, rows, base):
    return pl.pallas_call(
        pack_kernel,
        out_shape=jax.ShapeDtypeStruct((N_TB, SEND_ROWS, COLS), BF16),
        in_specs=[smem(), smem()] + [vmem()] * 5,
        out_specs=vmem(),
        scratch_shapes=[pltpu.VMEM((NB, PART, COLS), BF16)],
        compiler_params=params(16),
        name="pack",
    )(tile_ids, slots, *rows, base)


def join_kernel(r0_ref, r1_ref, r2_ref, r3_ref, out_ref):
    me = own_place()[0]
    for x, ref in enumerate((r0_ref, r1_ref, r2_ref, r3_ref)):
        out_ref[pl.ds(pl.multiple_of((me ^ x) * QROWS, QROWS), QROWS), :] = ref[...]


def join(rows):
    return pl.pallas_call(
        join_kernel,
        out_shape=jax.ShapeDtypeStruct((ROWS_DEV, COLS), BF16),
        in_specs=[vmem()] * 4,
        out_specs=vmem(),
        compiler_params=params(16),
        name="join",
    )(*rows)


def grid_kernel(flip, got_ref, out_ref, tab_ref, acc_ref):
    me, half, _ = own_place()
    chip = me // 2
    tiles = N_TB * SLOTS * PART // 128
    groups = N_TB // tiles
    coords = got_ref[:, SLOTS * PART :, :].astype(F32).reshape(tiles, groups, 8, COLS)
    coords = jnp.sum(coords, axis=1)
    y_pixel = (lax.broadcasted_iota(jnp.int32, (GRID, 1), 0) - GRID // 2).astype(F32)
    order = lax.broadcasted_iota(jnp.int32, (8, 1), 0)
    x_pixel = (16 * chip + 8 * (half ^ flip) + order - GRID // 2).astype(F32)
    scale = 1.0 / (2.0 * GRID)
    share = PIX // N_DIR
    step = 256
    per_step = step // 128

    def product(n):
        sources = step // (SLOTS * PART)
        rows = got_ref[n * sources : (n + 1) * sources, : SLOTS * PART, :].reshape(step, COLS)
        return jnp.dot(tab_ref[n], rows, preferred_element_type=F32)

    for tile in range(tiles):
        u = coords[tile, 0:1, :] * scale
        v = coords[tile, 1:2, :] * scale
        cx, sx = cos_sin_turns(x_pixel * u)
        cy, sy = cos_sin_turns(y_pixel * v)
        n, lanes = tile // per_step, slice(tile % per_step * 128, (tile % per_step + 1) * 128)
        for x in range(8):
            a, b = cx[x : x + 1], sx[x : x + 1]
            tab_ref[n, x * GRID : (x + 1) * GRID, lanes] = (a * cy - b * sy).astype(BF16)
            tab_ref[n, share + x * GRID : share + (x + 1) * GRID, lanes] = (b * cy + a * sy).astype(BF16)
        if tile % per_step == per_step - 1:
            if n == 0:
                acc_ref[...] = product(n)
            else:
                acc_ref[...] += product(n)
    total = acc_ref[...] * float(ROWS_DEV) ** (-0.5)
    for part in range(2):
        out_ref[part] = total[part * share : (part + 1) * share]


def grid_rows(flip, got):
    def kernel(*refs):
        grid_kernel(flip, *refs)

    return pl.pallas_call(
        kernel,
        out_shape=jax.ShapeDtypeStruct((2, PIX // N_DIR, COLS), F32),
        in_specs=[vmem()],
        out_specs=vmem(),
        scratch_shapes=[
            pltpu.VMEM((N_TB * SLOTS * PART // 256, 512, 256), BF16),
            pltpu.VMEM((512, COLS), F32),
        ],
        cost_estimate=pl.CostEstimate(flops=2 * 10**9, transcendentals=0, bytes_accessed=10**6),
        compiler_params=params(24),
        name="grid",
    )(got)


def after(value, done):
    return lax.optimization_barrier((value, done))[0]


def swap(value, flip):
    return lax.ppermute(value, "dir", [(i, i ^ flip) for i in range(N_DIR)])


def local(
    visibilities, uv_coords, comp_lm, spectra, ridge_weight, assignment, peel_order, block_tile
):
    lm8, uv8, wide = prepare(peel_order, assignment, comp_lm, uv_coords, spectra)
    far_a, far_b = predict((2, 3), uv8, lm8, wide)
    got_a, got_b = swap(far_a, 2), swap(far_b, 3)
    near, own = predict((1, 0), uv8, lm8, wide)
    got_near = swap(near, 1)
    tile_ids = block_tile[:, 0]
    base, slots = label(after(tile_ids, own), block_tile, uv_coords)
    rows, parts = peel(after(visibilities, slots), ridge_weight, (own, got_near, got_a, got_b))
    shared = [parts[0]] + [swap(parts[x], x) for x in range(1, N_DIR)]
    send = pack(tile_ids, slots, shared, base)
    got = lax.all_to_all(send, "tb", split_axis=0, concat_axis=0, tiled=True)
    late = after(rows, send)
    residual = join([late] + [swap(late, x) for x in range(1, N_DIR)])
    got = after(got, residual)
    moved = swap(grid_rows(1, got), 1)
    keep = grid_rows(0, got)
    return residual, (keep + moved)[None]


def solution(mesh):
    return jax.shard_map(
        local,
        mesh=mesh,
        in_specs=(
            P("tb", None),
            P(None, "tb"),
            P(None, "dir"),
            P(None, "dir", None),
            P(),
            P("dir"),
            P("dir"),
            P("tb", None),
        ),
        out_specs=(P("tb", None), P("tb", None, "dir", None)),
        check_vma=False,
    )
```

```python
import jax
import jax.numpy as jnp
from jax import lax
from jax.experimental import pallas as pl
from jax.experimental.pallas import tpu as pltpu
from jax.sharding import PartitionSpec as P

NCOMP = 1024
GRID = 32
DIR_DEV = 3
ITERS = 4
BB = 32
GB = 128
ROWS_DEV = 1024
PIX = 1024
COLS = 128
N_DIR = 4
N_TB = 64
NB = 32
SLOTS = 2
QROWS = ROWS_DEV // N_DIR
PART = BB // 2
POOL = DIR_DEV * NCOMP
WIDE = DIR_DEV * COLS
CHUNK = 256
NCHUNK = POOL // CHUNK
PIECES = 4
SEND_ROWS = SLOTS * PART + 8
QBLOCKS = QROWS // BB

F32 = jnp.float32
BF16 = jnp.bfloat16

SIN_C = (2.6417407853784525, -1.0859537956447276, 0.1306204657138272)
COS_C = (1.681792784129167, -2.074822793580374, 0.42650038149094444, -0.03432262097868313)
ROOT2 = 1.4142135623730951


def own_place():
    me = lax.axis_index("dir")
    return me, me & 1, (lax.axis_index("tb") & 3) * (SLOTS * PART)


def vmem():
    return pl.BlockSpec(memory_space=pltpu.VMEM)


def smem():
    return pl.BlockSpec(memory_space=pltpu.SMEM)


def params(mib):
    return pltpu.CompilerParams(vmem_limit_bytes=mib << 20)


def cos_sin_turns(turns):
    r = turns - jnp.round(turns)
    z = r * r
    s = ((SIN_C[2] * z + SIN_C[1]) * z + SIN_C[0]) * r
    c = ((COS_C[3] * z + COS_C[2]) * z + COS_C[1]) * z + COS_C[0]
    s1 = s * c
    c1 = ROOT2 - s * s
    return 1.0 - s1 * s1, s1 * c1


def three_parts(value):
    high = value.astype(BF16)
    left = value - high.astype(F32)
    mid = left.astype(BF16)
    low = (left - mid.astype(F32)).astype(BF16)
    return high, mid, low


def prepare_kernel(
    order_hbm, assign_hbm, lm_hbm, uv_hbm, spec_hbm, lm8_ref, uv8_ref, wide_ref,
    order_ref, assign_ref, lm_ref, uv_ref, spec_ref, pos_ref, sems
):
    pairs = [(assign_hbm, assign_ref), (order_hbm, order_ref), (lm_hbm, lm_ref), (uv_hbm, uv_ref)]
    for n in range(PIECES):
        piece = slice(n * (POOL // PIECES), (n + 1) * (POOL // PIECES))
        pairs.append((spec_hbm.at[:, piece, :], spec_ref.at[:, piece, :]))
    copies = [pltpu.make_async_copy(src, dst, sems.at[n]) for n, (src, dst) in enumerate(pairs)]
    for copy in copies:
        copy.start()
    column = lax.broadcasted_iota(jnp.int32, (32, POOL), 1) // 128
    pick = (column == lax.broadcasted_iota(jnp.int32, (32, POOL), 0)).astype(F32).astype(BF16)
    for copy in copies[:2]:
        copy.wait()
    assign = assign_ref[...]
    low = assign & 127
    high = assign >> 7
    pos = jnp.zeros((128, 32), F32)
    for d in range(DIR_DEV):
        place = jnp.where(order_ref[1] == d, 1.0, jnp.where(order_ref[2] == d, 2.0, 0.0))
        lanes = slice(d * NCOMP, (d + 1) * NCOMP)
        low_hot = (lax.broadcasted_iota(jnp.int32, (128, NCOMP), 0) == low[:, lanes]).astype(F32).astype(BF16)
        high_hot = (lax.broadcasted_iota(jnp.int32, (32, NCOMP), 0) == high[:, lanes]).astype(F32).astype(BF16)
        pos = pos + place * lax.dot_general(
            low_hot, high_hot, (((1,), (1,)), ((), ())), preferred_element_type=F32
        )
    pos_ref[...] = jnp.dot(pos.astype(BF16), pick, preferred_element_type=F32)
    for copy in copies[2:4]:
        copy.wait()
    lh, lmid, ll = three_parts(lm_ref[...])
    zero = jnp.zeros((2, POOL), BF16)
    lm8_ref[...] = jnp.concatenate(
        [lh[0:1], lmid[0:1], ll[0:1], lh[1:2], lmid[1:2], ll[1:2], zero], axis=0
    )
    for q in range(N_DIR):
        u = uv_ref[0:1, q * QROWS : (q + 1) * QROWS]
        v = uv_ref[1:2, q * QROWS : (q + 1) * QROWS]
        uv8_ref[q] = jnp.concatenate([u, u, u, v, v, v, jnp.zeros((2, QROWS), BF16)], axis=0)
    for column in range(POOL // 128):
        if column % (POOL // 128 // PIECES) == 0:
            copies[4 + column // (POOL // 128 // PIECES)].wait()
        place_here = pos_ref[:, column * 128 : (column + 1) * 128]
        for p in range(DIR_DEV):
            mask = jnp.where(place_here == float(p), 1.0, 0.0).astype(BF16)
            for part in range(2):
                first = part * CHUNK + (column % 2) * 128
                wide_ref[column // 2, first : first + 128, p * COLS : (p + 1) * COLS] = (
                    spec_ref[part, column * 128 : (column + 1) * 128, :] * mask
                )


def prepare(peel_order, assignment, comp_lm, uv_coords, spectra):
    return pl.pallas_call(
        prepare_kernel,
        out_shape=(
            jax.ShapeDtypeStruct((8, POOL), BF16),
            jax.ShapeDtypeStruct((N_DIR, 8, QROWS), BF16),
            jax.ShapeDtypeStruct((NCHUNK, 2 * CHUNK, WIDE), BF16),
        ),
        in_specs=[pl.BlockSpec(memory_space=pltpu.MemorySpace.HBM)] * 5,
        out_specs=(vmem(), vmem(), vmem()),
        scratch_shapes=[
            pltpu.SMEM((DIR_DEV,), jnp.int32),
            pltpu.VMEM((1, POOL), jnp.int32),
            pltpu.VMEM((2, POOL), F32),
            pltpu.VMEM((2, ROWS_DEV), BF16),
            pltpu.VMEM((2, POOL, COLS), BF16),
            pltpu.VMEM((128, POOL), F32),
            pltpu.SemaphoreType.DMA((4 + PIECES,)),
        ],
        compiler_params=params(16),
        name="prepare",
    )(*(
        pltpu.with_memory_space_constraint(value, pltpu.MemorySpace.HBM)
        for value in (peel_order, assignment.reshape(1, POOL), comp_lm, uv_coords, spectra)
    ))


def predict_kernel(flips, uv8_ref, lm8_ref, wide_ref, *rest):
    out_refs = rest[: len(flips)]
    tab_a, tab_b, acc_ref = rest[len(flips) :]
    me = own_place()[0]
    uv_rows = jnp.concatenate([uv8_ref[me ^ x].astype(F32).T for x in flips], axis=0).astype(BF16)

    def table(j, tab_ref):
        lm = lm8_ref[:, j * CHUNK : (j + 1) * CHUNK]
        turns = jnp.dot(uv_rows, lm, preferred_element_type=F32)
        cos, sin = cos_sin_turns(turns)
        tab_ref[:, :CHUNK] = cos.astype(BF16)
        tab_ref[:, CHUNK:] = sin.astype(BF16)

    tabs = (tab_a, tab_b)
    table(0, tab_a)
    for j in range(NCHUNK):
        if j + 1 < NCHUNK:
            table(j + 1, tabs[(j + 1) % 2])
        part = jnp.dot(tabs[j % 2][...], wide_ref[j], preferred_element_type=F32)
        if j == 0:
            acc_ref[...] = part
        else:
            acc_ref[...] += part
    for n in range(len(flips)):
        for p in range(DIR_DEV):
            out_refs[n][p] = acc_ref[n * QROWS : (n + 1) * QROWS, p * COLS : (p + 1) * COLS].astype(BF16)


def predict(flips, uv8, lm8, wide):
    rows = QROWS * len(flips)

    def kernel(*refs):
        predict_kernel(flips, *refs)

    return pl.pallas_call(
        kernel,
        out_shape=tuple(jax.ShapeDtypeStruct((DIR_DEV, QROWS, COLS), BF16) for _ in flips),
        in_specs=[vmem(), vmem(), vmem()],
        out_specs=tuple(vmem() for _ in flips),
        scratch_shapes=[
            pltpu.VMEM((rows, 2 * CHUNK), BF16),
            pltpu.VMEM((rows, 2 * CHUNK), BF16),
            pltpu.VMEM((rows, WIDE), F32),
        ],
        cost_estimate=pl.CostEstimate(
            flops=2 * rows * 2 * POOL * 2 * WIDE,
            transcendentals=0,
            bytes_accessed=2 * (2 * POOL * WIDE + rows * WIDE),
        ),
        compiler_params=params(16),
        name="predict",
    )(uv8, lm8, wide)


def per_block_sum(value):
    return jnp.sum(value.reshape(QROWS // GB, GB, COLS), axis=1)


def lane_shift(value, by):
    return pltpu.roll(value, (-by) % COLS, 1)


def sweeps(pull):
    lane = lax.broadcasted_iota(jnp.int32, pull.shape, 1)
    first, last = lane < 2, lane >= COLS - 2
    band = {0: jnp.ones_like(pull)}
    free = pull
    for _ in range(ITERS - 1):
        lower = {d: lane_shift(value, -2) for d, value in band.items()}
        upper = {d: lane_shift(value, 2) for d, value in band.items()}
        new = {}
        for d, value in band.items():
            for at, inside, kept in ((d - 2, lower[d], first), (d + 2, upper[d], last)):
                moved = jnp.where(kept, 0.0, inside)
                new[at] = new[at] + moved if at in new else moved
                stays = jnp.where(kept, value, 0.0)
                new[d] = new[d] + stays if d in new else stays
        band = {d: (0.5 * pull) * value for d, value in new.items()}
        band[0] = band[0] + 1.0
        around = jnp.where(first, free, lane_shift(free, -2)) + jnp.where(last, free, lane_shift(free, 2))
        free = pull * (0.5 * around)
    return band, free


SHIFTS = tuple(range(-2 * (ITERS - 1), 2 * ITERS, 2))


def peel_kernel(vis_ref, ridge_ref, m0_ref, m1_ref, m2_ref, m3_ref, out_ref, *rest):
    part_refs, (model_ref, inv_ref, band_ref, part_ref) = rest[:N_DIR], rest[N_DIR:]
    me = own_place()[0]
    ridge = ridge_ref[...]
    blocks = QROWS // GB
    for x, ref in enumerate((m0_ref, m1_ref, m2_ref, m3_ref)):
        owner = me ^ x
        for p in range(DIR_DEV):
            model = ref[p].astype(F32)
            model_ref[owner * DIR_DEV + p] = model
            inv_ref[pl.ds((owner * DIR_DEV + p) * 8, blocks), :] = per_block_sum(model * model)
    inv = 1.0 / (inv_ref[...] + ridge)
    band, free = sweeps(ridge * inv)
    for n, d in enumerate(SHIFTS):
        band_ref[n] = band[d] * lane_shift(inv, d)
    band_ref[len(SHIFTS)] = free
    remains = vis_ref[pl.ds(pl.multiple_of(me * QROWS, QROWS), QROWS), :].astype(F32)
    for j in range(N_DIR * DIR_DEV):
        model = model_ref[j]
        cross = per_block_sum(remains * model)
        gain = band_ref[len(SHIFTS), j * 8 : j * 8 + blocks, :]
        for n, d in enumerate(SHIFTS):
            gain = gain + band_ref[n, j * 8 : j * 8 + blocks, :] * (lane_shift(cross, d) if d else cross)
        spread = jnp.concatenate(
            [jnp.broadcast_to(gain[b : b + 1], (GB, COLS)) for b in range(blocks)], axis=0
        )
        remains = remains - spread * model
        if (j + 1) % DIR_DEV == 0:
            remains = remains.astype(BF16).astype(F32)
    out_ref[...] = remains.astype(BF16)
    part_ref[...] = remains.reshape(QBLOCKS, 2, PART, COLS)
    for x in range(N_DIR):
        part_refs[x][...] = part_ref[:, (me ^ x) & 1].astype(BF16)


def peel(visibilities, ridge_weight, models):
    out = pl.pallas_call(
        peel_kernel,
        out_shape=(jax.ShapeDtypeStruct((QROWS, COLS), BF16),)
        + (jax.ShapeDtypeStruct((QBLOCKS, PART, COLS), BF16),) * N_DIR,
        in_specs=[vmem()] * 6,
        out_specs=(vmem(),) * (1 + N_DIR),
        scratch_shapes=[
            pltpu.VMEM((N_DIR * DIR_DEV, QROWS, COLS), F32),
            pltpu.VMEM((N_DIR * DIR_DEV * 8, COLS), F32),
            pltpu.VMEM((len(SHIFTS) + 1, N_DIR * DIR_DEV * 8, COLS), F32),
            pltpu.VMEM((QBLOCKS, 2, PART, COLS), F32),
        ],
        compiler_params=params(16),
        name="peel",
    )(visibilities, ridge_weight.reshape(1, COLS), *models)
    return out[0], out[1:]


def label_kernel(tile_id_ref, tile_ref, uv_ref, out_ref, slot_ref, seen_ref):
    half = own_place()[1]
    offset = own_place()[2]
    tiles = tile_ref[...].astype(F32)
    block_of_lane = lax.broadcasted_iota(jnp.int32, (NB, ROWS_DEV), 1) // BB
    expand = (block_of_lane == lax.broadcasted_iota(jnp.int32, (NB, ROWS_DEV), 0)).astype(F32)
    tile_of_lane = jnp.sum(expand * tiles, axis=0, keepdims=True)
    sub = lax.broadcasted_iota(jnp.int32, (NB, NB), 0)
    col = lax.broadcasted_iota(jnp.int32, (NB, NB), 1)
    tile_row = jnp.sum(jnp.where(sub == col, tiles, 0.0), axis=0, keepdims=True)
    slot = jnp.sum(jnp.where((tiles == tile_row) & (col < sub), 1.0, 0.0), axis=1, keepdims=True)
    slot_of_row = lax.dot_general(
        expand.astype(BF16),
        jnp.broadcast_to(slot, (NB, COLS)).astype(BF16),
        (((0,), (0,)), ((), ())),
        preferred_element_type=F32,
    )
    within = lax.broadcasted_iota(jnp.int32, (ROWS_DEV, COLS), 0) % BB - half * PART
    lane = lax.broadcasted_iota(jnp.int32, (ROWS_DEV, COLS), 1)
    goal = slot_of_row.astype(jnp.int32) * PART + within + offset
    spot = jnp.where((goal == lane) & (within >= 0) & (within < PART), 1.0, 0.0).astype(BF16)
    row = lax.broadcasted_iota(jnp.int32, (N_TB * 8, ROWS_DEV), 0)
    u = uv_ref[0:1, :].astype(F32)
    v = uv_ref[1:2, :].astype(F32)
    value = jnp.where(row % 8 == 0, u, jnp.where(row % 8 == 1, v, 0.0))
    value = jnp.where((row // 8).astype(F32) == tile_of_lane, value, 0.0).astype(BF16)
    out = jnp.dot(value, spot, preferred_element_type=F32)
    out_ref[:, : SLOTS * PART, :] = jnp.zeros((N_TB, SLOTS * PART, COLS), BF16)
    out_ref[:, SLOTS * PART :, :] = out.reshape(N_TB, 8, COLS).astype(BF16)
    for t in range(N_TB):
        seen_ref[t] = 0
    for b in range(NB):
        tile = tile_id_ref[b]
        slot_ref[b] = seen_ref[tile]
        seen_ref[tile] = 1


def label(tile_ids, block_tile, uv_coords):
    return pl.pallas_call(
        label_kernel,
        out_shape=(
            jax.ShapeDtypeStruct((N_TB, SEND_ROWS, COLS), BF16),
            jax.ShapeDtypeStruct((NB,), jnp.int32),
        ),
        in_specs=[smem(), vmem(), vmem()],
        out_specs=(vmem(), smem()),
        scratch_shapes=[pltpu.SMEM((N_TB,), jnp.int32)],
        compiler_params=params(16),
        name="label",
    )(tile_ids, block_tile, uv_coords)


def pack_kernel(tile_ref, slot_ref, r0_ref, r1_ref, r2_ref, r3_ref, base_ref, out_ref, stage_ref):
    me = own_place()[0]
    out_ref[...] = base_ref[...]
    for x, ref in enumerate((r0_ref, r1_ref, r2_ref, r3_ref)):
        stage_ref[pl.ds((me ^ x) * QBLOCKS, QBLOCKS)] = ref[...]
    for b in range(NB):
        first = pl.multiple_of(slot_ref[b] * PART, PART)
        out_ref[tile_ref[b], pl.ds(first, PART), :] = stage_ref[b]


def pack(tile_ids, slots, rows, base):
    return pl.pallas_call(
        pack_kernel,
        out_shape=jax.ShapeDtypeStruct((N_TB, SEND_ROWS, COLS), BF16),
        in_specs=[smem(), smem()] + [vmem()] * 5,
        out_specs=vmem(),
        scratch_shapes=[pltpu.VMEM((NB, PART, COLS), BF16)],
        compiler_params=params(16),
        name="pack",
    )(tile_ids, slots, *rows, base)


def join_kernel(r0_ref, r1_ref, r2_ref, r3_ref, out_ref):
    me = own_place()[0]
    for x, ref in enumerate((r0_ref, r1_ref, r2_ref, r3_ref)):
        out_ref[pl.ds(pl.multiple_of((me ^ x) * QROWS, QROWS), QROWS), :] = ref[...]


def join(rows):
    return pl.pallas_call(
        join_kernel,
        out_shape=jax.ShapeDtypeStruct((ROWS_DEV, COLS), BF16),
        in_specs=[vmem()] * 4,
        out_specs=vmem(),
        compiler_params=params(16),
        name="join",
    )(*rows)


def grid_kernel(flip, got_ref, out_ref, tab_ref, acc_ref):
    me, half, _ = own_place()
    chip = me // 2
    tiles = N_TB * SLOTS * PART // 128
    groups = N_TB // tiles
    coords = got_ref[:, SLOTS * PART :, :].astype(F32).reshape(tiles, groups, 8, COLS)
    coords = jnp.sum(coords, axis=1)
    y_pixel = (lax.broadcasted_iota(jnp.int32, (GRID, 1), 0) - GRID // 2).astype(F32)
    order = lax.broadcasted_iota(jnp.int32, (8, 1), 0)
    x_pixel = (16 * chip + 8 * (half ^ flip) + order - GRID // 2).astype(F32)
    scale = 1.0 / (2.0 * GRID)
    share = PIX // N_DIR
    step = 256
    per_step = step // 128

    def product(n):
        sources = step // (SLOTS * PART)
        rows = got_ref[n * sources : (n + 1) * sources, : SLOTS * PART, :].reshape(step, COLS)
        return jnp.dot(tab_ref[n], rows, preferred_element_type=F32)

    for tile in range(tiles):
        u = coords[tile, 0:1, :] * scale
        v = coords[tile, 1:2, :] * scale
        cx, sx = cos_sin_turns(x_pixel * u)
        cy, sy = cos_sin_turns(y_pixel * v)
        n, lanes = tile // per_step, slice(tile % per_step * 128, (tile % per_step + 1) * 128)
        for x in range(8):
            a, b = cx[x : x + 1], sx[x : x + 1]
            tab_ref[n, x * GRID : (x + 1) * GRID, lanes] = (a * cy - b * sy).astype(BF16)
            tab_ref[n, share + x * GRID : share + (x + 1) * GRID, lanes] = (b * cy + a * sy).astype(BF16)
        if tile % per_step == per_step - 1:
            if n == 0:
                acc_ref[...] = product(n)
            else:
                acc_ref[...] += product(n)
    total = acc_ref[...] * float(ROWS_DEV) ** (-0.5)
    for part in range(2):
        out_ref[part] = total[part * share : (part + 1) * share]


def grid_rows(flip, got):
    def kernel(*refs):
        grid_kernel(flip, *refs)

    return pl.pallas_call(
        kernel,
        out_shape=jax.ShapeDtypeStruct((2, PIX // N_DIR, COLS), F32),
        in_specs=[vmem()],
        out_specs=vmem(),
        scratch_shapes=[
            pltpu.VMEM((N_TB * SLOTS * PART // 256, 512, 256), BF16),
            pltpu.VMEM((512, COLS), F32),
        ],
        cost_estimate=pl.CostEstimate(flops=2 * 10**9, transcendentals=0, bytes_accessed=10**6),
        compiler_params=params(24),
        name="grid",
    )(got)


def after(value, done):
    return lax.optimization_barrier((value, done))[0]


def swap(value, flip):
    return lax.ppermute(value, "dir", [(i, i ^ flip) for i in range(N_DIR)])


def local(
    visibilities, uv_coords, comp_lm, spectra, ridge_weight, assignment, peel_order, block_tile
):
    lm8, uv8, wide = prepare(peel_order, assignment, comp_lm, uv_coords, spectra)
    far_a, far_b = predict((2, 3), uv8, lm8, wide)
    got_a, got_b = swap(far_a, 2), swap(far_b, 3)
    near, own = predict((1, 0), uv8, lm8, wide)
    got_near = swap(near, 1)
    tile_ids = block_tile[:, 0]
    base, slots = label(after(tile_ids, own), block_tile, uv_coords)
    rows, parts = peel(after(visibilities, slots), ridge_weight, (own, got_near, got_a, got_b))
    shared = [parts[0]] + [swap(parts[x], x) for x in range(1, N_DIR)]
    send = pack(tile_ids, slots, shared, base)
    got = lax.all_to_all(send, "tb", split_axis=0, concat_axis=0, tiled=True)
    late = after(rows, send)
    residual = join([late] + [swap(late, x) for x in range(1, N_DIR)])
    got = after(got, residual)
    moved = swap(grid_rows(1, got), 1)
    keep = grid_rows(0, got)
    return residual, (keep + moved)[None]


def solution(mesh):
    return jax.shard_map(
        local,
        mesh=mesh,
        in_specs=(
            P("tb", None),
            P(None, "tb"),
            P(None, "dir"),
            P(None, "dir", None),
            P(),
            P("dir"),
            P("dir"),
            P("tb", None),
        ),
        out_specs=(P("tb", None), P("tb", None, "dir", None)),
        check_vma=False,
    )
```
